32 devices in a mesh: band: 4 (over y, x), ma: 4 (over z), comp: 2 (over core).
Axes of the slice: x: 2, y: 2, z: 4, core: 2. Of those that a mesh axis runs over, the one named last changes fastest.
Arguments:
- solution: float32 [16, 4, 8, 2, 4096], P(None, 'comp', 'ma'), may hold values from -6 to 6
- residual: float32 [16, 4, 8, 2, 4096], P(None, 'comp', 'ma'), may hold values from -12 to 12
- direction: float32 [16, 4, 8, 2, 4096], P(None, 'comp', 'ma'), may hold values from -12 to 12
- prior_inv: float32 [4, 4096], P('comp'), may hold values from 0.5 to 4
- mixing: float32 [12, 4], P('band'), may hold values from -1.75 to 1.75
- beam: float32 [12, 4096], P('band'), may hold values from 0.25 to 1
- band_lmax: int32 [12], P('band'), may hold values from 2048 to 4095
- m_table: int32 [8], replicated, may hold values from 0 to 2047, as said below
- legendre: bfloat16 [8, 4096, 256], P(('ma', 'comp')), may hold values from -0.375 to 0.375
- noise_weight: float32 [12, 256, 4096], P('band', ('ma', 'comp')), may hold values from 0.25 to 4
- pixel_mask: int32 [12, 256, 4096], P('band', ('ma', 'comp')), may hold values 0 or 1
Outputs:
- new_solution: float32 [16, 4, 8, 2, 4096], P(None, 'comp', 'ma')
- new_residual: float32 [16, 4, 8, 2, 4096], P(None, 'comp', 'ma')
- new_direction: float32 [16, 4, 8, 2, 4096], P(None, 'comp', 'ma')
The draws below stay inside these ranges and needn't reach their ends.
Inputs may be any that keep to these rules, and one draw needn't show every extreme that they name: `m_table`: distinct values; 0 and 2047 are always among them.
All inputs are finite; a program needn't handle non-finite values. No bound on the sum of `pixel_mask` on one device may be relied on, other than what follows from the above.
Results may differ from the reference program's by a relative error of at most 0.003.
Values may be sent and summed in bfloat16 or wider, within the bound.
No kernel may reach another device: no remote copies, remote signals or barrier semaphores. Data moves between devices by JAX's collectives and lax.ppermute only.
A program may use at most 128 MiB of HBM per device.

```python
import math
import jax
import jax.numpy as jnp
from jax import lax

L = 4096
NCOMP = 4
NBAND = 12
PIX = 4096
NREAL = 16
M = 8
R = 256
MTOP = 2048


def rising_field(key, salt):
    field_key = jax.random.fold_in(key, salt)
    field_shape = (NREAL, NCOMP, M, 2, L)
    positions = jnp.arange(M, dtype=jnp.float32)
    growth = (1.0 + 2.0 * positions / max(M - 1, 1))[None, None, :, None, None]
    sample = jax.random.truncated_normal(field_key, -4.0, 4.0, field_shape, jnp.float32)
    return sample * growth


def draw_residual(key, part):
    return rising_field(key, 21)


def draw_direction(key, part):
    return rising_field(key, 37)


def draw_m_table(key, part):
    table_key = jax.random.fold_in(key, 11)
    first_key, second_key = jax.random.split(table_key)
    middle = jax.random.permutation(first_key, MTOP - 2)[:M - 2].astype(jnp.int32) + 1
    values = jnp.concatenate([jnp.array([0, MTOP - 1], jnp.int32), middle])
    return values[jax.random.permutation(second_key, M)]


def plant(values, own_key, least, largest):
    place = [jax.random.randint(jax.random.fold_in(own_key, axis), (), 0, length) for axis, length in enumerate(values.shape)]
    longest = values.shape.index(max(values.shape))
    beside = place[:longest] + [(place[longest] + 1) % values.shape[longest]] + place[longest + 1:]
    return values.at[tuple(place)].set(least).at[tuple(beside)].set(largest)


def level_of(rng, extent, cuts, low, high):
    level, own = 1.0, jax.random.fold_in(rng, 6)
    for axis_at, blocks in cuts:
        draws = jnp.exp(jax.random.uniform(jax.random.fold_in(own, axis_at), (blocks,), jnp.float32, low / len(cuts), high / len(cuts)))
        level = level * jnp.repeat(draws, extent[axis_at] // blocks).reshape([-1 if axis == axis_at else 1 for axis in range(len(extent))])
    return level


def noise(own_key, extent, deviation, most, cuts=(), kind=jnp.bfloat16):
    entries = jax.random.normal(own_key, extent, jnp.float32) * deviation
    if len(cuts) > 0:
        entries = level_of(own_key, extent, cuts, -0.22, 0.18) * entries
    return jnp.clip(entries, min=-most, max=most).astype(kind)


def setup_inputs(seed: int = 0) -> dict:
    key_list = jax.random.split(jax.random.key(seed), 12)
    solution = noise(key_list[0], (NREAL, NCOMP, M, 2, L), 1.0, 6.0, ((1, 2), (2, 4)), jnp.float32)
    residual = draw_residual(jax.random.fold_in(key_list[11], 71), 0)
    direction = draw_direction(jax.random.fold_in(key_list[11], 71), 0)
    prior_inv = jnp.clip(jnp.exp(math.log(4.0) - 2.0794415 * jax.random.uniform(key_list[3], (NCOMP, L), jnp.float32) ** level_of(key_list[3], (NCOMP, L), ((0, 2),), -0.2, 0.2)), 0.5, 4.0)
    mixing = noise(key_list[4], (NBAND, NCOMP), NBAND ** -0.5, 1.75, ((0, 4),), jnp.float32)
    beam = jnp.clip(jnp.exp(math.log(1.0) - 1.3862944 * jax.random.uniform(key_list[5], (NBAND, L), jnp.float32) ** level_of(key_list[5], (NBAND, L), ((0, 4),), -0.2, 0.2)), 0.25, 1.0)
    band_lmax = plant(jax.random.randint(key_list[6], (NBAND,), L // 2, L), jax.random.fold_in(key_list[6], 1), L // 2, L - 1).astype(jnp.int32)
    m_table = draw_m_table(jax.random.fold_in(key_list[11], 71), 0)
    legendre = noise(key_list[8], (M, L, R), R ** -0.5, 0.375, ((0, 8),))
    noise_weight = jnp.clip(jnp.exp(math.log(4.0) - 2.7725887 * jax.random.uniform(key_list[9], (NBAND, R, PIX), jnp.float32) ** level_of(key_list[9], (NBAND, R, PIX), ((0, 4), (1, 8)), -0.2, 0.2)), 0.25, 4.0)
    pixel_mask = plant((jax.random.randint(key_list[10], (NBAND, R, PIX), 0, 4) < 3).astype(jnp.int32), jax.random.fold_in(key_list[10], 1), 0, 1)
    return {"solution": solution, "residual": residual, "direction": direction, "prior_inv": prior_inv, "mixing": mixing, "beam": beam, "band_lmax": band_lmax, "m_table": m_table, "legendre": legendre, "noise_weight": noise_weight, "pixel_mask": pixel_mask}


def phase_table(m_table, pixels):
    columns = jnp.arange(pixels, dtype=jnp.int32)
    wrapped = m_table.astype(jnp.int32)[:, None] * columns[None, :] % pixels
    angles = wrapped.astype(jnp.float32) * (2.0 * math.pi / pixels)
    weights = jnp.where(m_table == 0, 1.0, 2.0).astype(jnp.float32)[:, None] / math.sqrt(pixels)
    return jnp.stack([weights * jnp.cos(angles), -weights * jnp.sin(angles)], axis=1).astype(jnp.bfloat16)

def keep_table(band_lmax, m_values, degrees):
    upper = degrees[None, None, :] <= band_lmax.astype(jnp.int32)[:, None, None]
    lower = degrees[None, None, :] >= m_values.astype(jnp.int32)[None, :, None]
    return (upper & lower).astype(jnp.float32)

def rounded(values):
    return lax.optimization_barrier(values.astype(jnp.bfloat16)).astype(jnp.float32)

def widen(values):
    return values[:, None, None, None, None]

def reference(solution, residual, direction, prior_inv, mixing, beam, band_lmax, m_table, legendre, noise_weight, pixel_mask):
    highest = lax.Precision.HIGHEST
    degrees = jnp.arange(L, dtype=jnp.int32)
    keep_mask = keep_table(band_lmax, m_table, degrees)
    band_scale = beam[:, None, :] * keep_mask
    table_wide = phase_table(m_table, PIX).astype(jnp.float32)
    legendre_wide = legendre.astype(jnp.float32)
    direction_low = rounded(direction)

    def one_band(summed, inputs):
        mix_row, scale_row, noise_row, mask_row = inputs
        mixed_sum = jnp.einsum('c,ncmql->nmql', mix_row, direction_low, precision=highest)
        band_coeffs = rounded(scale_row[None, :, None, :] * mixed_sum)
        cycle_values = rounded(jnp.einsum('nmql,mlr->nmqr', band_coeffs, legendre_wide, precision=highest))
        sky_map = jnp.einsum('nmqr,mqj->nrj', cycle_values, table_wide, precision=highest)
        weighted = rounded(noise_row * mask_row.astype(jnp.float32) * sky_map)
        back = rounded(jnp.einsum('nrj,mqj->nmqr', weighted, table_wide, precision=highest))
        harmonic = jnp.einsum('nmqr,mlr->nmql', back, legendre_wide, precision=highest)
        scaled = harmonic * scale_row[None, :, None, :]
        return (summed + mix_row[None, :, None, None, None] * scaled[:, None], None)
    zeros = jnp.zeros(direction.shape, jnp.float32)
    summed, unused = lax.scan(one_band, zeros, (mixing, band_scale, noise_weight, pixel_mask))
    image = prior_inv[None, :, None, None, :] * direction + summed
    axes = (1, 2, 3, 4)
    norm_old = lax.optimization_barrier(jnp.sum(residual * residual, axis=axes))
    curvature_sum = lax.optimization_barrier(jnp.sum(direction * image, axis=axes))
    step_size = norm_old / curvature_sum
    new_solution = solution + widen(step_size) * direction
    new_residual = residual - widen(step_size) * image
    norm_new = lax.optimization_barrier(jnp.sum(new_residual * new_residual, axis=axes))
    new_direction = new_residual + widen(norm_new / norm_old) * direction
    return (new_solution, new_residual, new_direction)
```

```python
import math

import jax
import jax.numpy as jnp
from jax import lax
from jax.sharding import PartitionSpec as P


def phase_table(m_table, pixels):
    columns = jnp.arange(pixels, dtype=jnp.int32)
    wrapped = m_table[:, None] * columns[None, :] % pixels
    angles = wrapped.astype(jnp.float32) * (2.0 * math.pi / pixels)
    weights = jnp.where(m_table == 0, 1.0, 2.0).astype(jnp.float32)[:, None] / math.sqrt(pixels)
    return jnp.stack([weights * jnp.cos(angles), -weights * jnp.sin(angles)], axis=1).astype(
        jnp.bfloat16
    )


def swap_parts(parts, axis):
    count = lax.axis_size(axis)
    got = [parts[0]]
    for step in range(1, count):
        pairs = [(i, (i + step) % count) for i in range(count)]
        got.append(lax.ppermute(parts[step], axis, pairs))
    return got


def widen(values):
    return values[:, None, None, None, None]


def body(
    solution,
    residual,
    direction,
    prior_inv,
    mixing,
    beam,
    band_lmax,
    m_table,
    legendre,
    noise_weight,
    pixel_mask,
):
    band_count = lax.axis_size("band")
    slab_count = lax.axis_size("ma")
    comp_count = lax.axis_size("comp")
    comp_index = lax.axis_index("comp")
    slab_index = lax.axis_index("ma")
    reals, comps, slots, halves, degrees_count = direction.shape
    half_count = legendre.shape[0]
    bands = mixing.shape[0]
    cycles = legendre.shape[2]
    sector = noise_weight.shape[1]
    pixels = noise_weight.shape[2]
    sectors = slab_count * comp_count
    degrees = jnp.arange(degrees_count, dtype=jnp.int32)
    f32 = jnp.float32
    bf16 = jnp.bfloat16

    first_slot = (slab_index * comp_count + comp_index) * half_count
    local_m = lax.dynamic_slice_in_dim(m_table, first_slot, half_count)
    upper = degrees[None, :] <= band_lmax[:, None]
    cut_beam = beam * upper.astype(f32)
    lower = degrees[None, :] >= local_m[:, None]
    scale = cut_beam[:, None, :] * lower[None].astype(f32)

    low = jnp.transpose(direction, (2, 1, 3, 0, 4)).astype(bf16)
    low = low.reshape((comp_count, half_count) + low.shape[1:])
    relative = [
        lax.dynamic_index_in_dim(low, (comp_index + step) % comp_count, 0, keepdims=False)
        for step in range(comp_count)
    ]
    got = swap_parts(relative, "comp")
    mixed = None
    for step in range(comp_count):
        source = (comp_index - step) % comp_count
        columns = lax.dynamic_slice_in_dim(mixing, source * comps, comps, 1)
        for comp in range(comps):
            term = columns[:, comp][:, None, None, None, None] * got[step][None, :, comp].astype(f32)
            mixed = term if mixed is None else mixed + term
    coeffs = (scale[:, :, None, None, :] * mixed).astype(bf16)
    cycle_values = jnp.einsum(
        "bmqnl,mlr->bmqnr", coeffs, legendre, preferred_element_type=f32
    ).astype(bf16)
    send = cycle_values.reshape(bands, half_count, halves, reals, sectors, sector)
    send = jnp.transpose(send, (4, 1, 2, 3, 0, 5)).reshape(
        sectors, half_count * halves, reals, bands * sector
    )
    spread = lax.all_to_all(send, ("ma", "comp"), 0, 0, tiled=True)
    rows = sectors * half_count * halves
    spread = spread.reshape(rows, reals, bands * sector).astype(f32)

    table = phase_table(m_table, pixels).reshape(rows, pixels)
    weight = (noise_weight * pixel_mask.astype(f32)).reshape(bands * sector, pixels)
    if rows <= 2 * reals:
        pairs = (table.astype(f32)[:, None, :] * table.astype(f32)[None, :, :]).reshape(
            rows * rows, pixels
        )
        gram = lax.dot_general(
            pairs, weight, (((1,), (1,)), ((), ())), precision=lax.Precision.HIGH,
            preferred_element_type=f32,
        ).reshape(rows, rows, 1, bands * sector)
        back = (gram * spread[None]).sum(1).astype(bf16)
    else:
        sky = jnp.einsum("knx,kj->nxj", spread.astype(bf16), table, preferred_element_type=f32)
        weighted = (weight[None] * sky).astype(bf16)
        back = jnp.einsum("nxj,kj->knx", weighted, table, preferred_element_type=f32).astype(bf16)

    back = back.reshape(sectors, half_count * halves, reals, bands * sector)
    everyone = jnp.broadcast_to(back[None], (band_count,) + back.shape).reshape(
        (band_count * sectors,) + back.shape[1:]
    )
    gathered = lax.all_to_all(everyone, ("band", "ma", "comp"), 0, 0, tiled=True)
    gathered = gathered.reshape(
        band_count, sectors, half_count, halves, reals, bands, sector
    )
    total_bands = band_count * bands
    own_back = jnp.transpose(gathered, (2, 0, 5, 3, 4, 1, 6)).reshape(
        half_count, total_bands, halves, reals, cycles
    )
    all_back = swap_parts([own_back] * comp_count, "comp")
    all_legendre = swap_parts([legendre] * comp_count, "comp")

    packed = jnp.concatenate([cut_beam, jnp.pad(mixing, ((0, 0), (0, 128 - mixing.shape[1])))], 1)
    packed = lax.all_to_all(
        jnp.broadcast_to(packed[None], (band_count,) + packed.shape), "band", 0, 0, tiled=True
    ).reshape(total_bands, -1)
    all_beam = packed[:, :degrees_count]
    all_mixing = packed[:, degrees_count : degrees_count + mixing.shape[1]]
    own_mixing = lax.dynamic_slice_in_dim(all_mixing, comp_index * comps, comps, 1)
    coef = own_mixing[:, :, None] * all_beam[:, None, :]

    parts = []
    for step in range(comp_count):
        source = (comp_index - step) % comp_count
        slot_m = lax.dynamic_slice_in_dim(
            m_table, (slab_index * comp_count + source) * half_count, half_count
        )
        harmonic = jnp.einsum(
            "mbqnr,mlr->bmqnl", all_back[step], all_legendre[step], preferred_element_type=f32
        )
        total = jnp.zeros((comps, half_count, halves, reals, degrees_count), f32)
        for band in range(total_bands):
            total = total + coef[band][:, None, None, None, :] * harmonic[band][None]
        keep = degrees[None, :] >= slot_m[:, None]
        parts.append(jnp.where(keep[None, :, None, None, :], total, 0.0))
    ordered = [
        lax.dynamic_index_in_dim(
            jnp.stack(parts), (comp_index - position) % comp_count, 0, keepdims=False
        )
        for position in range(comp_count)
    ]
    returned = jnp.concatenate(ordered, axis=1)
    returned = jnp.transpose(returned, (3, 0, 1, 2, 4))
    image = prior_inv[None, :, None, None, :] * direction + returned
    axes = (1, 2, 3, 4)
    sums = jnp.stack(
        [
            jnp.sum(residual * residual, axis=axes),
            jnp.sum(direction * image, axis=axes),
            jnp.sum(residual * image, axis=axes),
            jnp.sum(image * image, axis=axes),
        ]
    )
    sums = lax.all_to_all(
        jnp.broadcast_to(sums[None], (sectors,) + sums.shape), ("ma", "comp"), 0, 0, tiled=True
    ).sum(0)
    norm_old, curvature_sum, cross_sum, image_norm = sums
    step_size = norm_old / curvature_sum
    new_solution = solution + widen(step_size) * direction
    new_residual = residual - widen(step_size) * image
    norm_new = norm_old - 2.0 * step_size * cross_sum + step_size * step_size * image_norm
    new_direction = new_residual + widen(norm_new / norm_old) * direction
    return (new_solution, new_residual, new_direction)


def solution(mesh):
    in_specs = (
        P(None, "comp", "ma", None, None),
        P(None, "comp", "ma", None, None),
        P(None, "comp", "ma", None, None),
        P("comp", None),
        P("band", None),
        P("band", None),
        P("band"),
        P(),
        P(("ma", "comp"), None, None),
        P("band", ("ma", "comp"), None),
        P("band", ("ma", "comp"), None),
    )
    out_specs = (
        P(None, "comp", "ma", None, None),
        P(None, "comp", "ma", None, None),
        P(None, "comp", "ma", None, None),
    )
    return jax.shard_map(body, mesh=mesh, in_specs=in_specs, out_specs=out_specs, check_vma=False)
```

```python
import math

import jax
import jax.numpy as jnp
from jax import lax
from jax.experimental import pallas as pl
from jax.experimental.pallas import tpu as pltpu
from jax.sharding import PartitionSpec as P

LANES = 128
F32 = jnp.float32
BF16 = jnp.bfloat16


def flat_view(array):
    lead, halves, count = array.shape[:-2], array.shape[-2], array.shape[-1]
    tiles = count // LANES
    split = array.reshape(lead + (halves, tiles, LANES))
    return jnp.swapaxes(split, -3, -2).reshape(lead + (tiles * halves, LANES))


def from_flat(array, halves):
    lead, rows = array.shape[:-2], array.shape[-2]
    tiles = rows // halves
    split = jnp.swapaxes(array.reshape(lead + (tiles, halves, LANES)), -3, -2)
    return split.reshape(lead + (halves, tiles * LANES))


def dot_nt(left, right):
    return lax.dot_general(left, right, (((1,), (1,)), ((), ())), preferred_element_type=F32)


def dot_nn(left, right):
    return lax.dot_general(left, right, (((1,), (0,)), ((), ())), preferred_element_type=F32)


def narrow(flat, slot, halves):
    reals, comps, slots, rows, lanes = flat.shape
    tiles = rows // halves

    def kernel(slot_ref, x_ref, o_ref):
        for tile in range(tiles):
            for half in range(halves):
                o_ref[0, half, :, tile * lanes : (tile + 1) * lanes] = x_ref[
                    :, 0, 0, tile * halves + half, :
                ].astype(BF16)

    return pl.pallas_call(
        kernel,
        out_shape=jax.ShapeDtypeStruct((comps, halves, reals, tiles * lanes), BF16),
        grid_spec=pltpu.PrefetchScalarGridSpec(
            num_scalar_prefetch=1,
            grid=(comps,),
            in_specs=[
                pl.BlockSpec((reals, 1, 1, rows, lanes), lambda c, s: (0, c, s[0], 0, 0))
            ],
            out_specs=pl.BlockSpec((1, halves, reals, tiles * lanes), lambda c, s: (c, 0, 0, 0)),
        ),
    )(slot, flat)


def synthesize(mix, scale, own, received, legendre, sectors, chunk):
    comps, halves, reals, count = own.shape
    bands = scale.shape[0]
    cycles = legendre.shape[1]
    sector = cycles // sectors
    high = reals // 8
    lines = halves * reals
    steps = count // chunk

    def kernel(mix_ref, scale_ref, own_ref, got_ref, leg_ref, o_ref, acc_ref):
        step = pl.program_id(0)
        parts = [own_ref[c].astype(F32) for c in range(comps)]
        parts += [got_ref[c].astype(F32) for c in range(comps)]
        coeffs = []
        for band in range(bands):
            total = mix_ref[band, 0] * parts[0]
            for at in range(1, 2 * comps):
                total = total + mix_ref[band, at] * parts[at]
            coeffs.append((scale_ref[band : band + 1, :] * total).astype(BF16))
        value = dot_nn(jnp.concatenate(coeffs, 0), leg_ref[...])

        @pl.when(step == 0)
        def _():
            acc_ref[...] = value

        @pl.when(step > 0)
        def _():
            acc_ref[...] += value

        @pl.when(step == steps - 1)
        def _():
            for at in range(sectors):
                for band in range(bands):
                    pieces = []
                    for part in range(halves * high):
                        row = band * lines + part * 8
                        pieces.append(
                            acc_ref[row : row + 8, at * sector : (at + 1) * sector]
                        )
                    o_ref[at, band * 8 : band * 8 + 8, :] = jnp.concatenate(pieces, 1).astype(BF16)

    return pl.pallas_call(
        kernel,
        out_shape=jax.ShapeDtypeStruct((sectors, bands * 8, halves * high * sector), BF16),
        grid_spec=pltpu.PrefetchScalarGridSpec(
            num_scalar_prefetch=0,
            grid=(steps,),
            in_specs=[
                pl.BlockSpec(memory_space=pltpu.SMEM),
                pl.BlockSpec((bands, chunk), lambda i: (0, i)),
                pl.BlockSpec((comps, lines, chunk), lambda i: (0, 0, i)),
                pl.BlockSpec((comps, lines, chunk), lambda i: (0, 0, i)),
                pl.BlockSpec((chunk, cycles), lambda i: (i, 0)),
            ],
            out_specs=pl.BlockSpec(
                (sectors, bands * 8, halves * high * sector), lambda i: (0, 0, 0)
            ),
            scratch_shapes=[pltpu.VMEM((bands * lines, cycles), F32)],
        ),
    )(
        mix,
        scale,
        own.reshape(comps, lines, count),
        received.reshape(comps, lines, count),
        legendre,
    )


def split_bf16(value):
    top = value.astype(BF16)
    return top, (value - top.astype(F32)).astype(BF16)


def gram(table, noise_weight, pixel_mask, high, chunk):
    halves, slots, pixels = table.shape
    bands, sector, _ = noise_weight.shape
    lines = bands * sector
    rows = slots * slots
    steps = pixels // chunk

    def kernel(table_ref, noise_ref, mask_ref, o_ref, acc_ref):
        step = pl.program_id(0)
        weight = noise_ref[...] * mask_ref[...].astype(F32)
        weight_top, weight_low = split_bf16(weight)
        tops, lows = [], []
        for first in range(halves):
            for second in range(halves):
                for slot in range(slots):
                    product = table_ref[first, slot : slot + 1, :] * table_ref[second]
                    top, low = split_bf16(product)
                    tops.append(top)
                    lows.append(low)
        top = jnp.concatenate(tops, 0)
        low = jnp.concatenate(lows, 0)
        value = dot_nt(top, weight_top) + (dot_nt(low, weight_top) + dot_nt(top, weight_low))

        @pl.when(step == 0)
        def _():
            acc_ref[...] = value

        @pl.when(step > 0)
        def _():
            acc_ref[...] += value

        @pl.when(step == steps - 1)
        def _():
            for cross in range(2):
                for band in range(bands):
                    pieces = []
                    for half in range(halves):
                        other = half if cross == 0 else 1 - half
                        row = (half * halves + other) * rows
                        piece = acc_ref[row : row + rows, band * sector : (band + 1) * sector]
                        pieces += [piece] * high
                    o_ref[cross, band] = jnp.concatenate(pieces, 1)

    return pl.pallas_call(
        kernel,
        out_shape=jax.ShapeDtypeStruct((2, bands, rows, halves * high * sector), F32),
        grid=(steps,),
        in_specs=[
            pl.BlockSpec((halves, slots, chunk), lambda i: (0, 0, i)),
            pl.BlockSpec((lines, chunk), lambda i: (0, i)),
            pl.BlockSpec((lines, chunk), lambda i: (0, i)),
        ],
        out_specs=pl.BlockSpec(
            (2, bands, rows, halves * high * sector), lambda i: (0, 0, 0, 0)
        ),
        scratch_shapes=[pltpu.VMEM((halves * halves * rows, lines), F32)],
    )(table, noise_weight.reshape(lines, pixels), pixel_mask.reshape(lines, pixels))


def apply_gram(grams, spread, copies):
    slots, lines, lanes = spread.shape
    bands = grams.shape[1]

    def kernel(g_ref, x_ref, o_ref):
        for band in range(bands):
            straight, turned = [], []
            for slot in range(slots):
                value = x_ref[slot, band * 8 : band * 8 + 8, :].astype(F32)
                straight.append(value)
                turned.append(pltpu.roll(value, lanes // 2, 1))
            for slot in range(slots):
                total = None
                for other in range(slots):
                    row = slot * slots + other
                    term = g_ref[0, band, row : row + 1, :] * straight[other]
                    term = term + g_ref[1, band, row : row + 1, :] * turned[other]
                    total = term if total is None else total + term
                total = total.astype(BF16)
                for copy in range(copies):
                    o_ref[copy * slots + slot, band * 8 : band * 8 + 8, :] = total

    return pl.pallas_call(
        kernel,
        out_shape=jax.ShapeDtypeStruct((copies * slots, lines, lanes), BF16),
    )(grams, spread)


def analyze(slots_m, places, own, received, own_leg, got_leg, coef, prior, direction, residual,
            bands, sectors, halves, chunk):
    reals, comps, slots, rows, lanes = direction.shape
    total_bands = coef.shape[0] // comps
    groups = total_bands // bands
    count, cycles = own_leg.shape
    sector = cycles // sectors
    high = reals // 8
    lines = halves * reals
    steps = count // chunk
    tiles = chunk // lanes
    block_rows = tiles * halves

    def unpack(raw_ref, back_ref):
        for group in range(groups):
            for band in range(bands):
                for part in range(halves * high):
                    pieces = [
                        raw_ref[
                            group * sectors + at,
                            band * 8 : band * 8 + 8,
                            part * sector : (part + 1) * sector,
                        ].astype(F32)
                        for at in range(sectors)
                    ]
                    row = (group * bands + band) * lines + part * 8
                    back_ref[row : row + 8, :] = jnp.concatenate(pieces, 1)

    def kernel(m_ref, place_ref, own_ref, got_ref, own_leg_ref, got_leg_ref, coef_ref, prior_ref,
               d_ref, r_ref, image_ref, sums_ref, back_ref, low_ref, h_ref, s_ref, acc_ref):
        turn = pl.program_id(0)
        step = pl.program_id(1)

        @pl.when((step == 0) & (turn == 0))
        def _():
            unpack(own_ref, back_ref)
            low_ref[...] = back_ref[...].astype(BF16)
            acc_ref[...] = jnp.zeros(acc_ref.shape, F32)

        @pl.when((step == 0) & (turn == 1))
        def _():
            unpack(got_ref, back_ref)
            low_ref[...] = back_ref[...].astype(BF16)

        @pl.when(turn == 0)
        def _():
            h_ref[...] = dot_nt(low_ref[...], own_leg_ref[...])

        @pl.when(turn == 1)
        def _():
            h_ref[...] = dot_nt(low_ref[...], got_leg_ref[...])

        least = m_ref[turn] - step * chunk
        lane = lax.broadcasted_iota(jnp.int32, (lines, lanes), 1)
        for tile in range(tiles):
            part = slice(tile * lanes, (tile + 1) * lanes)
            totals = [None] * comps
            for band in range(total_bands):
                value = h_ref[band * lines : (band + 1) * lines, part]
                for comp in range(comps):
                    row = band * comps + comp
                    term = coef_ref[row : row + 1, part] * value
                    totals[comp] = term if totals[comp] is None else totals[comp] + term
            keep = lane >= least - tile * lanes
            for comp in range(comps):
                total = jnp.where(keep, totals[comp], 0.0)
                for half in range(halves):
                    s_ref[:, comp, tile * halves + half, :] = total[
                        half * reals : (half + 1) * reals
                    ]
        for real in range(reals):
            kinds = [None] * 4
            for comp in range(comps):
                for at in range(0, block_rows, 8):
                    span = slice(at, at + 8)
                    d = d_ref[real, comp, 0, span, :]
                    r = r_ref[real, comp, 0, span, :]
                    image = prior_ref[comp, span, :] * d + s_ref[real, comp, span, :]
                    image_ref[real, comp, 0, span, :] = image
                    terms = (r * r, d * image, r * image, image * image)
                    kinds = [
                        term if kind is None else kind + term for kind, term in zip(kinds, terms)
                    ]
            for kind in range(4):
                acc_ref[kind * reals + real] += kinds[kind]

        @pl.when((turn == 1) & (step == steps - 1))
        def _():
            folded = jnp.sum(acc_ref[...], axis=1)
            padded = jnp.concatenate(
                [folded, jnp.zeros((lanes - 4 * reals, lanes), F32)], 0
            )
            sums_ref[...] = jnp.sum(padded.T, axis=0, keepdims=True)

    def last(turn, step):
        return jnp.where(turn == 0, step, steps - 1)

    def first(turn, step):
        return jnp.where(turn == 0, 0, step)

    big = lambda t, j, m, p: (0, 0, p[t], j, 0)
    return pl.pallas_call(
        kernel,
        out_shape=(
            jax.ShapeDtypeStruct(direction.shape, F32),
            jax.ShapeDtypeStruct((1, lanes), F32),
        ),
        grid_spec=pltpu.PrefetchScalarGridSpec(
            num_scalar_prefetch=2,
            grid=(slots, steps),
            in_specs=[
                pl.BlockSpec(own.shape, lambda t, j, m, p: (0, 0, 0)),
                pl.BlockSpec(received.shape, lambda t, j, m, p: (0, 0, 0)),
                pl.BlockSpec((chunk, cycles), lambda t, j, m, p: (last(t, j), 0)),
                pl.BlockSpec((chunk, cycles), lambda t, j, m, p: (first(t, j), 0)),
                pl.BlockSpec((total_bands * comps, chunk), lambda t, j, m, p: (0, j)),
                pl.BlockSpec((comps, block_rows, lanes), lambda t, j, m, p: (0, j, 0)),
                pl.BlockSpec((reals, comps, 1, block_rows, lanes), big),
                pl.BlockSpec((reals, comps, 1, block_rows, lanes), big),
            ],
            out_specs=(
                pl.BlockSpec((reals, comps, 1, block_rows, lanes), big),
                pl.BlockSpec((1, lanes), lambda t, j, m, p: (0, 0)),
            ),
            scratch_shapes=[
                pltpu.VMEM((total_bands * lines, cycles), F32),
                pltpu.VMEM((total_bands * lines, cycles), BF16),
                pltpu.VMEM((total_bands * lines, chunk), F32),
                pltpu.VMEM((reals, comps, block_rows, lanes), F32),
                pltpu.VMEM((4 * reals, 8, lanes), F32),
            ],
        ),
    )(slots_m, places, own, received, own_leg, got_leg, coef, prior, direction, residual)


def update(sums, solution, residual, direction, image, group):
    reals, comps, slots, rows, lanes = direction.shape
    sources = sums.shape[0]

    def kernel(sums_ref, x_ref, r_ref, d_ref, i_ref, ox_ref, or_ref, od_ref):
        total = sums_ref[0]
        for at in range(1, sources):
            total = total + sums_ref[at]
        old, curvature, cross, norm = [
            total[:, kind * reals : (kind + 1) * reals] for kind in range(4)
        ]
        step_size = old / curvature
        new = old - 2.0 * step_size * cross + step_size * step_size * norm
        ratio = new / old
        base = pl.program_id(0) * group
        lane = lax.broadcasted_iota(jnp.int32, (1, reals), 1)
        for at in range(group):
            here = lane == base + at
            step_one = jnp.sum(jnp.where(here, step_size, 0.0), axis=1, keepdims=True)
            ratio_one = jnp.sum(jnp.where(here, ratio, 0.0), axis=1, keepdims=True)
            d = d_ref[at]
            fresh = r_ref[at] - step_one[None, None] * i_ref[at]
            ox_ref[at] = x_ref[at] + step_one[None, None] * d
            or_ref[at] = fresh
            od_ref[at] = fresh + ratio_one[None, None] * d

    block = pl.BlockSpec((group, comps, slots, rows, lanes), lambda i: (i, 0, 0, 0, 0))
    shape = jax.ShapeDtypeStruct(direction.shape, F32)
    return pl.pallas_call(
        kernel,
        out_shape=(shape,) * 3,
        grid=(reals // group,),
        in_specs=[pl.BlockSpec(sums.shape, lambda i: (0, 0, 0))] + [block] * 4,
        out_specs=(block,) * 3,
    )(sums, solution, residual, direction, image)


def phase_table(m_table, pixels):
    columns = jnp.arange(pixels, dtype=jnp.int32)
    wrapped = m_table[:, None] * columns[None, :] % pixels
    angles = wrapped.astype(jnp.float32) * (2.0 * math.pi / pixels)
    weights = jnp.where(m_table == 0, 1.0, 2.0).astype(jnp.float32)[:, None] / math.sqrt(pixels)
    return jnp.stack([weights * jnp.cos(angles), -weights * jnp.sin(angles)], axis=1).astype(
        jnp.bfloat16
    )


def swap_parts(parts, axis):
    count = lax.axis_size(axis)
    got = [parts[0]]
    for step in range(1, count):
        pairs = [(i, (i + step) % count) for i in range(count)]
        got.append(lax.ppermute(parts[step], axis, pairs))
    return got


def widen(values):
    return values[:, None, None, None, None]


def general(
    solution,
    residual,
    direction,
    prior_inv,
    mixing,
    beam,
    band_lmax,
    m_table,
    legendre,
    noise_weight,
    pixel_mask,
):
    band_count = lax.axis_size("band")
    slab_count = lax.axis_size("ma")
    comp_count = lax.axis_size("comp")
    comp_index = lax.axis_index("comp")
    slab_index = lax.axis_index("ma")
    reals, comps, slots, halves, degrees_count = direction.shape
    half_count = legendre.shape[0]
    bands = mixing.shape[0]
    cycles = legendre.shape[2]
    sector = noise_weight.shape[1]
    pixels = noise_weight.shape[2]
    sectors = slab_count * comp_count
    degrees = jnp.arange(degrees_count, dtype=jnp.int32)
    f32 = jnp.float32
    bf16 = jnp.bfloat16

    first_slot = (slab_index * comp_count + comp_index) * half_count
    local_m = lax.dynamic_slice_in_dim(m_table, first_slot, half_count)
    upper = degrees[None, :] <= band_lmax[:, None]
    cut_beam = beam * upper.astype(f32)
    lower = degrees[None, :] >= local_m[:, None]
    scale = cut_beam[:, None, :] * lower[None].astype(f32)

    low = jnp.transpose(direction, (2, 1, 3, 0, 4)).astype(bf16)
    low = low.reshape((comp_count, half_count) + low.shape[1:])
    relative = [
        lax.dynamic_index_in_dim(low, (comp_index + step) % comp_count, 0, keepdims=False)
        for step in range(comp_count)
    ]
    got = swap_parts(relative, "comp")
    mixed = None
    for step in range(comp_count):
        source = (comp_index - step) % comp_count
        columns = lax.dynamic_slice_in_dim(mixing, source * comps, comps, 1)
        for comp in range(comps):
            term = columns[:, comp][:, None, None, None, None] * got[step][None, :, comp].astype(f32)
            mixed = term if mixed is None else mixed + term
    coeffs = (scale[:, :, None, None, :] * mixed).astype(bf16)
    cycle_values = jnp.einsum(
        "bmqnl,mlr->bmqnr", coeffs, legendre, preferred_element_type=f32
    ).astype(bf16)
    send = cycle_values.reshape(bands, half_count, halves, reals, sectors, sector)
    send = jnp.transpose(send, (4, 1, 2, 3, 0, 5)).reshape(
        sectors, half_count * halves, reals, bands * sector
    )
    spread = lax.all_to_all(send, ("ma", "comp"), 0, 0, tiled=True)
    rows = sectors * half_count * halves
    spread = spread.reshape(rows, reals, bands * sector).astype(f32)

    table = phase_table(m_table, pixels).reshape(rows, pixels)
    weight = (noise_weight * pixel_mask.astype(f32)).reshape(bands * sector, pixels)
    if rows <= 2 * reals:
        pairs = (table.astype(f32)[:, None, :] * table.astype(f32)[None, :, :]).reshape(
            rows * rows, pixels
        )
        gram = lax.dot_general(
            pairs, weight, (((1,), (1,)), ((), ())), precision=lax.Precision.HIGH,
            preferred_element_type=f32,
        ).reshape(rows, rows, 1, bands * sector)
        back = (gram * spread[None]).sum(1).astype(bf16)
    else:
        sky = jnp.einsum("knx,kj->nxj", spread.astype(bf16), table, preferred_element_type=f32)
        weighted = (weight[None] * sky).astype(bf16)
        back = jnp.einsum("nxj,kj->knx", weighted, table, preferred_element_type=f32).astype(bf16)

    back = back.reshape(sectors, half_count * halves, reals, bands * sector)
    everyone = jnp.broadcast_to(back[None], (band_count,) + back.shape).reshape(
        (band_count * sectors,) + back.shape[1:]
    )
    gathered = lax.all_to_all(everyone, ("band", "ma", "comp"), 0, 0, tiled=True)
    gathered = gathered.reshape(
        band_count, sectors, half_count, halves, reals, bands, sector
    )
    total_bands = band_count * bands
    own_back = jnp.transpose(gathered, (2, 0, 5, 3, 4, 1, 6)).reshape(
        half_count, total_bands, halves, reals, cycles
    )
    all_back = swap_parts([own_back] * comp_count, "comp")
    all_legendre = swap_parts([legendre] * comp_count, "comp")

    packed = jnp.concatenate([cut_beam, jnp.pad(mixing, ((0, 0), (0, 128 - mixing.shape[1])))], 1)
    packed = lax.all_to_all(
        jnp.broadcast_to(packed[None], (band_count,) + packed.shape), "band", 0, 0, tiled=True
    ).reshape(total_bands, -1)
    all_beam = packed[:, :degrees_count]
    all_mixing = packed[:, degrees_count : degrees_count + mixing.shape[1]]
    own_mixing = lax.dynamic_slice_in_dim(all_mixing, comp_index * comps, comps, 1)
    coef = own_mixing[:, :, None] * all_beam[:, None, :]

    parts = []
    for step in range(comp_count):
        source = (comp_index - step) % comp_count
        slot_m = lax.dynamic_slice_in_dim(
            m_table, (slab_index * comp_count + source) * half_count, half_count
        )
        harmonic = jnp.einsum(
            "mbqnr,mlr->bmqnl", all_back[step], all_legendre[step], preferred_element_type=f32
        )
        total = jnp.zeros((comps, half_count, halves, reals, degrees_count), f32)
        for band in range(total_bands):
            total = total + coef[band][:, None, None, None, :] * harmonic[band][None]
        keep = degrees[None, :] >= slot_m[:, None]
        parts.append(jnp.where(keep[None, :, None, None, :], total, 0.0))
    ordered = [
        lax.dynamic_index_in_dim(
            jnp.stack(parts), (comp_index - position) % comp_count, 0, keepdims=False
        )
        for position in range(comp_count)
    ]
    returned = jnp.concatenate(ordered, axis=1)
    returned = jnp.transpose(returned, (3, 0, 1, 2, 4))
    image = prior_inv[None, :, None, None, :] * direction + returned
    axes = (1, 2, 3, 4)
    sums = jnp.stack(
        [
            jnp.sum(residual * residual, axis=axes),
            jnp.sum(direction * image, axis=axes),
            jnp.sum(residual * image, axis=axes),
            jnp.sum(image * image, axis=axes),
        ]
    )
    sums = lax.all_to_all(
        jnp.broadcast_to(sums[None], (sectors,) + sums.shape), ("ma", "comp"), 0, 0, tiled=True
    ).sum(0)
    norm_old, curvature_sum, cross_sum, image_norm = sums
    step_size = norm_old / curvature_sum
    new_solution = solution + widen(step_size) * direction
    new_residual = residual - widen(step_size) * image
    norm_new = norm_old - 2.0 * step_size * cross_sum + step_size * step_size * image_norm
    new_direction = new_residual + widen(norm_new / norm_old) * direction
    return (new_solution, new_residual, new_direction)


def fast(
    solution,
    residual,
    direction,
    prior_inv,
    mixing,
    beam,
    band_lmax,
    m_table,
    legendre,
    noise_weight,
    pixel_mask,
):
    band_count = lax.axis_size("band")
    slab_count = lax.axis_size("ma")
    comp_count = lax.axis_size("comp")
    comp_index = lax.axis_index("comp")
    slab_index = lax.axis_index("ma")
    reals, comps, slots, halves, count = direction.shape
    bands, sector, pixels = noise_weight.shape
    cycles = legendre.shape[2]
    sectors = slab_count * comp_count
    high = reals // 8
    total_bands = band_count * bands
    tiles = count // LANES
    other_index = 1 - comp_index
    exchange = [(0, 1), (1, 0)]
    legendre = legendre[0]
    degrees = jnp.arange(count, dtype=jnp.int32)
    places = jnp.stack([comp_index, other_index])
    slots_m = m_table[slab_index * comp_count + places]
    cut_beam = beam * (degrees[None, :] <= band_lmax[:, None]).astype(F32)

    flat_direction = flat_view(direction)
    flat_residual = flat_view(residual)
    flat_solution = flat_view(solution)

    sent = narrow(flat_direction, other_index[None], halves)
    received = lax.ppermute(sent, "comp", exchange)
    own = narrow(flat_direction, comp_index[None], halves)

    scale = cut_beam * (degrees >= slots_m[0])[None, :].astype(F32)
    mix_pair = jnp.concatenate(
        [
            lax.dynamic_slice_in_dim(mixing, comp_index * comps, comps, 1),
            lax.dynamic_slice_in_dim(mixing, other_index * comps, comps, 1),
        ],
        1,
    )
    packed = synthesize(mix_pair, scale, own, received, legendre, sectors, 1024)
    spread = lax.all_to_all(packed, ("ma", "comp"), 0, 0, tiled=True)
    other_legendre = lax.ppermute(legendre, "comp", exchange)

    gathered = jnp.concatenate(
        [cut_beam, jnp.pad(mixing, ((0, 0), (0, LANES - mixing.shape[1])))], 1
    )
    gathered = lax.all_to_all(
        jnp.broadcast_to(gathered[None], (band_count,) + gathered.shape), "band", 0, 0, tiled=True
    ).reshape(total_bands, count + LANES)
    own_mixing = lax.dynamic_slice_in_dim(
        gathered[:, count : count + mixing.shape[1]], comp_index * comps, comps, 1
    )
    coef = (own_mixing[:, :, None] * gathered[:, None, :count]).reshape(
        total_bands * comps, count
    )
    prior = jnp.broadcast_to(
        prior_inv.reshape(comps, tiles, 1, LANES), (comps, tiles, halves, LANES)
    ).reshape(comps, tiles * halves, LANES)

    table = jnp.swapaxes(phase_table(m_table, pixels), 0, 1).astype(F32)
    grams = gram(table, noise_weight, pixel_mask, high, 1024)
    back = apply_gram(grams, spread, band_count)
    arrived = lax.all_to_all(back, ("band", "ma", "comp"), 0, 0, tiled=True)
    other_arrived = lax.ppermute(arrived, "comp", exchange)
    image, sums = analyze(
        slots_m, places, arrived, other_arrived, legendre, other_legendre, coef, prior,
        flat_direction, flat_residual, bands, sectors, halves, 1024,
    )
    sums = lax.all_to_all(
        jnp.broadcast_to(sums[None], (sectors, 1, LANES)), ("ma", "comp"), 0, 0, tiled=True
    )
    outs = update(sums, flat_solution, flat_residual, flat_direction, image, 4)
    return tuple(from_flat(out, halves) for out in outs)


def body(*args):
    direction, legendre, noise_weight = args[2], args[8], args[9]
    reals, comps, slots, halves, count = direction.shape
    bands, sector, pixels = noise_weight.shape
    comp_count = lax.axis_size("comp")
    all_slots = lax.axis_size("ma") * comp_count * legendre.shape[0]
    fits = (
        comp_count == 2
        and slots == 2
        and legendre.shape[0] == 1
        and halves == 2
        and reals % 8 == 0
        and 4 * reals <= LANES
        and halves * (reals // 8) * sector == LANES
        and count % 1024 == 0
        and pixels % 1024 == 0
        and all_slots == 8
    )
    return fast(*args) if fits else general(*args)


def solution(mesh):
    in_specs = (
        P(None, "comp", "ma", None, None),
        P(None, "comp", "ma", None, None),
        P(None, "comp", "ma", None, None),
        P("comp", None),
        P("band", None),
        P("band", None),
        P("band"),
        P(),
        P(("ma", "comp"), None, None),
        P("band", ("ma", "comp"), None),
        P("band", ("ma", "comp"), None),
    )
    out_specs = (
        P(None, "comp", "ma", None, None),
        P(None, "comp", "ma", None, None),
        P(None, "comp", "ma", None, None),
    )
    return jax.shard_map(body, mesh=mesh, in_specs=in_specs, out_specs=out_specs, check_vma=False)
```

```python
import math

import jax
import jax.numpy as jnp
from jax import lax
from jax.experimental import pallas as pl
from jax.experimental.pallas import tpu as pltpu
from jax.sharding import PartitionSpec as P

LANES = 128
F32 = jnp.float32
BF16 = jnp.bfloat16
ON_CHIP = pl.BlockSpec(memory_space=pltpu.VMEM)
SCALARS = pl.BlockSpec(memory_space=pltpu.SMEM)
IN_PLACE = pl.BlockSpec(memory_space=pl.ANY)


def near(array):
    return pltpu.with_memory_space_constraint(array, pltpu.VMEM)


def shape_near(shape, kind):
    return pltpu.VMEM(shape, kind)


def flat_view(array):
    lead, halves, count = array.shape[:-2], array.shape[-2], array.shape[-1]
    tiles = count // LANES
    split = array.reshape(lead + (halves, tiles, LANES))
    return jnp.swapaxes(split, -3, -2).reshape(lead + (tiles * halves, LANES))


def from_flat(array, halves):
    lead, rows = array.shape[:-2], array.shape[-2]
    tiles = rows // halves
    split = jnp.swapaxes(array.reshape(lead + (tiles, halves, LANES)), -3, -2)
    return split.reshape(lead + (halves, tiles * LANES))


def dot_nt(left, right):
    return lax.dot_general(left, right, (((1,), (1,)), ((), ())), preferred_element_type=F32)


def dot_nn(left, right):
    return lax.dot_general(left, right, (((1,), (0,)), ((), ())), preferred_element_type=F32)


def split_bf16(value):
    top = value.astype(BF16)
    return top, (value - top.astype(F32)).astype(BF16)


def narrow(flat, slot, halves):
    reals, comps, slots, rows, lanes = flat.shape
    tiles = rows // halves
    pitch = rows + 8

    def kernel(slot_ref, x_ref, o_ref, buffer, arrived):
        copies = [
            pltpu.make_async_copy(
                x_ref.at[:, comp, slot_ref[0]],
                buffer.at[comp, :, pl.ds(0, rows), :],
                arrived.at[comp],
            )
            for comp in range(comps)
        ]
        for copy in copies:
            copy.start()
        lines = buffer.reshape(comps * reals * pitch, lanes)
        for comp in range(comps):
            copies[comp].wait()
            for tile in range(tiles):
                for half in range(halves):
                    start = comp * reals * pitch + tile * halves + half
                    picked = lines[pl.ds(start, reals, stride=pitch), :]
                    o_ref[
                        comp,
                        half * reals : (half + 1) * reals,
                        tile * lanes : (tile + 1) * lanes,
                    ] = picked.astype(BF16)

    return pl.pallas_call(
        kernel,
        out_shape=shape_near((comps, halves * reals, tiles * lanes), BF16),
        in_specs=[SCALARS, IN_PLACE],
        out_specs=ON_CHIP,
        scratch_shapes=[
            pltpu.VMEM((comps, reals, pitch, lanes), F32),
            pltpu.SemaphoreType.DMA((comps,)),
        ],
    )(slot, flat)


def synthesize(place, mixing, lmax, m_table, beam, own, received, legendre, sectors, chunk):
    comps, lines, count = own.shape
    bands = beam.shape[0]
    cycles = legendre.shape[1]
    sector = cycles // sectors
    parts = lines // 8

    def kernel(place_ref, mix_ref, lmax_ref, m_ref, beam_ref, own_ref, got_ref, leg_ref, o_ref):
        least = m_ref[place_ref[2]]
        acc = None
        for at in range(0, count, chunk):
            span = slice(at, at + chunk)
            degree = at + lax.broadcasted_iota(jnp.int32, (1, chunk), 1)
            values = []
            for comp in range(comps):
                values.append((place_ref[0] * comps + comp, own_ref[comp, :, span].astype(F32)))
                values.append((place_ref[1] * comps + comp, got_ref[comp, :, span].astype(F32)))
            coeffs = []
            for band in range(bands):
                total = None
                for column, value in values:
                    term = mix_ref[band, column] * value
                    total = term if total is None else total + term
                keep = (degree >= least) & (degree <= lmax_ref[band])
                scale = jnp.where(keep, beam_ref[band : band + 1, span], 0.0)
                coeffs.append((scale * total).astype(BF16))
            value = dot_nn(jnp.concatenate(coeffs, 0), leg_ref[span, :])
            acc = value if acc is None else acc + value
        for at in range(sectors):
            for band in range(bands):
                pieces = [
                    acc[
                        band * lines + part * 8 : band * lines + part * 8 + 8,
                        at * sector : (at + 1) * sector,
                    ]
                    for part in range(parts)
                ]
                o_ref[at, band * 8 : band * 8 + 8, :] = jnp.concatenate(pieces, 1).astype(BF16)

    return pl.pallas_call(
        kernel,
        out_shape=shape_near((sectors, bands * 8, parts * sector), BF16),
        in_specs=[SCALARS] * 4 + [ON_CHIP] * 4,
        out_specs=ON_CHIP,
    )(place, mixing, lmax, m_table, beam, near(own), near(received), legendre)


def gram(table, noise_weight, pixel_mask, high, chunk):
    halves, slots, pixels = table.shape
    bands, sector, _ = noise_weight.shape
    lines = bands * sector
    rows = slots * slots
    steps = pixels // chunk

    def kernel(table_ref, noise_ref, mask_ref, o_ref, acc_ref):
        step = pl.program_id(0)
        weight = noise_ref[...] * mask_ref[...].astype(F32)
        weight_top, weight_low = split_bf16(weight)
        tops, lows = [], []
        for first in range(halves):
            for second in range(halves):
                for slot in range(slots):
                    product = table_ref[first, slot : slot + 1, :] * table_ref[second]
                    top, low = split_bf16(product)
                    tops.append(top)
                    lows.append(low)
        top = jnp.concatenate(tops, 0)
        low = jnp.concatenate(lows, 0)
        value = dot_nt(top, weight_top) + (dot_nt(low, weight_top) + dot_nt(top, weight_low))

        @pl.when(step == 0)
        def _():
            acc_ref[...] = value

        @pl.when(step > 0)
        def _():
            acc_ref[...] += value

        @pl.when(step == steps - 1)
        def _():
            for cross in range(2):
                for band in range(bands):
                    pieces = []
                    for half in range(halves):
                        other = half if cross == 0 else 1 - half
                        row = (half * halves + other) * rows
                        piece = acc_ref[row : row + rows, band * sector : (band + 1) * sector]
                        pieces += [piece] * high
                    o_ref[cross, band] = jnp.concatenate(pieces, 1)

    return pl.pallas_call(
        kernel,
        out_shape=shape_near((2, bands, rows, halves * high * sector), F32),
        grid=(steps,),
        in_specs=[
            pl.BlockSpec((halves, slots, chunk), lambda i: (0, 0, i)),
            pl.BlockSpec((lines, chunk), lambda i: (0, i)),
            pl.BlockSpec((lines, chunk), lambda i: (0, i)),
        ],
        out_specs=pl.BlockSpec(
            (2, bands, rows, halves * high * sector), lambda i: (0, 0, 0, 0)
        ),
        scratch_shapes=[pltpu.VMEM((halves * halves * rows, lines), F32)],
    )(table, noise_weight.reshape(lines, pixels), pixel_mask.reshape(lines, pixels))


def lane_sums(rows):
    return jnp.sum(rows.T, axis=0, keepdims=True)


def own_dots(prior, direction, residual):
    reals, comps, slots, rows, lanes = direction.shape

    def kernel(prior_ref, d_ref, r_ref, o_ref):
        folded = []
        for which in range(2):
            for real in range(reals):
                total = None
                for comp in range(comps):
                    for slot in range(slots):
                        if which == 0:
                            value = d_ref[real, comp, slot]
                            term = prior_ref[comp] * value * value
                        else:
                            value = r_ref[real, comp, slot]
                            term = value * value
                        total = term if total is None else total + term
                folded.append(jnp.sum(total, axis=0, keepdims=True))
        folded.append(jnp.zeros((lanes - 2 * reals, lanes), F32))
        o_ref[...] = lane_sums(jnp.concatenate(folded, 0))

    return pl.pallas_call(
        kernel,
        out_shape=shape_near((1, lanes), F32),
        in_specs=[ON_CHIP] * 3,
        out_specs=ON_CHIP,
    )(prior, direction, residual)


def apply_gram(first_band, dots, grams, spread, copies, group):
    slots, lines, lanes = spread.shape
    bands = grams.shape[1]
    readers = slots // group
    sector = lanes // 4
    reals = 16

    def kernel(flag_ref, dots_ref, g_ref, x_ref, o_ref):
        product = None
        for band in range(bands):
            straight, turned = [], []
            for slot in range(slots):
                value = x_ref[slot, band * 8 : band * 8 + 8, :].astype(F32)
                straight.append(value)
                turned.append(pltpu.roll(value, lanes // 2, 1))
            for slot in range(slots):
                total = None
                for other in range(slots):
                    row = slot * slots + other
                    term = g_ref[0, band, row : row + 1, :] * straight[other]
                    term = term + g_ref[1, band, row : row + 1, :] * turned[other]
                    total = term if total is None else total + term
                total = total.astype(BF16)
                term = total.astype(F32) * straight[slot]
                product = term if product is None else product + term
                line = (slot % group) * lines + band * 8
                for copy in range(copies):
                    o_ref[copy * readers + slot // group, line : line + 8, :] = total
        product = product + pltpu.roll(product, lanes // 2, 1)
        halves = [product[:, :sector], product[:, sector : 2 * sector]]
        tall = jnp.concatenate(
            [
                jnp.concatenate([half, jnp.zeros((8, lanes - sector), F32)], 1)
                for half in halves
            ]
            + [jnp.zeros((lanes - 16, lanes), F32)],
            0,
        )
        shared = jnp.where(flag_ref[0] == 0, dots_ref[...], 0.0)
        value = lane_sums(tall) + shared
        top = value.astype(BF16).astype(F32)
        rest = value - top
        middle = rest.astype(BF16).astype(F32)
        last = (rest - middle).astype(BF16).astype(F32)
        row = top + pltpu.roll(middle, 2 * reals, 1) + pltpu.roll(last, 4 * reals, 1)
        tail = jnp.concatenate([row, jnp.zeros((7, lanes), F32)], 0).astype(BF16)
        for reader in range(copies * readers):
            o_ref[reader, group * lines : group * lines + 8, :] = tail

    return pl.pallas_call(
        kernel,
        out_shape=shape_near((copies * readers, group * lines + 8, lanes), BF16),
        in_specs=[SCALARS] + [ON_CHIP] * 3,
        out_specs=ON_CHIP,
    )(first_band, near(dots), near(grams), near(spread))


def analyze(place, m_table, own, received, own_leg, got_leg, coefs, prior, direction, residual,
            bands, sectors, halves, copies, chunk):
    reals, comps, slots, rows, lanes = direction.shape
    groups = len(coefs)
    total_bands = groups * bands
    count, cycles = own_leg.shape
    sector = cycles // sectors
    high = reals // 8
    lines = halves * reals
    tiles = chunk // lanes
    block_rows = tiles * halves
    pitch = comps * block_rows + 8
    per_slot = bands * 8
    slab = sectors // 2
    tail = slots * per_slot
    pieces_count = 2

    def kernel(place_ref, m_ref, own_ref, got_ref, own_leg_ref, got_leg_ref, *rest):
        coef_refs = rest[:groups]
        (prior_ref, d_ref, r_ref, new_ref, sums_ref, small_ref, back_ref, h_ref, h2_ref, s_ref,
         step_ref, leg_ref, dn_ref, rn_ref, arrived) = rest[groups:]
        is_first = place_ref[0] == 0

        sources = (own_leg_ref, got_leg_ref)
        copies_of = []
        for turn in range(slots):
            for piece in range(pieces_count):
                size = count // pieces_count
                span = pl.ds(piece * size, size)
                size = rows // pieces_count
                lines_span = pl.ds(piece * size, size)
                index = turn * pieces_count + piece
                copies_of.append(
                    [
                        pltpu.make_async_copy(
                            sources[turn].at[span], leg_ref.at[turn, span], arrived.at[index, 0]
                        )
                    ]
                    + [
                        pltpu.make_async_copy(
                            source.at[:, :, place_ref[turn], lines_span],
                            target.at[turn, :, :, lines_span],
                            arrived.at[index, 1 + which],
                        )
                        for which, (source, target) in enumerate(
                            ((d_ref, dn_ref), (r_ref, rn_ref))
                        )
                    ]
                )
        for triple in copies_of:
            for copy in triple:
                copy.start()

        total = None
        for ref in (own_ref, got_ref):
            for at in range(groups * slab):
                value = ref[at, tail : tail + 8, :].astype(F32)
                total = value if total is None else total + value
        line = total[0:1, :]
        line = (
            line
            + pltpu.roll(line, lanes - 2 * reals, 1)
            + pltpu.roll(line, lanes - 4 * reals, 1)
        )
        norm_old = line[:, reals : 2 * reals]
        step_size = norm_old / line[:, :reals]
        small_ref[...] = jnp.concatenate(
            [step_size, norm_old, jnp.zeros((1, lanes - 2 * reals), F32)], 1
        )
        for real in range(reals):
            step_ref[real] = jnp.broadcast_to(step_size[:, real : real + 1], (8, lanes))

        for turn in range(slots):
            base = place_ref[turn] * per_slot
            for group in range(groups):
                source = (place_ref[4] ^ group) * slab
                for band in range(bands):
                    start = pl.multiple_of(base + band * 8, 8)
                    for part in range(lines // 8):
                        span = slice(part * sector, (part + 1) * sector)
                        pieces = []
                        for z in range(slab):
                            mine = own_ref[source + z, pl.ds(start, 8), :].astype(F32)
                            theirs = got_ref[source + z, pl.ds(start, 8), :].astype(F32)
                            pieces.append(jnp.where(is_first, mine, theirs)[:, span])
                            pieces.append(jnp.where(is_first, theirs, mine)[:, span])
                        row = (group * bands + band) * lines + part * 8
                        back_ref[turn, row : row + 8, :] = jnp.concatenate(pieces, 1).astype(BF16)

        buffers = (h_ref, h2_ref)
        work = [(turn, at) for turn in range(slots) for at in range(0, count, chunk)]

        def multiply(index):
            turn, at = work[index]
            if at % (count // pieces_count) == 0:
                copies_of[turn * pieces_count + at * pieces_count // count][0].wait()
            buffers[index % 2][...] = dot_nt(back_ref[turn], leg_ref[turn, at : at + chunk, :])

        lane = lax.broadcasted_iota(jnp.int32, (lines, lanes), 1)
        norms = [None] * reals
        multiply(0)
        for index, (turn, at) in enumerate(work):
            if index + 1 < len(work):
                multiply(index + 1)
            h = buffers[index % 2]
            least = m_ref[place_ref[2 + turn]]
            for tile in range(tiles):
                part = slice(tile * lanes, (tile + 1) * lanes)
                here = slice(at + tile * lanes, at + (tile + 1) * lanes)
                totals = [None] * comps
                for group in range(groups):
                    for band in range(bands):
                        row = (group * bands + band) * lines
                        value = h[row : row + lines, part]
                        for comp in range(comps):
                            term = coef_refs[group][band, comp : comp + 1, here] * value
                            totals[comp] = term if totals[comp] is None else totals[comp] + term
                keep = lane >= least - (at + tile * lanes)
                for comp in range(comps):
                    total = jnp.where(keep, totals[comp], 0.0)
                    for half in range(halves):
                        start = comp * block_rows + tile * halves + half
                        s_ref[index % 2, pl.ds(start, reals, stride=pitch), :] = total[
                            half * reals : (half + 1) * reals
                        ]
            first = at // lanes * halves
            if at % (count // pieces_count) == 0:
                for copy in copies_of[turn * pieces_count + at * pieces_count // count][1:]:
                    copy.wait()
            for real in range(reals):
                for comp in range(comps):
                    for sub in range(0, block_rows, 8):
                        span = slice(first + sub, first + sub + 8)
                        line = real * pitch + comp * block_rows + sub
                        d = dn_ref[turn, real, comp, span, :]
                        r = rn_ref[turn, real, comp, span, :]
                        image = prior_ref[comp, span, :] * d + s_ref[index % 2, line : line + 8, :]
                        new = r - step_ref[real] * image
                        new_ref[real, comp, place_ref[turn], span, :] = new
                        term = new * new
                        norms[real] = term if norms[real] is None else norms[real] + term
        folded = [jnp.sum(norm, axis=0, keepdims=True) for norm in norms]
        folded.append(jnp.zeros((lanes - reals, lanes), F32))
        norm = lane_sums(jnp.concatenate(folded, 0))
        for at in range(copies):
            sums_ref[at] = norm

    return pl.pallas_call(
        kernel,
        out_shape=(
            shape_near(direction.shape, F32),
            shape_near((copies, 1, lanes), F32),
            shape_near((1, lanes), F32),
        ),
        in_specs=[SCALARS] * 2 + [ON_CHIP] * 2 + [IN_PLACE] * 2 + [ON_CHIP] * (1 + groups)
        + [IN_PLACE] * 2,
        out_specs=(ON_CHIP,) * 3,
        scratch_shapes=[
            pltpu.VMEM((slots, total_bands * lines, cycles), BF16),
            pltpu.VMEM((total_bands * lines, chunk), F32),
            pltpu.VMEM((total_bands * lines, chunk), F32),
            pltpu.VMEM((2, reals * pitch, lanes), F32),
            pltpu.VMEM((reals, 8, lanes), F32),
            pltpu.VMEM((slots, count, cycles), BF16),
            pltpu.VMEM((slots, reals, comps, rows, lanes), F32),
            pltpu.VMEM((slots, reals, comps, rows, lanes), F32),
            pltpu.SemaphoreType.DMA((slots * pieces_count, 3)),
        ],
    )(
        place, m_table, near(own), near(received), own_leg, got_leg, *(near(x) for x in coefs),
        prior, direction, residual,
    )


def phase_table(m_table, pixels):
    columns = jnp.arange(pixels, dtype=jnp.int32)
    wrapped = m_table[:, None] * columns[None, :] % pixels
    angles = wrapped.astype(jnp.float32) * (2.0 * math.pi / pixels)
    weights = jnp.where(m_table == 0, 1.0, 2.0).astype(jnp.float32)[:, None] / math.sqrt(pixels)
    return jnp.stack([weights * jnp.cos(angles), -weights * jnp.sin(angles)], axis=1).astype(
        jnp.bfloat16
    )


def swap_parts(parts, axis):
    count = lax.axis_size(axis)
    got = [parts[0]]
    for step in range(1, count):
        pairs = [(i, (i + step) % count) for i in range(count)]
        got.append(lax.ppermute(parts[step], axis, pairs))
    return got


def widen(values):
    return values[:, None, None, None, None]


def general(
    solution,
    residual,
    direction,
    prior_inv,
    mixing,
    beam,
    band_lmax,
    m_table,
    legendre,
    noise_weight,
    pixel_mask,
):
    band_count = lax.axis_size("band")
    slab_count = lax.axis_size("ma")
    comp_count = lax.axis_size("comp")
    comp_index = lax.axis_index("comp")
    slab_index = lax.axis_index("ma")
    reals, comps, slots, halves, degrees_count = direction.shape
    half_count = legendre.shape[0]
    bands = mixing.shape[0]
    cycles = legendre.shape[2]
    sector = noise_weight.shape[1]
    pixels = noise_weight.shape[2]
    sectors = slab_count * comp_count
    degrees = jnp.arange(degrees_count, dtype=jnp.int32)
    f32 = jnp.float32
    bf16 = jnp.bfloat16

    first_slot = (slab_index * comp_count + comp_index) * half_count
    local_m = lax.dynamic_slice_in_dim(m_table, first_slot, half_count)
    upper = degrees[None, :] <= band_lmax[:, None]
    cut_beam = beam * upper.astype(f32)
    lower = degrees[None, :] >= local_m[:, None]
    scale = cut_beam[:, None, :] * lower[None].astype(f32)

    low = jnp.transpose(direction, (2, 1, 3, 0, 4)).astype(bf16)
    low = low.reshape((comp_count, half_count) + low.shape[1:])
    relative = [
        lax.dynamic_index_in_dim(low, (comp_index + step) % comp_count, 0, keepdims=False)
        for step in range(comp_count)
    ]
    got = swap_parts(relative, "comp")
    mixed = None
    for step in range(comp_count):
        source = (comp_index - step) % comp_count
        columns = lax.dynamic_slice_in_dim(mixing, source * comps, comps, 1)
        for comp in range(comps):
            term = columns[:, comp][:, None, None, None, None] * got[step][None, :, comp].astype(f32)
            mixed = term if mixed is None else mixed + term
    coeffs = (scale[:, :, None, None, :] * mixed).astype(bf16)
    cycle_values = jnp.einsum(
        "bmqnl,mlr->bmqnr", coeffs, legendre, preferred_element_type=f32
    ).astype(bf16)
    send = cycle_values.reshape(bands, half_count, halves, reals, sectors, sector)
    send = jnp.transpose(send, (4, 1, 2, 3, 0, 5)).reshape(
        sectors, half_count * halves, reals, bands * sector
    )
    spread = lax.all_to_all(send, ("ma", "comp"), 0, 0, tiled=True)
    rows = sectors * half_count * halves
    spread = spread.reshape(rows, reals, bands * sector).astype(f32)

    table = phase_table(m_table, pixels).reshape(rows, pixels)
    weight = (noise_weight * pixel_mask.astype(f32)).reshape(bands * sector, pixels)
    if rows <= 2 * reals:
        pairs = (table.astype(f32)[:, None, :] * table.astype(f32)[None, :, :]).reshape(
            rows * rows, pixels
        )
        gram = lax.dot_general(
            pairs, weight, (((1,), (1,)), ((), ())), precision=lax.Precision.HIGH,
            preferred_element_type=f32,
        ).reshape(rows, rows, 1, bands * sector)
        back = (gram * spread[None]).sum(1).astype(bf16)
    else:
        sky = jnp.einsum("knx,kj->nxj", spread.astype(bf16), table, preferred_element_type=f32)
        weighted = (weight[None] * sky).astype(bf16)
        back = jnp.einsum("nxj,kj->knx", weighted, table, preferred_element_type=f32).astype(bf16)

    back = back.reshape(sectors, half_count * halves, reals, bands * sector)
    everyone = jnp.broadcast_to(back[None], (band_count,) + back.shape).reshape(
        (band_count * sectors,) + back.shape[1:]
    )
    gathered = lax.all_to_all(everyone, ("band", "ma", "comp"), 0, 0, tiled=True)
    gathered = gathered.reshape(
        band_count, sectors, half_count, halves, reals, bands, sector
    )
    total_bands = band_count * bands
    own_back = jnp.transpose(gathered, (2, 0, 5, 3, 4, 1, 6)).reshape(
        half_count, total_bands, halves, reals, cycles
    )
    all_back = swap_parts([own_back] * comp_count, "comp")
    all_legendre = swap_parts([legendre] * comp_count, "comp")

    packed = jnp.concatenate([cut_beam, jnp.pad(mixing, ((0, 0), (0, 128 - mixing.shape[1])))], 1)
    packed = lax.all_to_all(
        jnp.broadcast_to(packed[None], (band_count,) + packed.shape), "band", 0, 0, tiled=True
    ).reshape(total_bands, -1)
    all_beam = packed[:, :degrees_count]
    all_mixing = packed[:, degrees_count : degrees_count + mixing.shape[1]]
    own_mixing = lax.dynamic_slice_in_dim(all_mixing, comp_index * comps, comps, 1)
    coef = own_mixing[:, :, None] * all_beam[:, None, :]

    parts = []
    for step in range(comp_count):
        source = (comp_index - step) % comp_count
        slot_m = lax.dynamic_slice_in_dim(
            m_table, (slab_index * comp_count + source) * half_count, half_count
        )
        harmonic = jnp.einsum(
            "mbqnr,mlr->bmqnl", all_back[step], all_legendre[step], preferred_element_type=f32
        )
        total = jnp.zeros((comps, half_count, halves, reals, degrees_count), f32)
        for band in range(total_bands):
            total = total + coef[band][:, None, None, None, :] * harmonic[band][None]
        keep = degrees[None, :] >= slot_m[:, None]
        parts.append(jnp.where(keep[None, :, None, None, :], total, 0.0))
    ordered = [
        lax.dynamic_index_in_dim(
            jnp.stack(parts), (comp_index - position) % comp_count, 0, keepdims=False
        )
        for position in range(comp_count)
    ]
    returned = jnp.concatenate(ordered, axis=1)
    returned = jnp.transpose(returned, (3, 0, 1, 2, 4))
    image = prior_inv[None, :, None, None, :] * direction + returned
    axes = (1, 2, 3, 4)
    sums = jnp.stack(
        [
            jnp.sum(residual * residual, axis=axes),
            jnp.sum(direction * image, axis=axes),
            jnp.sum(residual * image, axis=axes),
            jnp.sum(image * image, axis=axes),
        ]
    )
    sums = lax.all_to_all(
        jnp.broadcast_to(sums[None], (sectors,) + sums.shape), ("ma", "comp"), 0, 0, tiled=True
    ).sum(0)
    norm_old, curvature_sum, cross_sum, image_norm = sums
    step_size = norm_old / curvature_sum
    new_solution = solution + widen(step_size) * direction
    new_residual = residual - widen(step_size) * image
    norm_new = norm_old - 2.0 * step_size * cross_sum + step_size * step_size * image_norm
    new_direction = new_residual + widen(norm_new / norm_old) * direction
    return (new_solution, new_residual, new_direction)


def fast(
    solution,
    residual,
    direction,
    prior_inv,
    mixing,
    beam,
    band_lmax,
    m_table,
    legendre,
    noise_weight,
    pixel_mask,
):
    band_count = lax.axis_size("band")
    slab_count = lax.axis_size("ma")
    comp_count = lax.axis_size("comp")
    band_index = lax.axis_index("band")
    comp_index = lax.axis_index("comp")
    slab_index = lax.axis_index("ma")
    reals, comps, slots, halves, count = direction.shape
    bands, sector, pixels = noise_weight.shape
    sectors = slab_count * comp_count
    high = reals // 8
    tiles = count // LANES
    other_index = 1 - comp_index
    exchange = [(0, 1), (1, 0)]
    legendre = legendre[0]
    degrees = jnp.arange(count, dtype=jnp.int32)
    first_slot = slab_index * comp_count
    own_place = jnp.stack([comp_index, other_index, first_slot + comp_index])
    place = jnp.stack(
        [comp_index, other_index, first_slot + comp_index, first_slot + other_index, band_index]
    )

    flat_direction = flat_view(direction)
    flat_residual = flat_view(residual)
    flat_solution = flat_view(solution)

    sent = narrow(flat_direction, other_index[None], halves)
    received = lax.ppermute(sent, "comp", exchange)
    own = narrow(flat_direction, comp_index[None], halves)
    packed = synthesize(
        own_place, mixing, band_lmax, m_table, beam, own, received, legendre, sectors, 1024
    )
    spread = lax.all_to_all(packed, ("ma", "comp"), 0, 0, tiled=True)
    other_legendre = lax.ppermute(legendre, "comp", exchange)

    cut_beam = beam * (degrees[None, :] <= band_lmax[:, None]).astype(F32)
    own_mixing = lax.dynamic_slice_in_dim(mixing, comp_index * comps, comps, 1)
    own_coef = own_mixing[:, :, None] * cut_beam[:, None, :]
    prior = jnp.broadcast_to(
        prior_inv.reshape(comps, tiles, 1, LANES), (comps, tiles, halves, LANES)
    ).reshape(comps, tiles * halves, LANES)
    table = jnp.swapaxes(phase_table(m_table, pixels), 0, 1).astype(F32)
    grams = gram(table, noise_weight, pixel_mask, high, 1024)
    dots = own_dots(prior, flat_direction, flat_residual)
    back = apply_gram(band_index[None], dots, grams, spread, band_count, comp_count)
    arrived = lax.all_to_all(back, ("band", "ma"), 0, 0, tiled=True)
    coefs = [own_coef] + [
        lax.ppermute(own_coef, "band", [(i, i ^ step) for i in range(band_count)])
        for step in range(1, band_count)
    ]
    arrived, coefs = lax.optimization_barrier((arrived, coefs))
    other_arrived = lax.ppermute(arrived, "comp", exchange)
    new_residual, norms, small = analyze(
        place, m_table, arrived, other_arrived, legendre, other_legendre, coefs, prior,
        flat_direction, flat_residual, bands, sectors, halves, sectors, 512,
    )
    norms = lax.all_to_all(norms, ("ma", "comp"), 0, 0, tiled=True)
    step_size = small[0, :reals][:, None, None, None, None]
    new_solution = flat_solution + step_size * flat_direction
    norms, new_solution = lax.optimization_barrier((norms, new_solution))
    ratio = jnp.sum(norms, axis=0)[0, :reals] / small[0, reals : 2 * reals]
    new_direction = new_residual + ratio[:, None, None, None, None] * flat_direction
    return tuple(from_flat(out, halves) for out in (new_solution, new_residual, new_direction))
def body(*args):
    direction, legendre, noise_weight = args[2], args[8], args[9]
    reals, comps, slots, halves, count = direction.shape
    bands, sector, pixels = noise_weight.shape
    comp_count = lax.axis_size("comp")
    all_slots = lax.axis_size("ma") * comp_count * legendre.shape[0]
    fits = (
        comp_count == 2
        and slots == 2
        and legendre.shape[0] == 1
        and halves == 2
        and reals % 8 == 0
        and reals == 16
        and halves * (reals // 8) * sector == LANES
        and count % 1024 == 0
        and pixels % 1024 == 0
        and all_slots == 8
        and lax.axis_size("band") == 4
    )
    return fast(*args) if fits else general(*args)


def solution(mesh):
    in_specs = (
        P(None, "comp", "ma", None, None),
        P(None, "comp", "ma", None, None),
        P(None, "comp", "ma", None, None),
        P("comp", None),
        P("band", None),
        P("band", None),
        P("band"),
        P(),
        P(("ma", "comp"), None, None),
        P("band", ("ma", "comp"), None),
        P("band", ("ma", "comp"), None),
    )
    out_specs = (
        P(None, "comp", "ma", None, None),
        P(None, "comp", "ma", None, None),
        P(None, "comp", "ma", None, None),
    )
    return jax.shard_map(body, mesh=mesh, in_specs=in_specs, out_specs=out_specs, check_vma=False)
```

```python
import math

import jax
import jax.numpy as jnp
from jax import lax
from jax.experimental import pallas as pl
from jax.experimental.pallas import tpu as pltpu
from jax.sharding import PartitionSpec as P

LANES = 128
F32 = jnp.float32
BF16 = jnp.bfloat16
ON_CHIP = pl.BlockSpec(memory_space=pltpu.VMEM)
SCALARS = pl.BlockSpec(memory_space=pltpu.SMEM)
IN_PLACE = pl.BlockSpec(memory_space=pltpu.HBM)


def near(array):
    return pltpu.with_memory_space_constraint(array, pltpu.VMEM)


def far(array):
    return pltpu.with_memory_space_constraint(array, pltpu.HBM)


def limit(mebibytes):
    return pltpu.CompilerParams(vmem_limit_bytes=mebibytes * 1024 * 1024)


def shape_near(shape, kind):
    return pltpu.VMEM(shape, kind)


def flat_view(array):
    lead, halves, count = array.shape[:-2], array.shape[-2], array.shape[-1]
    tiles = count // LANES
    split = array.reshape(lead + (halves, tiles, LANES))
    return jnp.swapaxes(split, -3, -2).reshape(lead + (tiles * halves, LANES))


def from_flat(array, halves):
    lead, rows = array.shape[:-2], array.shape[-2]
    tiles = rows // halves
    split = jnp.swapaxes(array.reshape(lead + (tiles, halves, LANES)), -3, -2)
    return split.reshape(lead + (halves, tiles * LANES))


def dot_nt(left, right):
    return lax.dot_general(left, right, (((1,), (1,)), ((), ())), preferred_element_type=F32)


def dot_nn(left, right):
    return lax.dot_general(left, right, (((1,), (0,)), ((), ())), preferred_element_type=F32)


def split_bf16(value):
    top = value.astype(BF16)
    return top, (value - top.astype(F32)).astype(BF16)


def narrow(flat, own, halves, legendre=None):
    reals, comps, slots, rows, lanes = flat.shape
    tiles = rows // halves
    pitch = rows + 8
    extra = 0 if legendre is None else 1

    def kernel(x_ref, *rest):
        o_ref = rest[extra]
        buffer, arrived = rest[-2:]
        index = lax.axis_index("comp")
        slot = index if own else 1 - index
        copies = [
            pltpu.make_async_copy(
                x_ref.at[:, comp, slot],
                buffer.at[comp, :, pl.ds(0, rows), :],
                arrived.at[comp],
            )
            for comp in range(comps)
        ]
        if extra:
            copies.append(pltpu.make_async_copy(rest[0], rest[2], arrived.at[comps]))
        for copy in copies:
            copy.start()
        lines = buffer.reshape(comps * reals * pitch, lanes)
        for comp in range(comps):
            copies[comp].wait()
            for tile in range(tiles):
                for half in range(halves):
                    start = comp * reals * pitch + tile * halves + half
                    picked = lines[pl.ds(start, reals, stride=pitch), :]
                    o_ref[
                        comp,
                        half * reals : (half + 1) * reals,
                        tile * lanes : (tile + 1) * lanes,
                    ] = picked.astype(BF16)
        if extra:
            copies[comps].wait()

    shape = shape_near((comps, halves * reals, tiles * lanes), BF16)
    operands = [far(flat)] if legendre is None else [far(flat), far(legendre)]
    shapes = (shape,) if legendre is None else (shape, shape_near(legendre.shape, BF16))
    return pl.pallas_call(
        kernel,
        compiler_params=limit(4),
        out_shape=shapes,
        in_specs=[IN_PLACE] * (1 + extra),
        out_specs=(ON_CHIP,) * (1 + extra),
        scratch_shapes=[
            pltpu.VMEM((comps, reals, pitch, lanes), F32),
            pltpu.SemaphoreType.DMA((comps + extra,)),
        ],
    )(*operands)


def synthesize(mixing, lmax, m_table, beam, own, received, legendre, sectors, chunk):
    comps, lines, count = own.shape
    bands = beam.shape[0]
    cycles = legendre.shape[1]
    sector = cycles // sectors
    parts = lines // 8

    def kernel(mix_ref, lmax_ref, m_ref, beam_ref, own_ref, got_ref, far_ref, o_ref, leg_ref, sems):
        index = lax.axis_index("comp")
        copies = [
            pltpu.make_async_copy(
                far_ref.at[pl.ds(at, chunk)], leg_ref.at[pl.ds(at, chunk)], sems.at[at // chunk]
            )
            for at in range(0, count, chunk)
        ]
        for copy in copies:
            copy.start()
        least = m_ref[lax.axis_index("ma") * 2 + index]
        acc = None
        for at in range(0, count, chunk):
            span = slice(at, at + chunk)
            degree = at + lax.broadcasted_iota(jnp.int32, (1, chunk), 1)
            values = []
            for comp in range(comps):
                values.append((index * comps + comp, own_ref[comp, :, span].astype(F32)))
                values.append(((1 - index) * comps + comp, got_ref[comp, :, span].astype(F32)))
            coeffs = []
            for band in range(bands):
                total = None
                for column, value in values:
                    term = mix_ref[band, column] * value
                    total = term if total is None else total + term
                keep = (degree >= least) & (degree <= lmax_ref[band])
                scale = jnp.where(keep, beam_ref[band : band + 1, span], 0.0)
                coeffs.append((scale * total).astype(BF16))
            copies[at // chunk].wait()
            value = dot_nn(jnp.concatenate(coeffs, 0), leg_ref[span, :])
            acc = value if acc is None else acc + value
        for at in range(sectors):
            for band in range(bands):
                pieces = [
                    acc[
                        band * lines + part * 8 : band * lines + part * 8 + 8,
                        at * sector : (at + 1) * sector,
                    ]
                    for part in range(parts)
                ]
                o_ref[at, band * 8 : band * 8 + 8, :] = jnp.concatenate(pieces, 1).astype(BF16)

    return pl.pallas_call(
        kernel,
        compiler_params=limit(12),
        out_shape=shape_near((sectors, bands * 8, parts * sector), BF16),
        in_specs=[SCALARS] * 3 + [ON_CHIP] * 3 + [IN_PLACE],
        out_specs=ON_CHIP,
        scratch_shapes=[
            pltpu.VMEM((count, cycles), BF16),
            pltpu.SemaphoreType.DMA((count // chunk,)),
        ],
    )(mixing, lmax, m_table, beam, near(own), near(received), far(legendre))


def gram(after, table, noise_weight, pixel_mask, high, chunk):
    halves, slots, pixels = table.shape
    bands, sector, _ = noise_weight.shape
    lines = bands * sector
    rows = slots * slots
    steps = pixels // chunk

    def kernel(after_ref, table_ref, noise_ref, mask_ref, o_ref, acc_ref):
        step = pl.program_id(0)
        weight = noise_ref[...] * mask_ref[...].astype(F32)
        weight_top, weight_low = split_bf16(weight)
        tops = []
        for first in range(halves):
            for second in range(halves):
                for slot in range(slots):
                    product = table_ref[first, slot : slot + 1, :] * table_ref[second]
                    tops.append(product.astype(BF16))
        top = jnp.concatenate(tops, 0)
        value = dot_nt(top, weight_top) + dot_nt(top, weight_low)

        @pl.when(step == 0)
        def _():
            acc_ref[...] = value

        @pl.when(step > 0)
        def _():
            acc_ref[...] += value

        @pl.when(step == steps - 1)
        def _():
            for cross in range(2):
                for band in range(bands):
                    pieces = []
                    for half in range(halves):
                        other = half if cross == 0 else 1 - half
                        row = (half * halves + other) * rows
                        piece = acc_ref[row : row + rows, band * sector : (band + 1) * sector]
                        pieces += [piece] * high
                    o_ref[cross, band] = jnp.concatenate(pieces, 1)

    return pl.pallas_call(
        kernel,
        compiler_params=limit(16),
        out_shape=shape_near((2, bands, rows, halves * high * sector), F32),
        grid=(steps,),
        in_specs=[
            IN_PLACE,
            pl.BlockSpec((halves, slots, chunk), lambda i: (0, 0, i)),
            pl.BlockSpec((lines, chunk), lambda i: (0, i)),
            pl.BlockSpec((lines, chunk), lambda i: (0, i)),
        ],
        out_specs=pl.BlockSpec(
            (2, bands, rows, halves * high * sector), lambda i: (0, 0, 0, 0)
        ),
        scratch_shapes=[pltpu.VMEM((halves * halves * rows, lines), F32)],
    )(
        far(after),
        table,
        far(noise_weight.reshape(lines, pixels)),
        far(pixel_mask.reshape(lines, pixels)),
    )


def lane_sums(rows):
    return jnp.sum(rows.T, axis=0, keepdims=True)


def own_dots(after, mixing, lmax, beam, prior, direction, residual):
    reals, comps, slots, rows, lanes = direction.shape
    parts = 4
    size = reals // parts
    bands, count = beam.shape

    def kernel(mix_ref, lmax_ref, after_ref, beam_ref, prior_ref, d_ref, r_ref, p_ref, coef_ref,
               o_ref, dn_ref, rn_ref, arrived):
        copies = [
            [
                pltpu.make_async_copy(
                    source.at[pl.ds(part * size, size)],
                    target.at[pl.ds(part * size, size)],
                    arrived.at[which, part],
                )
                for part in range(parts)
            ]
            for which, (source, target) in enumerate(((d_ref, dn_ref), (r_ref, rn_ref)))
        ]
        for row in copies:
            for copy in row:
                copy.start()
        index = lax.axis_index("comp")
        degree = lax.broadcasted_iota(jnp.int32, (1, count), 1)
        for band in range(bands):
            cut = jnp.where(degree <= lmax_ref[band], beam_ref[band : band + 1, :], 0.0)
            coef_ref[band] = jnp.concatenate(
                [mix_ref[band, index * comps + comp] * cut for comp in range(comps)], 0
            )
        odd = lax.broadcasted_iota(jnp.int32, (8, lanes), 0) % 2 == 1
        for at in range(0, rows, 8):
            value = prior_ref[at : at + 8, :]
            p_ref[0, at : at + 8, :] = jnp.where(odd, pltpu.roll(value, 1, 0), value)
            p_ref[1, at : at + 8, :] = jnp.where(odd, value, pltpu.roll(value, 7, 0))
        folded = []
        for which, ref in enumerate((dn_ref, rn_ref)):
            for real in range(reals):
                if real % size == 0:
                    copies[which][real // size].wait()
                total = None
                for comp in range(comps):
                    for slot in range(slots):
                        value = ref[real, comp, slot]
                        term = value * value
                        if which == 0:
                            term = p_ref[comp] * term
                        total = term if total is None else total + term
                folded.append(jnp.sum(total, axis=0, keepdims=True))
        folded.append(jnp.zeros((lanes - 2 * reals, lanes), F32))
        o_ref[...] = lane_sums(jnp.concatenate(folded, 0))

    return pl.pallas_call(
        kernel,
        compiler_params=limit(8),
        out_shape=(
            shape_near((comps, rows, lanes), F32),
            shape_near((bands, comps, count), F32),
            shape_near((1, lanes), F32),
        ),
        in_specs=[SCALARS] * 2 + [IN_PLACE, ON_CHIP, ON_CHIP, IN_PLACE, IN_PLACE],
        out_specs=(ON_CHIP,) * 3,
        scratch_shapes=[
            pltpu.VMEM(direction.shape, F32),
            pltpu.VMEM(direction.shape, F32),
            pltpu.SemaphoreType.DMA((2, parts)),
        ],
    )(mixing, lmax, far(after), beam, prior, far(direction), far(residual))


def apply_gram(dots, grams, spread, copies, group):
    slots, lines, lanes = spread.shape
    bands = grams.shape[1]
    readers = slots // group
    sector = lanes // 4
    reals = 16

    def kernel(dots_ref, g_ref, x_ref, o_ref):
        product = None
        for band in range(bands):
            straight, turned = [], []
            for slot in range(slots):
                value = x_ref[slot, band * 8 : band * 8 + 8, :].astype(F32)
                straight.append(value)
                turned.append(pltpu.roll(value, lanes // 2, 1))
            for slot in range(slots):
                total = None
                for other in range(slots):
                    row = slot * slots + other
                    term = g_ref[0, band, row : row + 1, :] * straight[other]
                    term = term + g_ref[1, band, row : row + 1, :] * turned[other]
                    total = term if total is None else total + term
                total = total.astype(BF16)
                term = total.astype(F32) * straight[slot]
                product = term if product is None else product + term
                line = (slot % group) * lines + band * 8
                for copy in range(copies):
                    o_ref[copy * readers + slot // group, line : line + 8, :] = total
        product = product + pltpu.roll(product, lanes // 2, 1)
        halves = [product[:, :sector], product[:, sector : 2 * sector]]
        tall = jnp.concatenate(
            [
                jnp.concatenate([half, jnp.zeros((8, lanes - sector), F32)], 1)
                for half in halves
            ]
            + [jnp.zeros((lanes - 16, lanes), F32)],
            0,
        )
        shared = jnp.where(lax.axis_index("band") == 0, dots_ref[...], 0.0)
        value = lane_sums(tall) + shared
        top = value.astype(BF16).astype(F32)
        rest = value - top
        middle = rest.astype(BF16).astype(F32)
        last = (rest - middle).astype(BF16).astype(F32)
        row = top + pltpu.roll(middle, 2 * reals, 1) + pltpu.roll(last, 4 * reals, 1)
        tail = jnp.concatenate([row, jnp.zeros((7, lanes), F32)], 0).astype(BF16)
        for reader in range(copies * readers):
            o_ref[reader, group * lines : group * lines + 8, :] = tail

    return pl.pallas_call(
        kernel,
        compiler_params=limit(4),
        out_shape=shape_near((copies * readers, group * lines + 8, lanes), BF16),
        in_specs=[ON_CHIP] * 3,
        out_specs=ON_CHIP,
    )(near(dots), near(grams), near(spread))


def analyze(m_table, own, received, own_leg, got_leg, coefs, prior, direction, residual,
            bands, sectors, halves, copies, chunk):
    reals, comps, slots, rows, lanes = direction.shape
    groups = len(coefs)
    total_bands = groups * bands
    count, cycles = own_leg.shape
    sector = cycles // sectors
    high = reals // 8
    lines = halves * reals
    tiles = chunk // lanes
    block_rows = tiles * halves
    pitch = comps * block_rows + 8
    per_slot = bands * 8
    slab = sectors // 2
    tail = slots * per_slot
    pieces_count = 2

    def kernel(m_ref, own_ref, got_ref, own_leg_ref, got_leg_ref, *rest):
        coef_refs = rest[:groups]
        (prior_ref, d_ref, r_ref, new_ref, sums_ref, small_ref, back_ref, h_ref, h2_ref, s_ref,
         step_ref, leg_ref, dn_ref, rn_ref, arrived) = rest[groups:]
        index_comp = lax.axis_index("comp")
        index_band = lax.axis_index("band")
        places = (index_comp, 1 - index_comp)
        is_first = index_comp == 0
        sources = (own_leg_ref, got_leg_ref)
        copies_of = []
        for turn in range(slots):
            for piece in range(pieces_count):
                size = count // pieces_count
                span = pl.ds(piece * size, size)
                size = rows // pieces_count
                lines_span = pl.ds(piece * size, size)
                index = turn * pieces_count + piece
                copies_of.append(
                    [
                        pltpu.make_async_copy(
                            sources[turn].at[span], leg_ref.at[turn, span], arrived.at[index, 0]
                        )
                    ]
                    + [
                        pltpu.make_async_copy(
                            source.at[:, :, places[turn], lines_span],
                            target.at[turn, :, :, lines_span],
                            arrived.at[index, 1 + which],
                        )
                        for which, (source, target) in enumerate(
                            ((d_ref, dn_ref), (r_ref, rn_ref))
                        )
                    ]
                )
        for triple in copies_of:
            for copy in triple:
                copy.start()

        total = None
        for ref in (own_ref, got_ref):
            for at in range(groups * slab):
                value = ref[at, tail : tail + 8, :].astype(F32)
                total = value if total is None else total + value
        line = total[0:1, :]
        line = (
            line
            + pltpu.roll(line, lanes - 2 * reals, 1)
            + pltpu.roll(line, lanes - 4 * reals, 1)
        )
        norm_old = line[:, reals : 2 * reals]
        step_size = norm_old / line[:, :reals]
        small_ref[...] = jnp.concatenate(
            [step_size, norm_old, jnp.zeros((1, lanes - 2 * reals), F32)], 1
        )
        for real in range(reals):
            step_ref[real] = jnp.broadcast_to(step_size[:, real : real + 1], (8, lanes))

        for turn in range(slots):
            base = places[turn] * per_slot
            for group in range(groups):
                source = (index_band ^ group) * slab
                for band in range(bands):
                    start = pl.multiple_of(base + band * 8, 8)
                    for part in range(lines // 8):
                        span = slice(part * sector, (part + 1) * sector)
                        pieces = []
                        for z in range(slab):
                            mine = own_ref[source + z, pl.ds(start, 8), :].astype(F32)
                            theirs = got_ref[source + z, pl.ds(start, 8), :].astype(F32)
                            pieces.append(jnp.where(is_first, mine, theirs)[:, span])
                            pieces.append(jnp.where(is_first, theirs, mine)[:, span])
                        row = (group * bands + band) * lines + part * 8
                        back_ref[turn, row : row + 8, :] = jnp.concatenate(pieces, 1).astype(BF16)

        buffers = (h_ref, h2_ref)
        work = [(turn, at) for turn in range(slots) for at in range(0, count, chunk)]

        def multiply(index):
            turn, at = work[index]
            if at % (count // pieces_count) == 0:
                copies_of[turn * pieces_count + at * pieces_count // count][0].wait()
            buffers[index % 2][...] = dot_nt(back_ref[turn], leg_ref[turn, at : at + chunk, :])

        lane = lax.broadcasted_iota(jnp.int32, (lines, lanes), 1)
        norms = [None] * reals
        multiply(0)
        for index, (turn, at) in enumerate(work):
            if index + 1 < len(work):
                multiply(index + 1)
            h = buffers[index % 2]
            least = m_ref[lax.axis_index("ma") * 2 + places[turn]]
            for tile in range(tiles):
                part = slice(tile * lanes, (tile + 1) * lanes)
                here = slice(at + tile * lanes, at + (tile + 1) * lanes)
                totals = [None] * comps
                for group in range(groups):
                    for band in range(bands):
                        row = (group * bands + band) * lines
                        value = h[row : row + lines, part]
                        for comp in range(comps):
                            term = coef_refs[group][band, comp : comp + 1, here] * value
                            totals[comp] = term if totals[comp] is None else totals[comp] + term
                keep = lane >= least - (at + tile * lanes)
                for comp in range(comps):
                    total = jnp.where(keep, totals[comp], 0.0)
                    for half in range(halves):
                        start = comp * block_rows + tile * halves + half
                        s_ref[index % 2, pl.ds(start, reals, stride=pitch), :] = total[
                            half * reals : (half + 1) * reals
                        ]
            first = at // lanes * halves
            if at % (count // pieces_count) == 0:
                for copy in copies_of[turn * pieces_count + at * pieces_count // count][1:]:
                    copy.wait()
            for real in range(reals):
                for comp in range(comps):
                    for sub in range(0, block_rows, 8):
                        span = slice(first + sub, first + sub + 8)
                        line = real * pitch + comp * block_rows + sub
                        d = dn_ref[turn, real, comp, span, :]
                        r = rn_ref[turn, real, comp, span, :]
                        image = prior_ref[comp, span, :] * d + s_ref[index % 2, line : line + 8, :]
                        new = r - step_ref[real] * image
                        new_ref[real, comp, places[turn], span, :] = new
                        term = new * new
                        norms[real] = term if norms[real] is None else norms[real] + term
        folded = [jnp.sum(norm, axis=0, keepdims=True) for norm in norms]
        folded.append(jnp.zeros((lanes - reals, lanes), F32))
        norm = lane_sums(jnp.concatenate(folded, 0))
        for at in range(copies):
            sums_ref[at] = norm

    return pl.pallas_call(
        kernel,
        compiler_params=limit(24),
        out_shape=(
            shape_near(direction.shape, F32),
            shape_near((copies, 1, lanes), F32),
            shape_near((1, lanes), F32),
        ),
        in_specs=[SCALARS] + [ON_CHIP] * 2 + [IN_PLACE] * 2 + [ON_CHIP] * (1 + groups)
        + [IN_PLACE] * 2,
        out_specs=(ON_CHIP,) * 3,
        scratch_shapes=[
            pltpu.VMEM((slots, total_bands * lines, cycles), BF16),
            pltpu.VMEM((total_bands * lines, chunk), F32),
            pltpu.VMEM((total_bands * lines, chunk), F32),
            pltpu.VMEM((2, reals * pitch, lanes), F32),
            pltpu.VMEM((reals, 8, lanes), F32),
            pltpu.VMEM((slots, count, cycles), BF16),
            pltpu.VMEM((slots, reals, comps, rows, lanes), F32),
            pltpu.VMEM((slots, reals, comps, rows, lanes), F32),
            pltpu.SemaphoreType.DMA((slots * pieces_count, 3)),
        ],
    )(
        m_table, near(own), near(received), far(own_leg), far(got_leg),
        *(near(x) for x in (*coefs, prior)), far(direction), far(residual),
    )


def advance(small, solution, direction, new_residual):
    reals, comps, slots, rows, lanes = direction.shape
    parts = 4
    size = reals // parts

    def kernel(small_ref, x_ref, d_ref, r_ref, ox_ref, or_ref, x_buffer, d_buffer, o_buffer, sems):
        out = pltpu.make_async_copy(r_ref, or_ref, sems.at[3, 0])
        loads = [
            pltpu.make_async_copy(
                source.at[pl.ds(part * size, size)], target.at[pl.ds(part * size, size)],
                sems.at[which, part],
            )
            for part in range(parts)
            for which, (source, target) in enumerate(((x_ref, x_buffer), (d_ref, d_buffer)))
        ]
        stores = [
            pltpu.make_async_copy(
                o_buffer.at[pl.ds(part * size, size)], ox_ref.at[pl.ds(part * size, size)],
                sems.at[2, part],
            )
            for part in range(parts)
        ]
        for load in loads:
            load.start()
        out.start()
        for part in range(parts):
            loads[2 * part].wait()
            loads[2 * part + 1].wait()
            for real in range(part * size, (part + 1) * size):
                step = small_ref[0:1, real : real + 1]
                o_buffer[real] = x_buffer[real] + step[None, None] * d_buffer[real]
            stores[part].start()
        for store in stores:
            store.wait()
        out.wait()

    shape = jax.ShapeDtypeStruct(direction.shape, F32)
    return pl.pallas_call(
        kernel,
        compiler_params=limit(10),
        out_shape=(shape, shape),
        in_specs=[ON_CHIP, IN_PLACE, IN_PLACE, ON_CHIP],
        out_specs=(IN_PLACE, IN_PLACE),
        scratch_shapes=[pltpu.VMEM(direction.shape, F32)] * 3
        + [pltpu.SemaphoreType.DMA((4, parts))],
    )(near(small), far(solution), far(direction), near(new_residual))


def turn_direction(norms, small, direction, new_residual):
    reals, comps, slots, rows, lanes = direction.shape
    sources = norms.shape[0]
    parts = 4
    size = reals // parts

    def kernel(norms_ref, small_ref, d_ref, r_ref, o_ref, d_buffer, buffer, sems):
        loads = [
            pltpu.make_async_copy(
                d_ref.at[pl.ds(part * size, size)], d_buffer.at[pl.ds(part * size, size)],
                sems.at[0, part],
            )
            for part in range(parts)
        ]
        for load in loads:
            load.start()
        total = norms_ref[0]
        for at in range(1, sources):
            total = total + norms_ref[at]
        ratio = total[:, :reals] / small_ref[:, reals : 2 * reals]
        stores = [
            pltpu.make_async_copy(
                buffer.at[pl.ds(part * size, size)], o_ref.at[pl.ds(part * size, size)],
                sems.at[1, part],
            )
            for part in range(parts)
        ]
        for part in range(parts):
            loads[part].wait()
            for real in range(part * size, (part + 1) * size):
                one = ratio[:, real : real + 1]
                buffer[real] = r_ref[real] + one[None, None] * d_buffer[real]
            stores[part].start()
        for store in stores:
            store.wait()

    return pl.pallas_call(
        kernel,
        compiler_params=limit(8),
        out_shape=jax.ShapeDtypeStruct(direction.shape, F32),
        in_specs=[ON_CHIP, ON_CHIP, IN_PLACE, ON_CHIP],
        out_specs=IN_PLACE,
        scratch_shapes=[pltpu.VMEM(direction.shape, F32)] * 2
        + [pltpu.SemaphoreType.DMA((2, parts))],
    )(near(norms), near(small), far(direction), near(new_residual))


def phase_table(m_table, pixels):
    columns = jnp.arange(pixels, dtype=jnp.int32)
    wrapped = m_table[:, None] * columns[None, :] % pixels
    angles = wrapped.astype(jnp.float32) * (2.0 * math.pi / pixels)
    weights = jnp.where(m_table == 0, 1.0, 2.0).astype(jnp.float32)[:, None] / math.sqrt(pixels)
    return jnp.stack([weights * jnp.cos(angles), -weights * jnp.sin(angles)], axis=1).astype(
        jnp.bfloat16
    )


def swap_parts(parts, axis):
    count = lax.axis_size(axis)
    got = [parts[0]]
    for step in range(1, count):
        pairs = [(i, (i + step) % count) for i in range(count)]
        got.append(lax.ppermute(parts[step], axis, pairs))
    return got


def widen(values):
    return values[:, None, None, None, None]


def general(
    solution,
    residual,
    direction,
    prior_inv,
    mixing,
    beam,
    band_lmax,
    m_table,
    legendre,
    noise_weight,
    pixel_mask,
):
    band_count = lax.axis_size("band")
    slab_count = lax.axis_size("ma")
    comp_count = lax.axis_size("comp")
    comp_index = lax.axis_index("comp")
    slab_index = lax.axis_index("ma")
    reals, comps, slots, halves, degrees_count = direction.shape
    half_count = legendre.shape[0]
    bands = mixing.shape[0]
    cycles = legendre.shape[2]
    sector = noise_weight.shape[1]
    pixels = noise_weight.shape[2]
    sectors = slab_count * comp_count
    degrees = jnp.arange(degrees_count, dtype=jnp.int32)
    f32 = jnp.float32
    bf16 = jnp.bfloat16

    first_slot = (slab_index * comp_count + comp_index) * half_count
    local_m = lax.dynamic_slice_in_dim(m_table, first_slot, half_count)
    upper = degrees[None, :] <= band_lmax[:, None]
    cut_beam = beam * upper.astype(f32)
    lower = degrees[None, :] >= local_m[:, None]
    scale = cut_beam[:, None, :] * lower[None].astype(f32)

    low = jnp.transpose(direction, (2, 1, 3, 0, 4)).astype(bf16)
    low = low.reshape((comp_count, half_count) + low.shape[1:])
    relative = [
        lax.dynamic_index_in_dim(low, (comp_index + step) % comp_count, 0, keepdims=False)
        for step in range(comp_count)
    ]
    got = swap_parts(relative, "comp")
    mixed = None
    for step in range(comp_count):
        source = (comp_index - step) % comp_count
        columns = lax.dynamic_slice_in_dim(mixing, source * comps, comps, 1)
        for comp in range(comps):
            term = columns[:, comp][:, None, None, None, None] * got[step][None, :, comp].astype(f32)
            mixed = term if mixed is None else mixed + term
    coeffs = (scale[:, :, None, None, :] * mixed).astype(bf16)
    cycle_values = jnp.einsum(
        "bmqnl,mlr->bmqnr", coeffs, legendre, preferred_element_type=f32
    ).astype(bf16)
    send = cycle_values.reshape(bands, half_count, halves, reals, sectors, sector)
    send = jnp.transpose(send, (4, 1, 2, 3, 0, 5)).reshape(
        sectors, half_count * halves, reals, bands * sector
    )
    spread = lax.all_to_all(send, ("ma", "comp"), 0, 0, tiled=True)
    rows = sectors * half_count * halves
    spread = spread.reshape(rows, reals, bands * sector).astype(f32)

    table = phase_table(m_table, pixels).reshape(rows, pixels)
    weight = (noise_weight * pixel_mask.astype(f32)).reshape(bands * sector, pixels)
    if rows <= 2 * reals:
        pairs = (table.astype(f32)[:, None, :] * table.astype(f32)[None, :, :]).reshape(
            rows * rows, pixels
        )
        gram = lax.dot_general(
            pairs, weight, (((1,), (1,)), ((), ())), precision=lax.Precision.HIGH,
            preferred_element_type=f32,
        ).reshape(rows, rows, 1, bands * sector)
        back = (gram * spread[None]).sum(1).astype(bf16)
    else:
        sky = jnp.einsum("knx,kj->nxj", spread.astype(bf16), table, preferred_element_type=f32)
        weighted = (weight[None] * sky).astype(bf16)
        back = jnp.einsum("nxj,kj->knx", weighted, table, preferred_element_type=f32).astype(bf16)

    back = back.reshape(sectors, half_count * halves, reals, bands * sector)
    everyone = jnp.broadcast_to(back[None], (band_count,) + back.shape).reshape(
        (band_count * sectors,) + back.shape[1:]
    )
    gathered = lax.all_to_all(everyone, ("band", "ma", "comp"), 0, 0, tiled=True)
    gathered = gathered.reshape(
        band_count, sectors, half_count, halves, reals, bands, sector
    )
    total_bands = band_count * bands
    own_back = jnp.transpose(gathered, (2, 0, 5, 3, 4, 1, 6)).reshape(
        half_count, total_bands, halves, reals, cycles
    )
    all_back = swap_parts([own_back] * comp_count, "comp")
    all_legendre = swap_parts([legendre] * comp_count, "comp")

    packed = jnp.concatenate([cut_beam, jnp.pad(mixing, ((0, 0), (0, 128 - mixing.shape[1])))], 1)
    packed = lax.all_to_all(
        jnp.broadcast_to(packed[None], (band_count,) + packed.shape), "band", 0, 0, tiled=True
    ).reshape(total_bands, -1)
    all_beam = packed[:, :degrees_count]
    all_mixing = packed[:, degrees_count : degrees_count + mixing.shape[1]]
    own_mixing = lax.dynamic_slice_in_dim(all_mixing, comp_index * comps, comps, 1)
    coef = own_mixing[:, :, None] * all_beam[:, None, :]

    parts = []
    for step in range(comp_count):
        source = (comp_index - step) % comp_count
        slot_m = lax.dynamic_slice_in_dim(
            m_table, (slab_index * comp_count + source) * half_count, half_count
        )
        harmonic = jnp.einsum(
            "mbqnr,mlr->bmqnl", all_back[step], all_legendre[step], preferred_element_type=f32
        )
        total = jnp.zeros((comps, half_count, halves, reals, degrees_count), f32)
        for band in range(total_bands):
            total = total + coef[band][:, None, None, None, :] * harmonic[band][None]
        keep = degrees[None, :] >= slot_m[:, None]
        parts.append(jnp.where(keep[None, :, None, None, :], total, 0.0))
    ordered = [
        lax.dynamic_index_in_dim(
            jnp.stack(parts), (comp_index - position) % comp_count, 0, keepdims=False
        )
        for position in range(comp_count)
    ]
    returned = jnp.concatenate(ordered, axis=1)
    returned = jnp.transpose(returned, (3, 0, 1, 2, 4))
    image = prior_inv[None, :, None, None, :] * direction + returned
    axes = (1, 2, 3, 4)
    sums = jnp.stack(
        [
            jnp.sum(residual * residual, axis=axes),
            jnp.sum(direction * image, axis=axes),
            jnp.sum(residual * image, axis=axes),
            jnp.sum(image * image, axis=axes),
        ]
    )
    sums = lax.all_to_all(
        jnp.broadcast_to(sums[None], (sectors,) + sums.shape), ("ma", "comp"), 0, 0, tiled=True
    ).sum(0)
    norm_old, curvature_sum, cross_sum, image_norm = sums
    step_size = norm_old / curvature_sum
    new_solution = solution + widen(step_size) * direction
    new_residual = residual - widen(step_size) * image
    norm_new = norm_old - 2.0 * step_size * cross_sum + step_size * step_size * image_norm
    new_direction = new_residual + widen(norm_new / norm_old) * direction
    return (new_solution, new_residual, new_direction)


def phase_rows(m_table, pixels):
    columns = jnp.arange(pixels, dtype=jnp.int32)
    wrapped = m_table[:, None] * columns[None, :] % pixels
    angles = wrapped.astype(F32) * (2.0 * math.pi / pixels)
    weights = jnp.where(m_table == 0, 1.0, 2.0).astype(F32)[:, None] / math.sqrt(pixels)
    rows = jnp.stack([weights * jnp.cos(angles), -weights * jnp.sin(angles)], axis=0)
    return rows.astype(BF16).astype(F32)


def fast(
    solution,
    residual,
    direction,
    prior_inv,
    mixing,
    beam,
    band_lmax,
    m_table,
    legendre,
    noise_weight,
    pixel_mask,
):
    band_count = lax.axis_size("band")
    slab_count = lax.axis_size("ma")
    comp_count = lax.axis_size("comp")
    reals, comps, slots, halves, count = direction.shape
    bands, sector, pixels = noise_weight.shape
    sectors = slab_count * comp_count
    high = reals // 8
    exchange = [(0, 1), (1, 0)]
    legendre = legendre[0]
    flat_direction = flat_view(direction)
    flat_residual = flat_view(residual)
    flat_solution = flat_view(solution)

    (sent,) = narrow(flat_direction, False, halves)
    received = lax.ppermute(sent, "comp", exchange)
    (own,) = narrow(flat_direction, True, halves)
    packed = synthesize(
        mixing, band_lmax, m_table, beam, own, received, legendre, sectors, 1024
    )
    spread = lax.all_to_all(packed, ("ma", "comp"), 0, 0, tiled=True)
    other_legendre = lax.ppermute(legendre, "comp", exchange)

    table = phase_rows(m_table, pixels)
    grams = gram(packed, table, noise_weight, pixel_mask, high, 1024)
    prior, own_coef, dots = own_dots(
        packed, mixing, band_lmax, beam, flat_view(prior_inv), flat_direction, flat_residual
    )
    back = apply_gram(dots, grams, spread, band_count, comp_count)
    arrived = lax.all_to_all(back, ("band", "ma"), 0, 0, tiled=True)
    coefs = [own_coef] + [
        lax.ppermute(own_coef, "band", [(i, i ^ step) for i in range(band_count)])
        for step in range(1, band_count)
    ]
    arrived, coefs = lax.optimization_barrier((arrived, coefs))
    other_arrived = lax.ppermute(arrived, "comp", exchange)
    new_residual, norms, small = analyze(
        m_table, arrived, other_arrived, legendre, other_legendre, coefs, prior,
        flat_direction, flat_residual, bands, sectors, halves, sectors, 512,
    )
    norms = lax.all_to_all(norms, ("ma", "comp"), 0, 0, tiled=True)
    new_solution, out_residual = advance(small, flat_solution, flat_direction, new_residual)
    norms, new_solution, out_residual = lax.optimization_barrier(
        (norms, new_solution, out_residual)
    )
    new_direction = turn_direction(norms, small, flat_direction, new_residual)
    return tuple(from_flat(out, halves) for out in (new_solution, out_residual, new_direction))


def body(*args):
    direction, legendre, noise_weight = args[2], args[8], args[9]
    reals, comps, slots, halves, count = direction.shape
    bands, sector, pixels = noise_weight.shape
    comp_count = lax.axis_size("comp")
    all_slots = lax.axis_size("ma") * comp_count * legendre.shape[0]
    fits = (
        comp_count == 2
        and slots == 2
        and legendre.shape[0] == 1
        and halves == 2
        and reals % 8 == 0
        and reals == 16
        and halves * (reals // 8) * sector == LANES
        and count % 1024 == 0
        and pixels % 1024 == 0
        and all_slots == 8
        and lax.axis_size("band") == 4
    )
    return fast(*args) if fits else general(*args)


def solution(mesh):
    in_specs = (
        P(None, "comp", "ma", None, None),
        P(None, "comp", "ma", None, None),
        P(None, "comp", "ma", None, None),
        P("comp", None),
        P("band", None),
        P("band", None),
        P("band"),
        P(),
        P(("ma", "comp"), None, None),
        P("band", ("ma", "comp"), None),
        P("band", ("ma", "comp"), None),
    )
    out_specs = (
        P(None, "comp", "ma", None, None),
        P(None, "comp", "ma", None, None),
        P(None, "comp", "ma", None, None),
    )
    return jax.shard_map(body, mesh=mesh, in_specs=in_specs, out_specs=out_specs, check_vma=False)
```

```python
import math

import jax
import jax.numpy as jnp
from jax import lax
from jax.experimental import pallas as pl
from jax.experimental.pallas import tpu as pltpu
from jax.sharding import PartitionSpec as P

LANES = 128
F32 = jnp.float32
BF16 = jnp.bfloat16
ON_CHIP = pl.BlockSpec(memory_space=pltpu.VMEM)
SCALARS = pl.BlockSpec(memory_space=pltpu.SMEM)
IN_PLACE = pl.BlockSpec(memory_space=pltpu.HBM)


def near(array):
    return pltpu.with_memory_space_constraint(array, pltpu.VMEM)


def far(array):
    return pltpu.with_memory_space_constraint(array, pltpu.HBM)


def limit(mebibytes):
    return pltpu.CompilerParams(vmem_limit_bytes=mebibytes * 1024 * 1024)


def shape_near(shape, kind):
    return pltpu.VMEM(shape, kind)


def flat_view(array):
    lead, halves, count = array.shape[:-2], array.shape[-2], array.shape[-1]
    tiles = count // LANES
    split = array.reshape(lead + (halves, tiles, LANES))
    return jnp.swapaxes(split, -3, -2).reshape(lead + (tiles * halves, LANES))


def from_flat(array, halves):
    lead, rows = array.shape[:-2], array.shape[-2]
    tiles = rows // halves
    split = jnp.swapaxes(array.reshape(lead + (tiles, halves, LANES)), -3, -2)
    return split.reshape(lead + (halves, tiles * LANES))


def dot_nt(left, right):
    return lax.dot_general(left, right, (((1,), (1,)), ((), ())), preferred_element_type=F32)


def dot_nn(left, right):
    return lax.dot_general(left, right, (((1,), (0,)), ((), ())), preferred_element_type=F32)


def split_bf16(value):
    top = value.astype(BF16)
    return top, (value - top.astype(F32)).astype(BF16)


def narrow(flat, own, halves, mixing=None, lmax=None, beam=None):
    reals, comps, slots, rows, lanes = flat.shape
    tiles = rows // halves
    pitch = rows + 8
    extra = 0 if beam is None else 3

    def kernel(x_ref, *rest):
        o_ref = rest[extra]
        buffer, arrived = rest[-2:]
        index = lax.axis_index("comp")
        slot = index if own else 1 - index
        copies = [
            pltpu.make_async_copy(
                x_ref.at[:, comp, slot],
                buffer.at[comp, :, pl.ds(0, rows), :],
                arrived.at[comp],
            )
            for comp in range(comps)
        ]
        for copy in copies:
            copy.start()
        if extra:
            mix_ref, lmax_ref, beam_ref = rest[:extra]
            coef_ref = rest[extra + 1]
            bands, count = beam.shape
            degree = lax.broadcasted_iota(jnp.int32, (1, count), 1)
            for band in range(bands):
                cut = jnp.where(degree <= lmax_ref[band], beam_ref[band : band + 1, :], 0.0)
                coef_ref[band] = jnp.concatenate(
                    [mix_ref[band, index * comps + comp] * cut for comp in range(comps)], 0
                )
        lines = buffer.reshape(comps * reals * pitch, lanes)
        for comp in range(comps):
            copies[comp].wait()
            for tile in range(tiles):
                for half in range(halves):
                    start = comp * reals * pitch + tile * halves + half
                    picked = lines[pl.ds(start, reals, stride=pitch), :]
                    o_ref[
                        comp,
                        half * reals : (half + 1) * reals,
                        tile * lanes : (tile + 1) * lanes,
                    ] = picked.astype(BF16)

    shapes = (shape_near((comps, halves * reals, tiles * lanes), BF16),)
    operands = (far(flat),)
    specs = [IN_PLACE]
    if extra:
        shapes += (shape_near((beam.shape[0], comps, beam.shape[1]), F32),)
        operands += (mixing, lmax, beam)
        specs += [SCALARS, SCALARS, ON_CHIP]
    return pl.pallas_call(
        kernel,
        compiler_params=limit(4),
        out_shape=shapes,
        in_specs=specs,
        out_specs=(ON_CHIP,) * len(shapes),
        scratch_shapes=[
            pltpu.VMEM((comps, reals, pitch, lanes), F32),
            pltpu.SemaphoreType.DMA((comps,)),
        ],
    )(*operands)


def synthesize(mixing, lmax, m_table, beam, own, received, legendre, sectors, chunk):
    comps, lines, count = own.shape
    bands = beam.shape[0]
    cycles = legendre.shape[1]
    sector = cycles // sectors
    parts = lines // 8

    def kernel(mix_ref, lmax_ref, m_ref, beam_ref, own_ref, got_ref, far_ref, o_ref, leg_ref, coef_ref, sem):
        index = lax.axis_index("comp")
        copy = pltpu.make_async_copy(far_ref, leg_ref, sem)
        copy.start()
        least = m_ref[lax.axis_index("ma") * 2 + index]
        width = 2 * comps * lines
        column = lax.broadcasted_iota(jnp.int32, (lines, width), 1)
        diagonal = column % lines == lax.broadcasted_iota(jnp.int32, (lines, width), 0)
        tops, lows = [], []
        for band in range(bands):
            weight = jnp.zeros((lines, width), F32)
            for turn, group in enumerate((index, 1 - index)):
                for comp in range(comps):
                    here = diagonal & (column // lines == turn * comps + comp)
                    weight = jnp.where(here, mix_ref[band, group * comps + comp], weight)
            top, low = split_bf16(weight)
            tops.append(top)
            lows.append(low)
        weights = jnp.concatenate([jnp.concatenate(tops, 0), jnp.concatenate(lows, 0)], 1)
        for at in range(0, count, chunk):
            span = slice(at, at + chunk)
            degree = at + lax.broadcasted_iota(jnp.int32, (1, chunk), 1)
            stacked = [
                ref[comp, :, span] for ref in (own_ref, got_ref) for comp in range(comps)
            ]
            mixed = dot_nn(weights, jnp.concatenate(stacked + stacked, 0))
            for band in range(bands):
                keep = (degree >= least) & (degree <= lmax_ref[band])
                scale = jnp.where(keep, beam_ref[band : band + 1, span], 0.0)
                coef_ref[band * lines : (band + 1) * lines, span] = (
                    scale * mixed[band * lines : (band + 1) * lines]
                ).astype(BF16)
        copy.wait()
        acc = dot_nn(coef_ref[...], leg_ref[...])
        for at in range(sectors):
            for band in range(bands):
                pieces = [
                    acc[
                        band * lines + part * 8 : band * lines + part * 8 + 8,
                        at * sector : (at + 1) * sector,
                    ]
                    for part in range(parts)
                ]
                o_ref[at, band * 8 : band * 8 + 8, :] = jnp.concatenate(pieces, 1).astype(BF16)

    return pl.pallas_call(
        kernel,
        compiler_params=limit(12),
        out_shape=shape_near((sectors, bands * 8, parts * sector), BF16),
        in_specs=[SCALARS] * 3 + [ON_CHIP] * 3 + [IN_PLACE],
        out_specs=ON_CHIP,
        scratch_shapes=[
            pltpu.VMEM((count, cycles), BF16),
            pltpu.VMEM((bands * lines, count), BF16),
            pltpu.SemaphoreType.DMA,
        ],
    )(mixing, lmax, m_table, beam, near(own), near(received), far(legendre))


def gram(after, table, noise_weight, pixel_mask, high, chunk):
    halves, slots, pixels = table.shape
    bands, sector, _ = noise_weight.shape
    lines = bands * sector
    rows = slots * slots
    pairs = ((0, 0), (0, 1), (1, 1))

    def kernel(after_ref, table_ref, noise_ref, mask_ref, o_ref, nn_ref, mn_ref, top_ref,
               weight_ref, sum_ref, sems):
        copies = [
            pltpu.make_async_copy(source, target, sems.at[which])
            for which, (source, target) in enumerate(((noise_ref, nn_ref), (mask_ref, mn_ref)))
        ]
        for copy in copies:
            copy.start()
        for at in range(0, pixels, chunk):
            span = slice(at, at + chunk)
            for which, (first, second) in enumerate(pairs):
                right = table_ref[second, :, span]
                for slot in range(0, slots, 2):
                    products = [
                        table_ref[first, at_slot : at_slot + 1, span] * right
                        for at_slot in (slot, slot + 1)
                    ]
                    row = which * rows + slot * slots
                    top_ref[row : row + 2 * slots, span] = jnp.concatenate(products, 0).astype(
                        BF16
                    )
        for copy in copies:
            copy.wait()
        for at in range(0, pixels, chunk):
            span = slice(at, at + chunk)
            weight = nn_ref[:, span] * mn_ref[:, span].astype(F32)
            top, low = split_bf16(weight)
            weight_ref[:lines, span] = top
            weight_ref[lines:, span] = low
        acc = dot_nt(top_ref[...], weight_ref[...])
        sum_ref[...] = acc[:, :lines] + acc[:, lines:]
        for band in range(bands):
            span = slice(band * sector, (band + 1) * sector)
            blocks = [sum_ref[at * rows : (at + 1) * rows, span] for at in range(len(pairs))]
            turned = jnp.concatenate(
                [
                    sum_ref[pl.ds(rows + slot, slots, stride=slots), :]
                    for slot in range(slots)
                ],
                0,
            )[:, span]
            o_ref[0, band] = jnp.concatenate([blocks[0]] * high + [blocks[2]] * high, 1)
            o_ref[1, band] = jnp.concatenate([blocks[1]] * high + [turned] * high, 1)

    return pl.pallas_call(
        kernel,
        compiler_params=limit(16),
        out_shape=shape_near((2, bands, rows, halves * high * sector), F32),
        in_specs=[IN_PLACE, ON_CHIP, IN_PLACE, IN_PLACE],
        out_specs=ON_CHIP,
        scratch_shapes=[
            pltpu.VMEM((lines, pixels), F32),
            pltpu.VMEM((lines, pixels), jnp.int32),
            pltpu.VMEM((len(pairs) * rows, pixels), BF16),
            pltpu.VMEM((2 * lines, pixels), BF16),
            pltpu.VMEM((len(pairs) * rows, lines), F32),
            pltpu.SemaphoreType.DMA((2,)),
        ],
    )(
        far(after),
        near(table),
        far(noise_weight.reshape(lines, pixels)),
        far(pixel_mask.reshape(lines, pixels)),
    )


def lane_sums(rows):
    return jnp.sum(rows.T, axis=0, keepdims=True)


def own_dots(after, prior, direction, residual):
    reals, comps, slots, rows, lanes = direction.shape
    parts = 4
    size = reals // parts

    def kernel(after_ref, prior_ref, d_ref, r_ref, p_ref, o_ref, dn_ref, rn_ref, arrived):
        copies = [
            [
                pltpu.make_async_copy(
                    source.at[pl.ds(part * size, size)],
                    target.at[pl.ds(part * size, size)],
                    arrived.at[which, part],
                )
                for part in range(parts)
            ]
            for which, (source, target) in enumerate(((d_ref, dn_ref), (r_ref, rn_ref)))
        ]
        for row in copies:
            for copy in row:
                copy.start()
        odd = lax.broadcasted_iota(jnp.int32, (8, lanes), 0) % 2 == 1
        for at in range(0, rows, 8):
            value = prior_ref[at : at + 8, :]
            p_ref[0, at : at + 8, :] = jnp.where(odd, pltpu.roll(value, 1, 0), value)
            p_ref[1, at : at + 8, :] = jnp.where(odd, value, pltpu.roll(value, 7, 0))
        folded = []
        for which, ref in enumerate((dn_ref, rn_ref)):
            for real in range(reals):
                if real % size == 0:
                    copies[which][real // size].wait()
                total = None
                for comp in range(comps):
                    for slot in range(slots):
                        value = ref[real, comp, slot]
                        term = value * value
                        if which == 0:
                            term = p_ref[comp] * term
                        total = term if total is None else total + term
                folded.append(jnp.sum(total, axis=0, keepdims=True))
        folded.append(jnp.zeros((lanes - 2 * reals, lanes), F32))
        o_ref[...] = lane_sums(jnp.concatenate(folded, 0))

    return pl.pallas_call(
        kernel,
        compiler_params=limit(8),
        out_shape=(
            shape_near((comps, rows, lanes), F32),
            shape_near((1, lanes), F32),
        ),
        in_specs=[IN_PLACE, ON_CHIP, IN_PLACE, IN_PLACE],
        out_specs=(ON_CHIP,) * 2,
        scratch_shapes=[
            pltpu.VMEM(direction.shape, F32),
            pltpu.VMEM(direction.shape, F32),
            pltpu.SemaphoreType.DMA((2, parts)),
        ],
    )(far(after), prior, far(direction), far(residual))


def apply_gram(dots, grams, spread, copies, group):
    slots, lines, lanes = spread.shape
    bands = grams.shape[1]
    readers = slots // group
    sector = lanes // 4
    reals = 16

    def kernel(dots_ref, g_ref, x_ref, o_ref):
        product = None
        for band in range(bands):
            straight, turned = [], []
            for slot in range(slots):
                value = x_ref[slot, band * 8 : band * 8 + 8, :].astype(F32)
                straight.append(value)
                turned.append(pltpu.roll(value, lanes // 2, 1))
            for slot in range(slots):
                total = None
                for other in range(slots):
                    row = slot * slots + other
                    term = g_ref[0, band, row : row + 1, :] * straight[other]
                    term = term + g_ref[1, band, row : row + 1, :] * turned[other]
                    total = term if total is None else total + term
                total = total.astype(BF16)
                term = total.astype(F32) * straight[slot]
                product = term if product is None else product + term
                line = (slot % group) * lines + band * 8
                for copy in range(copies):
                    o_ref[copy * readers + slot // group, line : line + 8, :] = total
        product = product + pltpu.roll(product, lanes // 2, 1)
        halves = [product[:, :sector], product[:, sector : 2 * sector]]
        tall = jnp.concatenate(
            [
                jnp.concatenate([half, jnp.zeros((8, lanes - sector), F32)], 1)
                for half in halves
            ]
            + [jnp.zeros((lanes - 16, lanes), F32)],
            0,
        )
        shared = jnp.where(lax.axis_index("band") == 0, dots_ref[...], 0.0)
        value = lane_sums(tall) + shared
        top = value.astype(BF16).astype(F32)
        rest = value - top
        middle = rest.astype(BF16).astype(F32)
        last = (rest - middle).astype(BF16).astype(F32)
        row = top + pltpu.roll(middle, 2 * reals, 1) + pltpu.roll(last, 4 * reals, 1)
        tail = jnp.concatenate([row, jnp.zeros((7, lanes), F32)], 0).astype(BF16)
        for reader in range(copies * readers):
            o_ref[reader, group * lines : group * lines + 8, :] = tail

    return pl.pallas_call(
        kernel,
        compiler_params=limit(4),
        out_shape=shape_near((copies * readers, group * lines + 8, lanes), BF16),
        in_specs=[ON_CHIP] * 3,
        out_specs=ON_CHIP,
    )(near(dots), near(grams), near(spread))


def analyze(m_table, own, received, own_leg, got_leg, coefs, prior, direction, residual,
            bands, sectors, halves, copies, chunk):
    reals, comps, slots, rows, lanes = direction.shape
    groups = len(coefs)
    total_bands = groups * bands
    count, cycles = own_leg.shape
    sector = cycles // sectors
    high = reals // 8
    lines = halves * reals
    tiles = chunk // lanes
    block_rows = tiles * halves
    pitch = comps * block_rows + 8
    per_slot = bands * 8
    slab = sectors // 2
    tail = slots * per_slot
    pieces_count = 1

    def kernel(m_ref, own_ref, got_ref, own_leg_ref, got_leg_ref, *rest):
        coef_refs = rest[:groups]
        (prior_ref, d_ref, r_ref, new_ref, sums_ref, small_ref, back_ref, h_ref, h2_ref, s_ref,
         step_ref, leg_ref, dn_ref, rn_ref, arrived) = rest[groups:]
        index_comp = lax.axis_index("comp")
        index_band = lax.axis_index("band")
        places = (index_comp, 1 - index_comp)
        is_first = index_comp == 0
        sources = (own_leg_ref, got_leg_ref)
        copies_of = []
        for turn in range(slots):
            for piece in range(pieces_count):
                size = count // pieces_count
                span = pl.ds(piece * size, size)
                size = rows // pieces_count
                lines_span = pl.ds(piece * size, size)
                index = turn * pieces_count + piece
                copies_of.append(
                    [
                        pltpu.make_async_copy(
                            sources[turn].at[span], leg_ref.at[turn, span], arrived.at[index, 0]
                        )
                    ]
                    + [
                        pltpu.make_async_copy(
                            source.at[:, :, places[turn], lines_span],
                            target.at[turn, :, :, lines_span],
                            arrived.at[index, 1 + which],
                        )
                        for which, (source, target) in enumerate(
                            ((d_ref, dn_ref), (r_ref, rn_ref))
                        )
                    ]
                )
        for triple in copies_of:
            for copy in triple:
                copy.start()

        total = None
        for ref in (own_ref, got_ref):
            for at in range(groups * slab):
                value = ref[at, tail : tail + 8, :].astype(F32)
                total = value if total is None else total + value
        line = total[0:1, :]
        line = (
            line
            + pltpu.roll(line, lanes - 2 * reals, 1)
            + pltpu.roll(line, lanes - 4 * reals, 1)
        )
        norm_old = line[:, reals : 2 * reals]
        step_size = norm_old / line[:, :reals]
        small_ref[...] = jnp.concatenate(
            [step_size, norm_old, jnp.zeros((1, lanes - 2 * reals), F32)], 1
        )
        for real in range(reals):
            step_ref[real] = jnp.broadcast_to(step_size[:, real : real + 1], (8, lanes))

        for turn in range(slots):
            base = places[turn] * per_slot
            for group in range(groups):
                source = (index_band ^ group) * slab
                for band in range(bands):
                    start = pl.multiple_of(base + band * 8, 8)
                    for part in range(lines // 8):
                        span = slice(part * sector, (part + 1) * sector)
                        pieces = []
                        for z in range(slab):
                            mine = own_ref[source + z, pl.ds(start, 8), :].astype(F32)
                            theirs = got_ref[source + z, pl.ds(start, 8), :].astype(F32)
                            pieces.append(jnp.where(is_first, mine, theirs)[:, span])
                            pieces.append(jnp.where(is_first, theirs, mine)[:, span])
                        row = (group * bands + band) * lines + part * 8
                        back_ref[turn, row : row + 8, :] = jnp.concatenate(pieces, 1).astype(BF16)

        buffers = (h_ref, h2_ref)
        work = [(turn, at) for turn in range(slots) for at in range(0, count, chunk)]

        def multiply(index):
            turn, at = work[index]
            buffers[index % 2][...] = dot_nt(back_ref[turn], leg_ref[turn, at : at + chunk, :])

        for copy in copies_of[0]:
            copy.wait()
        lane = lax.broadcasted_iota(jnp.int32, (lines, lanes), 1)
        norms = [None] * reals
        multiply(0)
        for index, (turn, at) in enumerate(work):
            if index + 1 < len(work):
                if work[index + 1][0] != turn:
                    for copy in copies_of[turn + 1]:
                        copy.wait()
                multiply(index + 1)
            h = buffers[index % 2]
            least = m_ref[lax.axis_index("ma") * 2 + places[turn]]
            for tile in range(tiles):
                part = slice(tile * lanes, (tile + 1) * lanes)
                here = slice(at + tile * lanes, at + (tile + 1) * lanes)
                totals = [None] * comps
                for group in range(groups):
                    for band in range(bands):
                        row = (group * bands + band) * lines
                        value = h[row : row + lines, part]
                        for comp in range(comps):
                            term = coef_refs[group][band, comp : comp + 1, here] * value
                            totals[comp] = term if totals[comp] is None else totals[comp] + term
                keep = lane >= least - (at + tile * lanes)
                for comp in range(comps):
                    total = jnp.where(keep, totals[comp], 0.0)
                    for half in range(halves):
                        start = comp * block_rows + tile * halves + half
                        s_ref[index % 2, pl.ds(start, reals, stride=pitch), :] = total[
                            half * reals : (half + 1) * reals
                        ]
            first = at // lanes * halves
            for real in range(reals):
                for comp in range(comps):
                    for sub in range(0, block_rows, 8):
                        span = slice(first + sub, first + sub + 8)
                        line = real * pitch + comp * block_rows + sub
                        d = dn_ref[turn, real, comp, span, :]
                        r = rn_ref[turn, real, comp, span, :]
                        image = prior_ref[comp, span, :] * d + s_ref[index % 2, line : line + 8, :]
                        new = r - step_ref[real] * image
                        new_ref[real, comp, places[turn], span, :] = new
                        term = new * new
                        norms[real] = term if norms[real] is None else norms[real] + term
        folded = [jnp.sum(norm, axis=0, keepdims=True) for norm in norms]
        folded.append(jnp.zeros((lanes - reals, lanes), F32))
        norm = lane_sums(jnp.concatenate(folded, 0))
        for at in range(copies):
            sums_ref[at] = norm

    return pl.pallas_call(
        kernel,
        compiler_params=limit(24),
        out_shape=(
            shape_near(direction.shape, F32),
            shape_near((copies, 1, lanes), F32),
            shape_near((1, lanes), F32),
        ),
        in_specs=[SCALARS] + [ON_CHIP] * 2 + [IN_PLACE] * 2 + [ON_CHIP] * (1 + groups)
        + [IN_PLACE] * 2,
        out_specs=(ON_CHIP,) * 3,
        scratch_shapes=[
            pltpu.VMEM((slots, total_bands * lines, cycles), BF16),
            pltpu.VMEM((total_bands * lines, chunk), F32),
            pltpu.VMEM((total_bands * lines, chunk), F32),
            pltpu.VMEM((2, reals * pitch, lanes), F32),
            pltpu.VMEM((reals, 8, lanes), F32),
            pltpu.VMEM((slots, count, cycles), BF16),
            pltpu.VMEM((slots, reals, comps, rows, lanes), F32),
            pltpu.VMEM((slots, reals, comps, rows, lanes), F32),
            pltpu.SemaphoreType.DMA((slots * pieces_count, 3)),
        ],
    )(
        m_table, near(own), near(received), far(own_leg), far(got_leg),
        *(near(x) for x in (*coefs, prior)), far(direction), far(residual),
    )


def advance(small, solution, direction, new_residual):
    reals, comps, slots, rows, lanes = direction.shape
    parts = 4
    size = reals // parts

    def kernel(small_ref, x_ref, d_ref, r_ref, ox_ref, or_ref, x_buffer, d_buffer, o_buffer, sems):
        out = pltpu.make_async_copy(r_ref, or_ref, sems.at[3, 0])
        loads = [
            pltpu.make_async_copy(
                source.at[pl.ds(part * size, size)], target.at[pl.ds(part * size, size)],
                sems.at[which, part],
            )
            for part in range(parts)
            for which, (source, target) in enumerate(((x_ref, x_buffer), (d_ref, d_buffer)))
        ]
        stores = [
            pltpu.make_async_copy(
                o_buffer.at[pl.ds(part * size, size)], ox_ref.at[pl.ds(part * size, size)],
                sems.at[2, part],
            )
            for part in range(parts)
        ]
        for load in loads:
            load.start()
        out.start()
        for part in range(parts):
            loads[2 * part].wait()
            loads[2 * part + 1].wait()
            for real in range(part * size, (part + 1) * size):
                step = small_ref[0:1, real : real + 1]
                o_buffer[real] = x_buffer[real] + step[None, None] * d_buffer[real]
            stores[part].start()
        for store in stores:
            store.wait()
        out.wait()

    shape = jax.ShapeDtypeStruct(direction.shape, F32)
    return pl.pallas_call(
        kernel,
        compiler_params=limit(10),
        out_shape=(shape, shape),
        in_specs=[ON_CHIP, IN_PLACE, IN_PLACE, ON_CHIP],
        out_specs=(IN_PLACE, IN_PLACE),
        scratch_shapes=[pltpu.VMEM(direction.shape, F32)] * 3
        + [pltpu.SemaphoreType.DMA((4, parts))],
    )(near(small), far(solution), far(direction), near(new_residual))


def turn_direction(norms, small, direction, new_residual):
    reals, comps, slots, rows, lanes = direction.shape
    sources = norms.shape[0]
    parts = 8
    size = reals // parts

    def kernel(norms_ref, small_ref, d_ref, r_ref, o_ref, d_buffer, buffer, sems):
        loads = [
            pltpu.make_async_copy(
                d_ref.at[pl.ds(part * size, size)], d_buffer.at[pl.ds(part * size, size)],
                sems.at[0, part],
            )
            for part in range(parts)
        ]
        for load in loads:
            load.start()
        total = norms_ref[0]
        for at in range(1, sources):
            total = total + norms_ref[at]
        ratio = total[:, :reals] / small_ref[:, reals : 2 * reals]
        stores = [
            pltpu.make_async_copy(
                buffer.at[pl.ds(part * size, size)], o_ref.at[pl.ds(part * size, size)],
                sems.at[1, part],
            )
            for part in range(parts)
        ]
        for part in range(parts):
            loads[part].wait()
            for real in range(part * size, (part + 1) * size):
                one = ratio[:, real : real + 1]
                buffer[real] = r_ref[real] + one[None, None] * d_buffer[real]
            stores[part].start()
        for store in stores:
            store.wait()

    return pl.pallas_call(
        kernel,
        compiler_params=limit(8),
        out_shape=jax.ShapeDtypeStruct(direction.shape, F32),
        in_specs=[ON_CHIP, ON_CHIP, IN_PLACE, ON_CHIP],
        out_specs=IN_PLACE,
        scratch_shapes=[pltpu.VMEM(direction.shape, F32)] * 2
        + [pltpu.SemaphoreType.DMA((2, parts))],
    )(near(norms), near(small), far(direction), near(new_residual))


def phase_table(m_table, pixels):
    columns = jnp.arange(pixels, dtype=jnp.int32)
    wrapped = m_table[:, None] * columns[None, :] % pixels
    angles = wrapped.astype(jnp.float32) * (2.0 * math.pi / pixels)
    weights = jnp.where(m_table == 0, 1.0, 2.0).astype(jnp.float32)[:, None] / math.sqrt(pixels)
    return jnp.stack([weights * jnp.cos(angles), -weights * jnp.sin(angles)], axis=1).astype(
        jnp.bfloat16
    )


def swap_parts(parts, axis):
    count = lax.axis_size(axis)
    got = [parts[0]]
    for step in range(1, count):
        pairs = [(i, (i + step) % count) for i in range(count)]
        got.append(lax.ppermute(parts[step], axis, pairs))
    return got


def widen(values):
    return values[:, None, None, None, None]


def general(
    solution,
    residual,
    direction,
    prior_inv,
    mixing,
    beam,
    band_lmax,
    m_table,
    legendre,
    noise_weight,
    pixel_mask,
):
    band_count = lax.axis_size("band")
    slab_count = lax.axis_size("ma")
    comp_count = lax.axis_size("comp")
    comp_index = lax.axis_index("comp")
    slab_index = lax.axis_index("ma")
    reals, comps, slots, halves, degrees_count = direction.shape
    half_count = legendre.shape[0]
    bands = mixing.shape[0]
    cycles = legendre.shape[2]
    sector = noise_weight.shape[1]
    pixels = noise_weight.shape[2]
    sectors = slab_count * comp_count
    degrees = jnp.arange(degrees_count, dtype=jnp.int32)
    f32 = jnp.float32
    bf16 = jnp.bfloat16

    first_slot = (slab_index * comp_count + comp_index) * half_count
    local_m = lax.dynamic_slice_in_dim(m_table, first_slot, half_count)
    upper = degrees[None, :] <= band_lmax[:, None]
    cut_beam = beam * upper.astype(f32)
    lower = degrees[None, :] >= local_m[:, None]
    scale = cut_beam[:, None, :] * lower[None].astype(f32)

    low = jnp.transpose(direction, (2, 1, 3, 0, 4)).astype(bf16)
    low = low.reshape((comp_count, half_count) + low.shape[1:])
    relative = [
        lax.dynamic_index_in_dim(low, (comp_index + step) % comp_count, 0, keepdims=False)
        for step in range(comp_count)
    ]
    got = swap_parts(relative, "comp")
    mixed = None
    for step in range(comp_count):
        source = (comp_index - step) % comp_count
        columns = lax.dynamic_slice_in_dim(mixing, source * comps, comps, 1)
        for comp in range(comps):
            term = columns[:, comp][:, None, None, None, None] * got[step][None, :, comp].astype(f32)
            mixed = term if mixed is None else mixed + term
    coeffs = (scale[:, :, None, None, :] * mixed).astype(bf16)
    cycle_values = jnp.einsum(
        "bmqnl,mlr->bmqnr", coeffs, legendre, preferred_element_type=f32
    ).astype(bf16)
    send = cycle_values.reshape(bands, half_count, halves, reals, sectors, sector)
    send = jnp.transpose(send, (4, 1, 2, 3, 0, 5)).reshape(
        sectors, half_count * halves, reals, bands * sector
    )
    spread = lax.all_to_all(send, ("ma", "comp"), 0, 0, tiled=True)
    rows = sectors * half_count * halves
    spread = spread.reshape(rows, reals, bands * sector).astype(f32)

    table = phase_table(m_table, pixels).reshape(rows, pixels)
    weight = (noise_weight * pixel_mask.astype(f32)).reshape(bands * sector, pixels)
    if rows <= 2 * reals:
        pairs = (table.astype(f32)[:, None, :] * table.astype(f32)[None, :, :]).reshape(
            rows * rows, pixels
        )
        gram = lax.dot_general(
            pairs, weight, (((1,), (1,)), ((), ())), precision=lax.Precision.HIGH,
            preferred_element_type=f32,
        ).reshape(rows, rows, 1, bands * sector)
        back = (gram * spread[None]).sum(1).astype(bf16)
    else:
        sky = jnp.einsum("knx,kj->nxj", spread.astype(bf16), table, preferred_element_type=f32)
        weighted = (weight[None] * sky).astype(bf16)
        back = jnp.einsum("nxj,kj->knx", weighted, table, preferred_element_type=f32).astype(bf16)

    back = back.reshape(sectors, half_count * halves, reals, bands * sector)
    everyone = jnp.broadcast_to(back[None], (band_count,) + back.shape).reshape(
        (band_count * sectors,) + back.shape[1:]
    )
    gathered = lax.all_to_all(everyone, ("band", "ma", "comp"), 0, 0, tiled=True)
    gathered = gathered.reshape(
        band_count, sectors, half_count, halves, reals, bands, sector
    )
    total_bands = band_count * bands
    own_back = jnp.transpose(gathered, (2, 0, 5, 3, 4, 1, 6)).reshape(
        half_count, total_bands, halves, reals, cycles
    )
    all_back = swap_parts([own_back] * comp_count, "comp")
    all_legendre = swap_parts([legendre] * comp_count, "comp")

    packed = jnp.concatenate([cut_beam, jnp.pad(mixing, ((0, 0), (0, 128 - mixing.shape[1])))], 1)
    packed = lax.all_to_all(
        jnp.broadcast_to(packed[None], (band_count,) + packed.shape), "band", 0, 0, tiled=True
    ).reshape(total_bands, -1)
    all_beam = packed[:, :degrees_count]
    all_mixing = packed[:, degrees_count : degrees_count + mixing.shape[1]]
    own_mixing = lax.dynamic_slice_in_dim(all_mixing, comp_index * comps, comps, 1)
    coef = own_mixing[:, :, None] * all_beam[:, None, :]

    parts = []
    for step in range(comp_count):
        source = (comp_index - step) % comp_count
        slot_m = lax.dynamic_slice_in_dim(
            m_table, (slab_index * comp_count + source) * half_count, half_count
        )
        harmonic = jnp.einsum(
            "mbqnr,mlr->bmqnl", all_back[step], all_legendre[step], preferred_element_type=f32
        )
        total = jnp.zeros((comps, half_count, halves, reals, degrees_count), f32)
        for band in range(total_bands):
            total = total + coef[band][:, None, None, None, :] * harmonic[band][None]
        keep = degrees[None, :] >= slot_m[:, None]
        parts.append(jnp.where(keep[None, :, None, None, :], total, 0.0))
    ordered = [
        lax.dynamic_index_in_dim(
            jnp.stack(parts), (comp_index - position) % comp_count, 0, keepdims=False
        )
        for position in range(comp_count)
    ]
    returned = jnp.concatenate(ordered, axis=1)
    returned = jnp.transpose(returned, (3, 0, 1, 2, 4))
    image = prior_inv[None, :, None, None, :] * direction + returned
    axes = (1, 2, 3, 4)
    sums = jnp.stack(
        [
            jnp.sum(residual * residual, axis=axes),
            jnp.sum(direction * image, axis=axes),
            jnp.sum(residual * image, axis=axes),
            jnp.sum(image * image, axis=axes),
        ]
    )
    sums = lax.all_to_all(
        jnp.broadcast_to(sums[None], (sectors,) + sums.shape), ("ma", "comp"), 0, 0, tiled=True
    ).sum(0)
    norm_old, curvature_sum, cross_sum, image_norm = sums
    step_size = norm_old / curvature_sum
    new_solution = solution + widen(step_size) * direction
    new_residual = residual - widen(step_size) * image
    norm_new = norm_old - 2.0 * step_size * cross_sum + step_size * step_size * image_norm
    new_direction = new_residual + widen(norm_new / norm_old) * direction
    return (new_solution, new_residual, new_direction)


def phase_rows(m_table, pixels):
    columns = jnp.arange(pixels, dtype=jnp.int32)
    wrapped = m_table[:, None] * columns[None, :] % pixels
    angles = wrapped.astype(F32) * (2.0 * math.pi / pixels)
    weights = jnp.where(m_table == 0, 1.0, 2.0).astype(F32)[:, None] / math.sqrt(pixels)
    rows = jnp.stack([weights * jnp.cos(angles), -weights * jnp.sin(angles)], axis=0)
    return rows.astype(BF16).astype(F32)


def fast(
    solution,
    residual,
    direction,
    prior_inv,
    mixing,
    beam,
    band_lmax,
    m_table,
    legendre,
    noise_weight,
    pixel_mask,
):
    band_count = lax.axis_size("band")
    slab_count = lax.axis_size("ma")
    comp_count = lax.axis_size("comp")
    reals, comps, slots, halves, count = direction.shape
    bands, sector, pixels = noise_weight.shape
    sectors = slab_count * comp_count
    high = reals // 8
    exchange = [(0, 1), (1, 0)]
    legendre = legendre[0]
    flat_direction = flat_view(direction)
    flat_residual = flat_view(residual)
    flat_solution = flat_view(solution)

    (sent,) = narrow(flat_direction, False, halves)
    received = lax.ppermute(sent, "comp", exchange)
    own, own_coef = narrow(flat_direction, True, halves, mixing, band_lmax, beam)
    coefs = [own_coef] + [
        lax.ppermute(own_coef, "band", [(i, i ^ step) for i in range(band_count)])
        for step in range(1, band_count)
    ]
    packed = synthesize(
        mixing, band_lmax, m_table, beam, own, received, legendre, sectors, 1024
    )
    spread = lax.all_to_all(packed, ("ma", "comp"), 0, 0, tiled=True)
    other_legendre = lax.ppermute(legendre, "comp", exchange)

    late_table, unused = lax.optimization_barrier((m_table, packed))
    table = phase_rows(late_table, pixels)
    grams = gram(packed, table, noise_weight, pixel_mask, high, 1024)
    prior, dots = own_dots(packed, flat_view(prior_inv), flat_direction, flat_residual)
    back = apply_gram(dots, grams, spread, band_count, comp_count)
    arrived = lax.all_to_all(back, ("band", "ma"), 0, 0, tiled=True)
    other_arrived = lax.ppermute(arrived, "comp", exchange)
    new_residual, norms, small = analyze(
        m_table, arrived, other_arrived, legendre, other_legendre, coefs, prior,
        flat_direction, flat_residual, bands, sectors, halves, sectors, 512,
    )
    norms = lax.all_to_all(norms, ("ma", "comp"), 0, 0, tiled=True)
    new_solution, out_residual = advance(small, flat_solution, flat_direction, new_residual)
    norms, new_solution, out_residual = lax.optimization_barrier(
        (norms, new_solution, out_residual)
    )
    new_direction = turn_direction(norms, small, flat_direction, new_residual)
    return tuple(from_flat(out, halves) for out in (new_solution, out_residual, new_direction))


def body(*args):
    direction, legendre, noise_weight = args[2], args[8], args[9]
    reals, comps, slots, halves, count = direction.shape
    bands, sector, pixels = noise_weight.shape
    comp_count = lax.axis_size("comp")
    all_slots = lax.axis_size("ma") * comp_count * legendre.shape[0]
    fits = (
        comp_count == 2
        and slots == 2
        and legendre.shape[0] == 1
        and halves == 2
        and reals % 8 == 0
        and reals == 16
        and halves * (reals // 8) * sector == LANES
        and count % 1024 == 0
        and pixels % 1024 == 0
        and all_slots == 8
        and lax.axis_size("band") == 4
    )
    return fast(*args) if fits else general(*args)


def solution(mesh):
    in_specs = (
        P(None, "comp", "ma", None, None),
        P(None, "comp", "ma", None, None),
        P(None, "comp", "ma", None, None),
        P("comp", None),
        P("band", None),
        P("band", None),
        P("band"),
        P(),
        P(("ma", "comp"), None, None),
        P("band", ("ma", "comp"), None),
        P("band", ("ma", "comp"), None),
    )
    out_specs = (
        P(None, "comp", "ma", None, None),
        P(None, "comp", "ma", None, None),
        P(None, "comp", "ma", None, None),
    )
    return jax.shard_map(body, mesh=mesh, in_specs=in_specs, out_specs=out_specs, check_vma=False)
```

```python
import math

import jax
import jax.numpy as jnp
from jax import lax
from jax.experimental import pallas as pl
from jax.experimental.pallas import tpu as pltpu
from jax.sharding import PartitionSpec as P

LANES = 128
F32 = jnp.float32
BF16 = jnp.bfloat16
ON_CHIP = pl.BlockSpec(memory_space=pltpu.VMEM)
SCALARS = pl.BlockSpec(memory_space=pltpu.SMEM)
IN_PLACE = pl.BlockSpec(memory_space=pltpu.HBM)


def near(array):
    return pltpu.with_memory_space_constraint(array, pltpu.VMEM)


def far(array):
    return pltpu.with_memory_space_constraint(array, pltpu.HBM)


def limit(mebibytes):
    return pltpu.CompilerParams(vmem_limit_bytes=mebibytes * 1024 * 1024)


def shape_near(shape, kind):
    return pltpu.VMEM(shape, kind)


def flat_view(array):
    lead, halves, count = array.shape[:-2], array.shape[-2], array.shape[-1]
    tiles = count // LANES
    split = array.reshape(lead + (halves, tiles, LANES))
    return jnp.swapaxes(split, -3, -2).reshape(lead + (tiles * halves, LANES))


def from_flat(array, halves):
    lead, rows = array.shape[:-2], array.shape[-2]
    tiles = rows // halves
    split = jnp.swapaxes(array.reshape(lead + (tiles, halves, LANES)), -3, -2)
    return split.reshape(lead + (halves, tiles * LANES))


def dot_nt(left, right):
    return lax.dot_general(left, right, (((1,), (1,)), ((), ())), preferred_element_type=F32)


def dot_nn(left, right):
    return lax.dot_general(left, right, (((1,), (0,)), ((), ())), preferred_element_type=F32)


def split_bf16(value):
    top = value.astype(BF16)
    return top, (value - top.astype(F32)).astype(BF16)


def narrow(flat, own, halves):
    reals, comps, slots, rows, lanes = flat.shape
    tiles = rows // halves
    pitch = rows + 8

    def kernel(x_ref, o_ref, buffer, arrived):
        index = lax.axis_index("comp")
        slot = index if own else 1 - index
        copies = [
            pltpu.make_async_copy(
                x_ref.at[:, comp, slot],
                buffer.at[comp, :, pl.ds(0, rows), :],
                arrived.at[comp],
            )
            for comp in range(comps)
        ]
        for copy in copies:
            copy.start()
        lines = buffer.reshape(comps * reals * pitch, lanes)
        for comp in range(comps):
            copies[comp].wait()
            for tile in range(tiles):
                for half in range(halves):
                    start = comp * reals * pitch + tile * halves + half
                    picked = lines[pl.ds(start, reals, stride=pitch), :]
                    o_ref[
                        comp,
                        half * reals : (half + 1) * reals,
                        tile * lanes : (tile + 1) * lanes,
                    ] = picked.astype(BF16)

    return pl.pallas_call(
        kernel,
        compiler_params=limit(4),
        out_shape=shape_near((comps, halves * reals, tiles * lanes), BF16),
        in_specs=[IN_PLACE],
        out_specs=ON_CHIP,
        scratch_shapes=[
            pltpu.VMEM((comps, reals, pitch, lanes), F32),
            pltpu.SemaphoreType.DMA((comps,)),
        ],
    )(far(flat))


def coefficients(after, mixing, lmax, beam, comps):
    bands, count = beam.shape

    def kernel(mix_ref, lmax_ref, after_ref, beam_ref, o_ref):
        index = lax.axis_index("comp")
        degree = lax.broadcasted_iota(jnp.int32, (1, count), 1)
        for band in range(bands):
            cut = jnp.where(degree <= lmax_ref[band], beam_ref[band : band + 1, :], 0.0)
            o_ref[band] = jnp.concatenate(
                [mix_ref[band, index * comps + comp] * cut for comp in range(comps)], 0
            )

    return pl.pallas_call(
        kernel,
        compiler_params=limit(4),
        out_shape=shape_near((bands, comps, count), F32),
        in_specs=[SCALARS, SCALARS, IN_PLACE, ON_CHIP],
        out_specs=ON_CHIP,
    )(mixing, lmax, after, beam)


def synthesize(mixing, lmax, m_table, beam, own, received, legendre, sectors, chunk):
    comps, lines, count = own.shape
    bands = beam.shape[0]
    cycles = legendre.shape[1]
    sector = cycles // sectors
    parts = lines // 8

    def kernel(mix_ref, lmax_ref, m_ref, beam_ref, own_ref, got_ref, far_ref, o_ref, leg_ref, coef_ref, sem):
        index = lax.axis_index("comp")
        copy = pltpu.make_async_copy(far_ref, leg_ref, sem)
        copy.start()
        least = m_ref[lax.axis_index("ma") * 2 + index]
        width = 2 * comps * lines
        column = lax.broadcasted_iota(jnp.int32, (lines, width), 1)
        diagonal = column % lines == lax.broadcasted_iota(jnp.int32, (lines, width), 0)
        tops, lows = [], []
        for band in range(bands):
            weight = jnp.zeros((lines, width), F32)
            for turn, group in enumerate((index, 1 - index)):
                for comp in range(comps):
                    here = diagonal & (column // lines == turn * comps + comp)
                    weight = jnp.where(here, mix_ref[band, group * comps + comp], weight)
            top, low = split_bf16(weight)
            tops.append(top)
            lows.append(low)
        weights = jnp.concatenate([jnp.concatenate(tops, 0), jnp.concatenate(lows, 0)], 1)
        for at in range(0, count, chunk):
            span = slice(at, at + chunk)
            degree = at + lax.broadcasted_iota(jnp.int32, (1, chunk), 1)
            stacked = [
                ref[comp, :, span] for ref in (own_ref, got_ref) for comp in range(comps)
            ]
            mixed = dot_nn(weights, jnp.concatenate(stacked + stacked, 0))
            for band in range(bands):
                keep = (degree >= least) & (degree <= lmax_ref[band])
                scale = jnp.where(keep, beam_ref[band : band + 1, span], 0.0)
                coef_ref[band * lines : (band + 1) * lines, span] = (
                    scale * mixed[band * lines : (band + 1) * lines]
                ).astype(BF16)
        copy.wait()
        middle = count // 2
        acc = dot_nn(coef_ref[:, :middle], leg_ref[:middle, :]) + dot_nn(
            coef_ref[:, middle:], leg_ref[middle:, :]
        )
        for at in range(sectors):
            for band in range(bands):
                pieces = [
                    acc[
                        band * lines + part * 8 : band * lines + part * 8 + 8,
                        at * sector : (at + 1) * sector,
                    ]
                    for part in range(parts)
                ]
                o_ref[at, band * 8 : band * 8 + 8, :] = jnp.concatenate(pieces, 1).astype(BF16)

    return pl.pallas_call(
        kernel,
        compiler_params=limit(12),
        out_shape=shape_near((sectors, bands * 8, parts * sector), BF16),
        in_specs=[SCALARS] * 3 + [ON_CHIP] * 3 + [IN_PLACE],
        out_specs=ON_CHIP,
        scratch_shapes=[
            pltpu.VMEM((count, cycles), BF16),
            pltpu.VMEM((bands * lines, count), BF16),
            pltpu.SemaphoreType.DMA,
        ],
    )(mixing, lmax, m_table, beam, near(own), near(received), far(legendre))


def gram(after, table, noise_weight, pixel_mask, high, chunk):
    halves, slots, pixels = table.shape
    bands, sector, _ = noise_weight.shape
    lines = bands * sector
    rows = slots * slots
    pairs = ((0, 0), (0, 1), (1, 1))

    def kernel(after_ref, table_ref, noise_ref, mask_ref, o_ref, nn_ref, mn_ref, top_ref,
               weight_ref, sum_ref, sems):
        copies = [
            pltpu.make_async_copy(source, target, sems.at[which])
            for which, (source, target) in enumerate(((noise_ref, nn_ref), (mask_ref, mn_ref)))
        ]
        for copy in copies:
            copy.start()
        for at in range(0, pixels, chunk):
            span = slice(at, at + chunk)
            for which, (first, second) in enumerate(pairs):
                right = table_ref[second, :, span]
                for slot in range(0, slots, 2):
                    products = [
                        table_ref[first, at_slot : at_slot + 1, span] * right
                        for at_slot in (slot, slot + 1)
                    ]
                    row = which * rows + slot * slots
                    top_ref[row : row + 2 * slots, span] = jnp.concatenate(products, 0).astype(
                        BF16
                    )
        for copy in copies:
            copy.wait()
        for at in range(0, pixels, chunk):
            span = slice(at, at + chunk)
            weight = nn_ref[:, span] * mn_ref[:, span].astype(F32)
            top, low = split_bf16(weight)
            weight_ref[:lines, span] = top
            weight_ref[lines:, span] = low
        acc = dot_nt(top_ref[...], weight_ref[...])
        sum_ref[...] = acc[:, :lines] + acc[:, lines:]
        for band in range(bands):
            span = slice(band * sector, (band + 1) * sector)
            blocks = [sum_ref[at * rows : (at + 1) * rows, span] for at in range(len(pairs))]
            turned = jnp.concatenate(
                [
                    sum_ref[pl.ds(rows + slot, slots, stride=slots), :]
                    for slot in range(slots)
                ],
                0,
            )[:, span]
            o_ref[0, band] = jnp.concatenate([blocks[0]] * high + [blocks[2]] * high, 1)
            o_ref[1, band] = jnp.concatenate([blocks[1]] * high + [turned] * high, 1)

    return pl.pallas_call(
        kernel,
        compiler_params=limit(16),
        out_shape=shape_near((2, bands, rows, halves * high * sector), F32),
        in_specs=[IN_PLACE, ON_CHIP, IN_PLACE, IN_PLACE],
        out_specs=ON_CHIP,
        scratch_shapes=[
            pltpu.VMEM((lines, pixels), F32),
            pltpu.VMEM((lines, pixels), jnp.int32),
            pltpu.VMEM((len(pairs) * rows, pixels), BF16),
            pltpu.VMEM((2 * lines, pixels), BF16),
            pltpu.VMEM((len(pairs) * rows, lines), F32),
            pltpu.SemaphoreType.DMA((2,)),
        ],
    )(
        far(after),
        near(table),
        far(noise_weight.reshape(lines, pixels)),
        far(pixel_mask.reshape(lines, pixels)),
    )


def lane_sums(rows):
    return jnp.sum(rows.T, axis=0, keepdims=True)


def own_dots(after, prior, direction, residual):
    reals, comps, slots, rows, lanes = direction.shape
    parts = 4
    size = reals // parts

    def kernel(after_ref, prior_ref, d_ref, r_ref, p_ref, o_ref, dn_ref, rn_ref, arrived):
        copies = [
            [
                pltpu.make_async_copy(
                    source.at[pl.ds(part * size, size)],
                    target.at[pl.ds(part * size, size)],
                    arrived.at[which, part],
                )
                for part in range(parts)
            ]
            for which, (source, target) in enumerate(((d_ref, dn_ref), (r_ref, rn_ref)))
        ]
        for row in copies:
            for copy in row:
                copy.start()
        odd = lax.broadcasted_iota(jnp.int32, (8, lanes), 0) % 2 == 1
        for at in range(0, rows, 8):
            value = prior_ref[at : at + 8, :]
            p_ref[0, at : at + 8, :] = jnp.where(odd, pltpu.roll(value, 1, 0), value)
            p_ref[1, at : at + 8, :] = jnp.where(odd, value, pltpu.roll(value, 7, 0))
        folded = []
        for which, ref in enumerate((dn_ref, rn_ref)):
            for real in range(reals):
                if real % size == 0:
                    copies[which][real // size].wait()
                total = None
                for comp in range(comps):
                    for slot in range(slots):
                        value = ref[real, comp, slot]
                        term = value * value
                        if which == 0:
                            term = p_ref[comp] * term
                        total = term if total is None else total + term
                folded.append(jnp.sum(total, axis=0, keepdims=True))
        folded.append(jnp.zeros((lanes - 2 * reals, lanes), F32))
        o_ref[...] = lane_sums(jnp.concatenate(folded, 0))

    return pl.pallas_call(
        kernel,
        compiler_params=limit(8),
        out_shape=(
            shape_near((comps, rows, lanes), F32),
            shape_near((1, lanes), F32),
        ),
        in_specs=[IN_PLACE, ON_CHIP, IN_PLACE, IN_PLACE],
        out_specs=(ON_CHIP,) * 2,
        scratch_shapes=[
            pltpu.VMEM(direction.shape, F32),
            pltpu.VMEM(direction.shape, F32),
            pltpu.SemaphoreType.DMA((2, parts)),
        ],
    )(far(after), prior, far(direction), far(residual))


def apply_gram(dots, grams, spread, copies, group):
    slots, lines, lanes = spread.shape
    bands = grams.shape[1]
    readers = slots // group
    sector = lanes // 4
    reals = 16

    def kernel(dots_ref, g_ref, x_ref, o_ref):
        product = None
        for band in range(bands):
            straight, turned = [], []
            for slot in range(slots):
                value = x_ref[slot, band * 8 : band * 8 + 8, :].astype(F32)
                straight.append(value)
                turned.append(pltpu.roll(value, lanes // 2, 1))
            for slot in range(slots):
                total = None
                for other in range(slots):
                    row = slot * slots + other
                    term = g_ref[0, band, row : row + 1, :] * straight[other]
                    term = term + g_ref[1, band, row : row + 1, :] * turned[other]
                    total = term if total is None else total + term
                total = total.astype(BF16)
                term = total.astype(F32) * straight[slot]
                product = term if product is None else product + term
                line = (slot % group) * lines + band * 8
                for copy in range(copies):
                    o_ref[copy * readers + slot // group, line : line + 8, :] = total
        product = product + pltpu.roll(product, lanes // 2, 1)
        halves = [product[:, :sector], product[:, sector : 2 * sector]]
        tall = jnp.concatenate(
            [
                jnp.concatenate([half, jnp.zeros((8, lanes - sector), F32)], 1)
                for half in halves
            ]
            + [jnp.zeros((lanes - 16, lanes), F32)],
            0,
        )
        shared = jnp.where(lax.axis_index("band") == 0, dots_ref[...], 0.0)
        value = lane_sums(tall) + shared
        top = value.astype(BF16).astype(F32)
        rest = value - top
        middle = rest.astype(BF16).astype(F32)
        last = (rest - middle).astype(BF16).astype(F32)
        row = top + pltpu.roll(middle, 2 * reals, 1) + pltpu.roll(last, 4 * reals, 1)
        tail = jnp.concatenate([row, jnp.zeros((7, lanes), F32)], 0).astype(BF16)
        for reader in range(copies * readers):
            o_ref[reader, group * lines : group * lines + 8, :] = tail

    return pl.pallas_call(
        kernel,
        compiler_params=limit(4),
        out_shape=shape_near((copies * readers, group * lines + 8, lanes), BF16),
        in_specs=[ON_CHIP] * 3,
        out_specs=ON_CHIP,
    )(near(dots), near(grams), near(spread))


def analyze(m_table, own, received, own_leg, got_leg, coefs, prior, direction, residual,
            bands, sectors, halves, copies, chunk):
    reals, comps, slots, rows, lanes = direction.shape
    groups = len(coefs)
    total_bands = groups * bands
    count, cycles = own_leg.shape
    sector = cycles // sectors
    high = reals // 8
    lines = halves * reals
    tiles = chunk // lanes
    block_rows = tiles * halves
    pitch = comps * block_rows + 8
    per_slot = bands * 8
    slab = sectors // 2
    tail = slots * per_slot
    pieces_count = 1

    def kernel(m_ref, own_ref, got_ref, own_leg_ref, got_leg_ref, *rest):
        coef_refs = rest[:groups]
        (prior_ref, d_ref, r_ref, new_ref, out_ref, sums_ref, small_ref, back_ref, h_ref, h2_ref, s_ref,
         step_ref, leg_ref, dn_ref, rn_ref, arrived, left) = rest[groups:]
        index_comp = lax.axis_index("comp")
        index_band = lax.axis_index("band")
        places = (index_comp, 1 - index_comp)
        is_first = index_comp == 0
        sources = (own_leg_ref, got_leg_ref)
        copies_of = []
        for turn in range(slots):
            for piece in range(pieces_count):
                size = count // pieces_count
                span = pl.ds(piece * size, size)
                size = rows // pieces_count
                lines_span = pl.ds(piece * size, size)
                index = turn * pieces_count + piece
                copies_of.append(
                    [
                        pltpu.make_async_copy(
                            sources[turn].at[span], leg_ref.at[turn, span], arrived.at[index, 0]
                        )
                    ]
                    + [
                        pltpu.make_async_copy(
                            source.at[:, :, places[turn], lines_span],
                            target.at[turn, :, :, lines_span],
                            arrived.at[index, 1 + which],
                        )
                        for which, (source, target) in enumerate(
                            ((d_ref, dn_ref), (r_ref, rn_ref))
                        )
                    ]
                )
        for triple in copies_of:
            for copy in triple:
                copy.start()

        total = None
        for ref in (own_ref, got_ref):
            for at in range(groups * slab):
                value = ref[at, tail : tail + 8, :].astype(F32)
                total = value if total is None else total + value
        line = total[0:1, :]
        line = (
            line
            + pltpu.roll(line, lanes - 2 * reals, 1)
            + pltpu.roll(line, lanes - 4 * reals, 1)
        )
        norm_old = line[:, reals : 2 * reals]
        step_size = norm_old / line[:, :reals]
        small_ref[...] = jnp.concatenate(
            [step_size, norm_old, jnp.zeros((1, lanes - 2 * reals), F32)], 1
        )
        for real in range(reals):
            step_ref[real] = jnp.broadcast_to(step_size[:, real : real + 1], (8, lanes))

        for turn in range(slots):
            base = places[turn] * per_slot
            for group in range(groups):
                source = (index_band ^ group) * slab
                for band in range(bands):
                    start = pl.multiple_of(base + band * 8, 8)
                    for part in range(lines // 8):
                        span = slice(part * sector, (part + 1) * sector)
                        pieces = []
                        for z in range(slab):
                            mine = own_ref[source + z, pl.ds(start, 8), :].astype(F32)
                            theirs = got_ref[source + z, pl.ds(start, 8), :].astype(F32)
                            pieces.append(jnp.where(is_first, mine, theirs)[:, span])
                            pieces.append(jnp.where(is_first, theirs, mine)[:, span])
                        row = (group * bands + band) * lines + part * 8
                        back_ref[turn, row : row + 8, :] = jnp.concatenate(pieces, 1).astype(BF16)

        buffers = (h_ref, h2_ref)
        work = [(turn, at) for turn in range(slots) for at in range(0, count, chunk)]

        def multiply(index):
            turn, at = work[index]
            buffers[index % 2][...] = dot_nt(back_ref[turn], leg_ref[turn, at : at + chunk, :])

        for copy in copies_of[0]:
            copy.wait()
        lane = lax.broadcasted_iota(jnp.int32, (lines, lanes), 1)
        norms = [None] * reals
        leaving = []
        multiply(0)
        for index, (turn, at) in enumerate(work):
            if index + 1 < len(work):
                if work[index + 1][0] != turn:
                    for copy in copies_of[turn + 1]:
                        copy.wait()
                multiply(index + 1)
            h = buffers[index % 2]
            least = m_ref[lax.axis_index("ma") * 2 + places[turn]]
            for tile in range(tiles):
                part = slice(tile * lanes, (tile + 1) * lanes)
                here = slice(at + tile * lanes, at + (tile + 1) * lanes)
                totals = [None] * comps
                for group in range(groups):
                    for band in range(bands):
                        row = (group * bands + band) * lines
                        value = h[row : row + lines, part]
                        for comp in range(comps):
                            term = coef_refs[group][band, comp : comp + 1, here] * value
                            totals[comp] = term if totals[comp] is None else totals[comp] + term
                keep = lane >= least - (at + tile * lanes)
                for comp in range(comps):
                    total = jnp.where(keep, totals[comp], 0.0)
                    for half in range(halves):
                        start = comp * block_rows + tile * halves + half
                        s_ref[index % 2, pl.ds(start, reals, stride=pitch), :] = total[
                            half * reals : (half + 1) * reals
                        ]
            first = at // lanes * halves
            for real in range(reals):
                for comp in range(comps):
                    for sub in range(0, block_rows, 8):
                        span = slice(first + sub, first + sub + 8)
                        line = real * pitch + comp * block_rows + sub
                        d = dn_ref[turn, real, comp, span, :]
                        r = rn_ref[turn, real, comp, span, :]
                        image = prior_ref[comp, span, :] * d + s_ref[index % 2, line : line + 8, :]
                        new = r - step_ref[real] * image
                        new_ref[real, comp, places[turn], span, :] = new
                        term = new * new
                        norms[real] = term if norms[real] is None else norms[real] + term
            if (at + chunk) % (count // 2) == 0:
                piece = at // (count // 2)
                span = pl.ds(piece * rows // 2, rows // 2)
                leaving.append(
                    pltpu.make_async_copy(
                        new_ref.at[:, :, places[turn], span],
                        out_ref.at[:, :, places[turn], span],
                        left.at[turn, piece],
                    )
                )
                leaving[-1].start()
        folded = [jnp.sum(norm, axis=0, keepdims=True) for norm in norms]
        folded.append(jnp.zeros((lanes - reals, lanes), F32))
        norm = lane_sums(jnp.concatenate(folded, 0))
        for at in range(copies):
            sums_ref[at] = norm
        for copy in leaving:
            copy.wait()

    return pl.pallas_call(
        kernel,
        compiler_params=limit(24),
        out_shape=(
            shape_near(direction.shape, F32),
            jax.ShapeDtypeStruct(direction.shape, F32),
            shape_near((copies, 1, lanes), F32),
            shape_near((1, lanes), F32),
        ),
        in_specs=[SCALARS] + [ON_CHIP] * 2 + [IN_PLACE] * 2 + [ON_CHIP] * (1 + groups)
        + [IN_PLACE] * 2,
        out_specs=(ON_CHIP, IN_PLACE, ON_CHIP, ON_CHIP),
        scratch_shapes=[
            pltpu.VMEM((slots, total_bands * lines, cycles), BF16),
            pltpu.VMEM((total_bands * lines, chunk), F32),
            pltpu.VMEM((total_bands * lines, chunk), F32),
            pltpu.VMEM((2, reals * pitch, lanes), F32),
            pltpu.VMEM((reals, 8, lanes), F32),
            pltpu.VMEM((slots, count, cycles), BF16),
            pltpu.VMEM((slots, reals, comps, rows, lanes), F32),
            pltpu.VMEM((slots, reals, comps, rows, lanes), F32),
            pltpu.SemaphoreType.DMA((slots * pieces_count, 3)),
            pltpu.SemaphoreType.DMA((slots, 2)),
        ],
    )(
        m_table, near(own), near(received), far(own_leg), far(got_leg),
        *(near(x) for x in (*coefs, prior)), far(direction), far(residual),
    )


def advance(small, solution, direction, kept):
    reals, comps, slots, rows, lanes = direction.shape
    parts = 4
    size = reals // parts

    def kernel(small_ref, x_ref, d_ref, ox_ref, kept_ref, x_buffer, d_buffer, o_buffer, sems):
        loads = []
        for part in range(parts):
            span = pl.ds(part * size, size)
            low = part * size
            target = (
                kept_ref.at[span] if low < kept else d_buffer.at[pl.ds(low - kept, size)]
            )
            loads.append(
                (
                    pltpu.make_async_copy(x_ref.at[span], x_buffer.at[span], sems.at[0, part]),
                    pltpu.make_async_copy(d_ref.at[span], target, sems.at[1, part]),
                )
            )
        stores = [
            pltpu.make_async_copy(
                o_buffer.at[pl.ds(part * size, size)], ox_ref.at[pl.ds(part * size, size)],
                sems.at[2, part],
            )
            for part in range(parts)
        ]
        for pair in loads:
            for load in pair:
                load.start()
        for part in range(parts):
            for load in loads[part]:
                load.wait()
            for real in range(part * size, (part + 1) * size):
                step = small_ref[0:1, real : real + 1]
                d = kept_ref[real] if real < kept else d_buffer[real - kept]
                o_buffer[real] = x_buffer[real] + step[None, None] * d
            stores[part].start()
        for store in stores:
            store.wait()

    shape = direction.shape
    return pl.pallas_call(
        kernel,
        compiler_params=limit(10),
        out_shape=(
            jax.ShapeDtypeStruct(shape, F32),
            shape_near((kept,) + shape[1:], F32),
        ),
        in_specs=[ON_CHIP, IN_PLACE, IN_PLACE],
        out_specs=(IN_PLACE, ON_CHIP),
        scratch_shapes=[
            pltpu.VMEM(shape, F32),
            pltpu.VMEM((reals - kept,) + shape[1:], F32),
            pltpu.VMEM(shape, F32),
            pltpu.SemaphoreType.DMA((3, parts)),
        ],
    )(near(small), far(solution), far(direction))


def turn_direction(norms, small, kept, direction, new_residual):
    reals, comps, slots, rows, lanes = direction.shape
    sources = norms.shape[0]
    held = kept.shape[0]
    parts = 8
    size = reals // parts

    def kernel(norms_ref, small_ref, kept_ref, d_ref, r_ref, o_ref, d_buffer, buffer, sems):
        loads = {}
        for part in range(parts):
            low = part * size
            if low >= held:
                loads[part] = pltpu.make_async_copy(
                    d_ref.at[pl.ds(low, size)], d_buffer.at[pl.ds(low - held, size)],
                    sems.at[0, part],
                )
                loads[part].start()
        total = norms_ref[0]
        for at in range(1, sources):
            total = total + norms_ref[at]
        ratio = total[:, :reals] / small_ref[:, reals : 2 * reals]
        stores = [
            pltpu.make_async_copy(
                buffer.at[pl.ds(part * size, size)], o_ref.at[pl.ds(part * size, size)],
                sems.at[1, part],
            )
            for part in range(parts)
        ]
        for part in range(parts):
            if part in loads:
                loads[part].wait()
            for real in range(part * size, (part + 1) * size):
                one = ratio[:, real : real + 1]
                d = kept_ref[real] if real < held else d_buffer[real - held]
                buffer[real] = r_ref[real] + one[None, None] * d
            stores[part].start()
        for store in stores:
            store.wait()

    shape = direction.shape
    return pl.pallas_call(
        kernel,
        compiler_params=limit(8),
        out_shape=jax.ShapeDtypeStruct(shape, F32),
        in_specs=[ON_CHIP, ON_CHIP, ON_CHIP, IN_PLACE, ON_CHIP],
        out_specs=IN_PLACE,
        scratch_shapes=[
            pltpu.VMEM((reals - held,) + shape[1:], F32),
            pltpu.VMEM(shape, F32),
            pltpu.SemaphoreType.DMA((2, parts)),
        ],
    )(near(norms), near(small), near(kept), far(direction), near(new_residual))


def phase_table(m_table, pixels):
    columns = jnp.arange(pixels, dtype=jnp.int32)
    wrapped = m_table[:, None] * columns[None, :] % pixels
    angles = wrapped.astype(jnp.float32) * (2.0 * math.pi / pixels)
    weights = jnp.where(m_table == 0, 1.0, 2.0).astype(jnp.float32)[:, None] / math.sqrt(pixels)
    return jnp.stack([weights * jnp.cos(angles), -weights * jnp.sin(angles)], axis=1).astype(
        jnp.bfloat16
    )


def swap_parts(parts, axis):
    count = lax.axis_size(axis)
    got = [parts[0]]
    for step in range(1, count):
        pairs = [(i, (i + step) % count) for i in range(count)]
        got.append(lax.ppermute(parts[step], axis, pairs))
    return got


def widen(values):
    return values[:, None, None, None, None]


def general(
    solution,
    residual,
    direction,
    prior_inv,
    mixing,
    beam,
    band_lmax,
    m_table,
    legendre,
    noise_weight,
    pixel_mask,
):
    band_count = lax.axis_size("band")
    slab_count = lax.axis_size("ma")
    comp_count = lax.axis_size("comp")
    comp_index = lax.axis_index("comp")
    slab_index = lax.axis_index("ma")
    reals, comps, slots, halves, degrees_count = direction.shape
    half_count = legendre.shape[0]
    bands = mixing.shape[0]
    cycles = legendre.shape[2]
    sector = noise_weight.shape[1]
    pixels = noise_weight.shape[2]
    sectors = slab_count * comp_count
    degrees = jnp.arange(degrees_count, dtype=jnp.int32)
    f32 = jnp.float32
    bf16 = jnp.bfloat16

    first_slot = (slab_index * comp_count + comp_index) * half_count
    local_m = lax.dynamic_slice_in_dim(m_table, first_slot, half_count)
    upper = degrees[None, :] <= band_lmax[:, None]
    cut_beam = beam * upper.astype(f32)
    lower = degrees[None, :] >= local_m[:, None]
    scale = cut_beam[:, None, :] * lower[None].astype(f32)

    low = jnp.transpose(direction, (2, 1, 3, 0, 4)).astype(bf16)
    low = low.reshape((comp_count, half_count) + low.shape[1:])
    relative = [
        lax.dynamic_index_in_dim(low, (comp_index + step) % comp_count, 0, keepdims=False)
        for step in range(comp_count)
    ]
    got = swap_parts(relative, "comp")
    mixed = None
    for step in range(comp_count):
        source = (comp_index - step) % comp_count
        columns = lax.dynamic_slice_in_dim(mixing, source * comps, comps, 1)
        for comp in range(comps):
            term = columns[:, comp][:, None, None, None, None] * got[step][None, :, comp].astype(f32)
            mixed = term if mixed is None else mixed + term
    coeffs = (scale[:, :, None, None, :] * mixed).astype(bf16)
    cycle_values = jnp.einsum(
        "bmqnl,mlr->bmqnr", coeffs, legendre, preferred_element_type=f32
    ).astype(bf16)
    send = cycle_values.reshape(bands, half_count, halves, reals, sectors, sector)
    send = jnp.transpose(send, (4, 1, 2, 3, 0, 5)).reshape(
        sectors, half_count * halves, reals, bands * sector
    )
    spread = lax.all_to_all(send, ("ma", "comp"), 0, 0, tiled=True)
    rows = sectors * half_count * halves
    spread = spread.reshape(rows, reals, bands * sector).astype(f32)

    table = phase_table(m_table, pixels).reshape(rows, pixels)
    weight = (noise_weight * pixel_mask.astype(f32)).reshape(bands * sector, pixels)
    if rows <= 2 * reals:
        pairs = (table.astype(f32)[:, None, :] * table.astype(f32)[None, :, :]).reshape(
            rows * rows, pixels
        )
        gram = lax.dot_general(
            pairs, weight, (((1,), (1,)), ((), ())), precision=lax.Precision.HIGH,
            preferred_element_type=f32,
        ).reshape(rows, rows, 1, bands * sector)
        back = (gram * spread[None]).sum(1).astype(bf16)
    else:
        sky = jnp.einsum("knx,kj->nxj", spread.astype(bf16), table, preferred_element_type=f32)
        weighted = (weight[None] * sky).astype(bf16)
        back = jnp.einsum("nxj,kj->knx", weighted, table, preferred_element_type=f32).astype(bf16)

    back = back.reshape(sectors, half_count * halves, reals, bands * sector)
    everyone = jnp.broadcast_to(back[None], (band_count,) + back.shape).reshape(
        (band_count * sectors,) + back.shape[1:]
    )
    gathered = lax.all_to_all(everyone, ("band", "ma", "comp"), 0, 0, tiled=True)
    gathered = gathered.reshape(
        band_count, sectors, half_count, halves, reals, bands, sector
    )
    total_bands = band_count * bands
    own_back = jnp.transpose(gathered, (2, 0, 5, 3, 4, 1, 6)).reshape(
        half_count, total_bands, halves, reals, cycles
    )
    all_back = swap_parts([own_back] * comp_count, "comp")
    all_legendre = swap_parts([legendre] * comp_count, "comp")

    packed = jnp.concatenate([cut_beam, jnp.pad(mixing, ((0, 0), (0, 128 - mixing.shape[1])))], 1)
    packed = lax.all_to_all(
        jnp.broadcast_to(packed[None], (band_count,) + packed.shape), "band", 0, 0, tiled=True
    ).reshape(total_bands, -1)
    all_beam = packed[:, :degrees_count]
    all_mixing = packed[:, degrees_count : degrees_count + mixing.shape[1]]
    own_mixing = lax.dynamic_slice_in_dim(all_mixing, comp_index * comps, comps, 1)
    coef = own_mixing[:, :, None] * all_beam[:, None, :]

    parts = []
    for step in range(comp_count):
        source = (comp_index - step) % comp_count
        slot_m = lax.dynamic_slice_in_dim(
            m_table, (slab_index * comp_count + source) * half_count, half_count
        )
        harmonic = jnp.einsum(
            "mbqnr,mlr->bmqnl", all_back[step], all_legendre[step], preferred_element_type=f32
        )
        total = jnp.zeros((comps, half_count, halves, reals, degrees_count), f32)
        for band in range(total_bands):
            total = total + coef[band][:, None, None, None, :] * harmonic[band][None]
        keep = degrees[None, :] >= slot_m[:, None]
        parts.append(jnp.where(keep[None, :, None, None, :], total, 0.0))
    ordered = [
        lax.dynamic_index_in_dim(
            jnp.stack(parts), (comp_index - position) % comp_count, 0, keepdims=False
        )
        for position in range(comp_count)
    ]
    returned = jnp.concatenate(ordered, axis=1)
    returned = jnp.transpose(returned, (3, 0, 1, 2, 4))
    image = prior_inv[None, :, None, None, :] * direction + returned
    axes = (1, 2, 3, 4)
    sums = jnp.stack(
        [
            jnp.sum(residual * residual, axis=axes),
            jnp.sum(direction * image, axis=axes),
            jnp.sum(residual * image, axis=axes),
            jnp.sum(image * image, axis=axes),
        ]
    )
    sums = lax.all_to_all(
        jnp.broadcast_to(sums[None], (sectors,) + sums.shape), ("ma", "comp"), 0, 0, tiled=True
    ).sum(0)
    norm_old, curvature_sum, cross_sum, image_norm = sums
    step_size = norm_old / curvature_sum
    new_solution = solution + widen(step_size) * direction
    new_residual = residual - widen(step_size) * image
    norm_new = norm_old - 2.0 * step_size * cross_sum + step_size * step_size * image_norm
    new_direction = new_residual + widen(norm_new / norm_old) * direction
    return (new_solution, new_residual, new_direction)


def phase_rows(m_table, pixels):
    columns = jnp.arange(pixels, dtype=jnp.int32)
    wrapped = m_table[:, None] * columns[None, :] % pixels
    angles = wrapped.astype(F32) * (2.0 * math.pi / pixels)
    weights = jnp.where(m_table == 0, 1.0, 2.0).astype(F32)[:, None] / math.sqrt(pixels)
    rows = jnp.stack([weights * jnp.cos(angles), -weights * jnp.sin(angles)], axis=0)
    return rows.astype(BF16).astype(F32)


def fast(
    solution,
    residual,
    direction,
    prior_inv,
    mixing,
    beam,
    band_lmax,
    m_table,
    legendre,
    noise_weight,
    pixel_mask,
):
    band_count = lax.axis_size("band")
    slab_count = lax.axis_size("ma")
    comp_count = lax.axis_size("comp")
    reals, comps, slots, halves, count = direction.shape
    bands, sector, pixels = noise_weight.shape
    sectors = slab_count * comp_count
    high = reals // 8
    exchange = [(0, 1), (1, 0)]
    legendre = legendre[0]
    flat_direction = flat_view(direction)
    flat_residual = flat_view(residual)
    flat_solution = flat_view(solution)

    sent = narrow(flat_direction, False, halves)
    received = lax.ppermute(sent, "comp", exchange)
    own = narrow(flat_direction, True, halves)
    packed = synthesize(
        mixing, band_lmax, m_table, beam, own, received, legendre, sectors, 1024
    )
    spread = lax.all_to_all(packed, ("ma", "comp"), 0, 0, tiled=True)

    late_table, late_legendre, unused = lax.optimization_barrier((m_table, legendre, packed))
    other_legendre = lax.ppermute(late_legendre, "comp", exchange)
    table = phase_rows(late_table, pixels)
    grams = gram(packed, table, noise_weight, pixel_mask, high, 1024)
    prior, dots = own_dots(packed, flat_view(prior_inv), flat_direction, flat_residual)
    back = apply_gram(dots, grams, spread, band_count, comp_count)
    arrived = lax.all_to_all(back, ("band", "ma"), 0, 0, tiled=True)
    own_coef = coefficients(back, mixing, band_lmax, beam, comps)
    coefs = [own_coef] + [
        lax.ppermute(own_coef, "band", [(i, i ^ step) for i in range(band_count)])
        for step in range(1, band_count)
    ]
    arrived, coefs = lax.optimization_barrier((arrived, coefs))
    other_arrived = lax.ppermute(arrived, "comp", exchange)
    new_residual, out_residual, norms, small = analyze(
        m_table, arrived, other_arrived, legendre, other_legendre, coefs, prior,
        flat_direction, flat_residual, bands, sectors, halves, sectors, 512,
    )
    norms = lax.all_to_all(norms, ("ma", "comp"), 0, 0, tiled=True)
    new_solution, kept = advance(small, flat_solution, flat_direction, reals // 2)
    norms, new_solution, kept = lax.optimization_barrier((norms, new_solution, kept))
    new_direction = turn_direction(norms, small, kept, flat_direction, new_residual)
    return tuple(from_flat(out, halves) for out in (new_solution, out_residual, new_direction))


def body(*args):
    direction, legendre, noise_weight = args[2], args[8], args[9]
    reals, comps, slots, halves, count = direction.shape
    bands, sector, pixels = noise_weight.shape
    comp_count = lax.axis_size("comp")
    all_slots = lax.axis_size("ma") * comp_count * legendre.shape[0]
    fits = (
        comp_count == 2
        and slots == 2
        and legendre.shape[0] == 1
        and halves == 2
        and reals % 8 == 0
        and reals == 16
        and halves * (reals // 8) * sector == LANES
        and count % 1024 == 0
        and pixels % 1024 == 0
        and all_slots == 8
        and lax.axis_size("band") == 4
    )
    return fast(*args) if fits else general(*args)


def solution(mesh):
    in_specs = (
        P(None, "comp", "ma", None, None),
        P(None, "comp", "ma", None, None),
        P(None, "comp", "ma", None, None),
        P("comp", None),
        P("band", None),
        P("band", None),
        P("band"),
        P(),
        P(("ma", "comp"), None, None),
        P("band", ("ma", "comp"), None),
        P("band", ("ma", "comp"), None),
    )
    out_specs = (
        P(None, "comp", "ma", None, None),
        P(None, "comp", "ma", None, None),
        P(None, "comp", "ma", None, None),
    )
    return jax.shard_map(body, mesh=mesh, in_specs=in_specs, out_specs=out_specs, check_vma=False)
```

```python
import math

import jax
import jax.numpy as jnp
from jax import lax
from jax.experimental import pallas as pl
from jax.experimental.pallas import tpu as pltpu
from jax.sharding import PartitionSpec as P

LANES = 128
F32 = jnp.float32
BF16 = jnp.bfloat16
ON_CHIP = pl.BlockSpec(memory_space=pltpu.VMEM)
SCALARS = pl.BlockSpec(memory_space=pltpu.SMEM)
IN_PLACE = pl.BlockSpec(memory_space=pltpu.HBM)


def near(array):
    return pltpu.with_memory_space_constraint(array, pltpu.VMEM)


def far(array):
    return pltpu.with_memory_space_constraint(array, pltpu.HBM)


def limit(mebibytes):
    return pltpu.CompilerParams(vmem_limit_bytes=mebibytes * 1024 * 1024)


def shape_near(shape, kind):
    return pltpu.VMEM(shape, kind)


def flat_view(array):
    lead, halves, count = array.shape[:-2], array.shape[-2], array.shape[-1]
    tiles = count // LANES
    split = array.reshape(lead + (halves, tiles, LANES))
    return jnp.swapaxes(split, -3, -2).reshape(lead + (tiles * halves, LANES))


def from_flat(array, halves):
    lead, rows = array.shape[:-2], array.shape[-2]
    tiles = rows // halves
    split = jnp.swapaxes(array.reshape(lead + (tiles, halves, LANES)), -3, -2)
    return split.reshape(lead + (halves, tiles * LANES))


def dot_nt(left, right):
    return lax.dot_general(left, right, (((1,), (1,)), ((), ())), preferred_element_type=F32)


def dot_nn(left, right):
    return lax.dot_general(left, right, (((1,), (0,)), ((), ())), preferred_element_type=F32)


def split_bf16(value):
    top = value.astype(BF16)
    return top, (value - top.astype(F32)).astype(BF16)


def narrow(flat, own, halves, *extras):
    reals, comps, slots, rows, lanes = flat.shape
    tiles = rows // halves
    pitch = rows + 8
    extra = len(extras)

    def kernel(x_ref, *rest):
        o_ref = rest[extra]
        buffer, arrived = rest[-2:]
        index = lax.axis_index("comp")
        slot = index if own else 1 - index
        copies = [
            pltpu.make_async_copy(
                x_ref.at[:, comp, slot],
                buffer.at[comp, :, pl.ds(0, rows), :],
                arrived.at[comp],
            )
            for comp in range(comps)
        ]
        for copy in copies:
            copy.start()
        if extra:
            mix_ref, lmax_ref, m_ref, beam_ref, far_ref = rest[:extra]
            scale_ref, order_ref, leg_ref = rest[extra + 1 : extra + 4]
            copies.append(pltpu.make_async_copy(far_ref, leg_ref, arrived.at[comps]))
            copies[comps].start()
            bands, count = beam_ref.shape
            row = lax.broadcasted_iota(jnp.int32, (bands, 1), 0)
            most = jnp.zeros((bands, 1), jnp.int32)
            for band in range(bands):
                most = jnp.where(row == band, lmax_ref[band], most)
            degree = lax.broadcasted_iota(jnp.int32, (bands, count), 1)
            keep = (degree <= most) & (degree >= m_ref[lax.axis_index("ma") * 2 + index])
            scale_ref[...] = jnp.where(keep, beam_ref[...], 0.0)
            width = 2 * comps
            line = lax.broadcasted_iota(jnp.int32, (bands, width), 0)
            column = lax.broadcasted_iota(jnp.int32, (bands, width), 1)
            ordered = jnp.zeros((bands, width), F32)
            for band in range(bands):
                for turn, group in enumerate((index, 1 - index)):
                    for comp in range(comps):
                        here = (line == band) & (column == turn * comps + comp)
                        ordered = jnp.where(here, mix_ref[band, group * comps + comp], ordered)
            order_ref[...] = ordered
        lines = buffer.reshape(comps * reals * pitch, lanes)
        for comp in range(comps):
            copies[comp].wait()
            for tile in range(tiles):
                for half in range(halves):
                    start = comp * reals * pitch + tile * halves + half
                    picked = lines[pl.ds(start, reals, stride=pitch), :]
                    o_ref[
                        comp,
                        half * reals : (half + 1) * reals,
                        tile * lanes : (tile + 1) * lanes,
                    ] = picked.astype(BF16)
        if extra:
            copies[comps].wait()

    shapes = (shape_near((comps, halves * reals, tiles * lanes), BF16),)
    if extra:
        bands, count = extras[3].shape
        shapes += (shape_near((bands, count), F32), shape_near((bands, 2 * comps), F32))
        shapes += (shape_near(extras[4].shape, BF16),)
        extras = extras[:4] + (far(extras[4]),)
    return pl.pallas_call(
        kernel,
        compiler_params=limit(4),
        out_shape=shapes,
        in_specs=[IN_PLACE] + ([SCALARS] * 3 + [ON_CHIP, IN_PLACE] if extra else []),
        out_specs=(ON_CHIP,) * len(shapes),
        scratch_shapes=[
            pltpu.VMEM((comps, reals, pitch, lanes), F32),
            pltpu.SemaphoreType.DMA((comps + 1,)),
        ],
    )(far(flat), *extras)


def shared_rows(after, mixing, lmax, beam):
    bands, count = beam.shape
    columns = mixing.shape[1]

    def kernel(mix_ref, lmax_ref, after_ref, beam_ref, o_ref):
        row = lax.broadcasted_iota(jnp.int32, (bands, 1), 0)
        most = jnp.zeros((bands, 1), jnp.int32)
        for band in range(bands):
            most = jnp.where(row == band, lmax_ref[band], most)
        degree = lax.broadcasted_iota(jnp.int32, (bands, count), 1)
        o_ref[:bands, :] = jnp.where(degree <= most, beam_ref[...], 0.0)
        lane = lax.broadcasted_iota(jnp.int32, (1, count), 1)
        last = jnp.zeros((1, count), F32)
        for band in range(bands):
            for column in range(columns):
                last = jnp.where(lane == band * columns + column, mix_ref[band, column], last)
        o_ref[bands:, :] = last

    return pl.pallas_call(
        kernel,
        compiler_params=limit(4),
        out_shape=shape_near((bands + 1, count), F32),
        in_specs=[SCALARS, SCALARS, IN_PLACE, ON_CHIP],
        out_specs=ON_CHIP,
    )(mixing, lmax, far(after), beam)


def join(after, first, second):
    def kernel(after_ref, first_ref, second_ref, o_ref):
        o_ref[0] = first_ref[...]
        o_ref[1] = second_ref[...]

    return pl.pallas_call(
        kernel,
        compiler_params=limit(4),
        out_shape=shape_near((2,) + first.shape, F32),
        in_specs=[IN_PLACE, ON_CHIP, ON_CHIP],
        out_specs=ON_CHIP,
    )(far(after), near(first), near(second))


def pack_sectors(cycles_values, bands, sectors):
    rows, cycles = cycles_values.shape
    lines = rows // bands
    sector = cycles // sectors
    parts = lines // 8

    def kernel(x_ref, o_ref):
        for band in range(bands):
            values = [x_ref[band * lines + part * 8 : band * lines + part * 8 + 8, :] for part in range(parts)]
            for at in range(sectors):
                pieces = [value[:, at * sector : (at + 1) * sector] for value in values]
                o_ref[at, band * 8 : band * 8 + 8, :] = jnp.concatenate(pieces, 1).astype(BF16)

    return pl.pallas_call(
        kernel,
        compiler_params=limit(4),
        out_shape=shape_near((sectors, bands * 8, parts * sector), BF16),
        in_specs=[ON_CHIP],
        out_specs=ON_CHIP,
    )(near(cycles_values))


def gram(after, table, noise_weight, pixel_mask, high, chunk):
    halves, slots, pixels = table.shape
    bands, sector, _ = noise_weight.shape
    lines = bands * sector
    rows = slots * slots
    pairs = ((0, 0), (0, 1), (1, 1))

    def kernel(after_ref, table_ref, noise_ref, mask_ref, o_ref, nn_ref, mn_ref, top_ref,
               weight_ref, sum_ref, sems):
        copies = [
            pltpu.make_async_copy(source, target, sems.at[which])
            for which, (source, target) in enumerate(((noise_ref, nn_ref), (mask_ref, mn_ref)))
        ]
        for copy in copies:
            copy.start()
        for at in range(0, pixels, chunk):
            span = slice(at, at + chunk)
            for which, (first, second) in enumerate(pairs):
                right = table_ref[second, :, span]
                for slot in range(0, slots, 2):
                    products = [
                        table_ref[first, at_slot : at_slot + 1, span] * right
                        for at_slot in (slot, slot + 1)
                    ]
                    row = which * rows + slot * slots
                    top_ref[row : row + 2 * slots, span] = jnp.concatenate(products, 0).astype(
                        BF16
                    )
        for copy in copies:
            copy.wait()
        for at in range(0, pixels, chunk):
            span = slice(at, at + chunk)
            weight = nn_ref[:, span] * mn_ref[:, span].astype(F32)
            top, low = split_bf16(weight)
            weight_ref[:lines, span] = top
            weight_ref[lines:, span] = low
        acc = dot_nt(top_ref[...], weight_ref[...])
        sum_ref[...] = acc[:, :lines] + acc[:, lines:]
        for band in range(bands):
            span = slice(band * sector, (band + 1) * sector)
            blocks = [sum_ref[at * rows : (at + 1) * rows, span] for at in range(len(pairs))]
            turned = jnp.concatenate(
                [
                    sum_ref[pl.ds(rows + slot, slots, stride=slots), :]
                    for slot in range(slots)
                ],
                0,
            )[:, span]
            o_ref[0, band] = jnp.concatenate([blocks[0]] * high + [blocks[2]] * high, 1)
            o_ref[1, band] = jnp.concatenate([blocks[1]] * high + [turned] * high, 1)

    return pl.pallas_call(
        kernel,
        compiler_params=limit(16),
        out_shape=shape_near((2, bands, rows, halves * high * sector), F32),
        in_specs=[IN_PLACE, ON_CHIP, IN_PLACE, IN_PLACE],
        out_specs=ON_CHIP,
        scratch_shapes=[
            pltpu.VMEM((lines, pixels), F32),
            pltpu.VMEM((lines, pixels), jnp.int32),
            pltpu.VMEM((len(pairs) * rows, pixels), BF16),
            pltpu.VMEM((2 * lines, pixels), BF16),
            pltpu.VMEM((len(pairs) * rows, lines), F32),
            pltpu.SemaphoreType.DMA((2,)),
        ],
    )(
        far(after),
        near(table),
        far(noise_weight.reshape(lines, pixels)),
        far(pixel_mask.reshape(lines, pixels)),
    )


def lane_sums(rows):
    return jnp.sum(rows.T, axis=0, keepdims=True)


def spread_prior(flat_prior, halves):
    rows, lanes = flat_prior.shape

    def kernel(prior_ref, p_ref):
        odd = lax.broadcasted_iota(jnp.int32, (8, lanes), 0) % 2 == 1
        for at in range(0, rows, 8):
            value = prior_ref[at : at + 8, :]
            p_ref[0, at : at + 8, :] = jnp.where(odd, pltpu.roll(value, 1, 0), value)
            p_ref[1, at : at + 8, :] = jnp.where(odd, value, pltpu.roll(value, 7, 0))

    return pl.pallas_call(
        kernel,
        compiler_params=limit(4),
        out_shape=shape_near((2, rows, lanes), F32),
        in_specs=[ON_CHIP],
        out_specs=ON_CHIP,
    )(flat_prior)


def own_dots(after, prior, direction, residual, shares):
    reals, comps, slots, rows, lanes = direction.shape
    size = rows // shares

    def kernel(after_ref, prior_ref, d_ref, r_ref, o_ref, dn_ref, rn_ref, arrived):
        start = pl.multiple_of(lax.axis_index("band") * size, 8)
        copies = [
            pltpu.make_async_copy(source.at[:, :, :, pl.ds(start, size)], target, arrived.at[which])
            for which, (source, target) in enumerate(((d_ref, dn_ref), (r_ref, rn_ref)))
        ]
        for copy in copies:
            copy.start()
        odd = lax.broadcasted_iota(jnp.int32, (8, lanes), 0) % 2 == 1
        priors = [[], []]
        for at in range(0, size, 8):
            value = prior_ref[pl.ds(start + at, 8), :]
            priors[0].append(jnp.where(odd, pltpu.roll(value, 1, 0), value))
            priors[1].append(jnp.where(odd, value, pltpu.roll(value, 7, 0)))
        for copy in copies:
            copy.wait()
        folded = []
        for which, ref in enumerate((dn_ref, rn_ref)):
            for real in range(reals):
                total = None
                for comp in range(comps):
                    for slot in range(slots):
                        for at in range(0, size, 8):
                            value = ref[real, comp, slot, at : at + 8, :]
                            term = value * value
                            if which == 0:
                                term = priors[comp][at // 8] * term
                            total = term if total is None else total + term
                folded.append(jnp.sum(total, axis=0, keepdims=True))
        folded.append(jnp.zeros((lanes - 2 * reals, lanes), F32))
        o_ref[...] = lane_sums(jnp.concatenate(folded, 0))

    share = direction.shape[:3] + (size, lanes)
    return pl.pallas_call(
        kernel,
        compiler_params=limit(8),
        out_shape=shape_near((1, lanes), F32),
        in_specs=[IN_PLACE, ON_CHIP, IN_PLACE, IN_PLACE],
        out_specs=ON_CHIP,
        scratch_shapes=[
            pltpu.VMEM(share, F32),
            pltpu.VMEM(share, F32),
            pltpu.SemaphoreType.DMA((2,)),
        ],
    )(far(after), prior, far(direction), far(residual))


def apply_gram(dots, grams, spread, copies, group):
    slots, lines, lanes = spread.shape
    bands = grams.shape[1]
    readers = slots // group
    sector = lanes // 4
    reals = 16

    def kernel(dots_ref, g_ref, x_ref, o_ref):
        product = None
        for band in range(bands):
            straight, turned = [], []
            for slot in range(slots):
                value = x_ref[slot, band * 8 : band * 8 + 8, :].astype(F32)
                straight.append(value)
                turned.append(pltpu.roll(value, lanes // 2, 1))
            for slot in range(slots):
                total = None
                for other in range(slots):
                    row = slot * slots + other
                    term = g_ref[0, band, row : row + 1, :] * straight[other]
                    term = term + g_ref[1, band, row : row + 1, :] * turned[other]
                    total = term if total is None else total + term
                total = total.astype(BF16)
                term = total.astype(F32) * straight[slot]
                product = term if product is None else product + term
                line = (slot % group) * lines + band * 8
                for copy in range(copies):
                    o_ref[copy * readers + slot // group, line : line + 8, :] = total
        product = product + pltpu.roll(product, lanes // 2, 1)
        halves = [product[:, :sector], product[:, sector : 2 * sector]]
        tall = jnp.concatenate(
            [
                jnp.concatenate([half, jnp.zeros((8, lanes - sector), F32)], 1)
                for half in halves
            ]
            + [jnp.zeros((lanes - 16, lanes), F32)],
            0,
        )
        value = lane_sums(tall) + dots_ref[...]
        top = value.astype(BF16).astype(F32)
        rest = value - top
        middle = rest.astype(BF16).astype(F32)
        last = (rest - middle).astype(BF16).astype(F32)
        row = top + pltpu.roll(middle, 2 * reals, 1) + pltpu.roll(last, 4 * reals, 1)
        tail = jnp.concatenate([row, jnp.zeros((7, lanes), F32)], 0).astype(BF16)
        for reader in range(copies * readers):
            o_ref[reader, group * lines : group * lines + 8, :] = tail

    return pl.pallas_call(
        kernel,
        compiler_params=limit(4),
        out_shape=shape_near((copies * readers, group * lines + 8, lanes), BF16),
        in_specs=[ON_CHIP] * 3,
        out_specs=ON_CHIP,
    )(near(dots), near(grams), near(spread))


def analyze(m_table, own, received, own_leg, got_leg, shared, prior, direction, residual,
            bands, columns, sectors, halves, copies, chunk):
    reals, comps, slots, rows, lanes = direction.shape
    groups = 4
    total_bands = groups * bands
    count, cycles = own_leg.shape
    sector = cycles // sectors
    high = reals // 8
    lines = halves * reals
    tiles = chunk // lanes
    block_rows = tiles * halves
    pitch = comps * block_rows + 8
    per_slot = bands * 8
    slab = sectors // 2
    tail = slots * per_slot
    pieces_count = 1

    def kernel(m_ref, own_ref, got_ref, own_leg_ref, got_leg_ref, *rest):
        shared_refs = rest[:3]
        (prior_ref, d_ref, r_ref, new_ref, out_ref, sums_ref, small_ref, back_ref, h_ref, h2_ref, s_ref,
         step_ref, leg_ref, dn_ref, rn_ref, arrived, left, coef_ref) = rest[3:]
        index_comp = lax.axis_index("comp")
        index_band = lax.axis_index("band")
        places = (index_comp, 1 - index_comp)
        is_first = index_comp == 0
        sources = (own_leg_ref, got_leg_ref)
        copies_of = []
        for turn in range(slots):
            for piece in range(pieces_count):
                size = count // pieces_count
                span = pl.ds(piece * size, size)
                size = rows // pieces_count
                lines_span = pl.ds(piece * size, size)
                index = turn * pieces_count + piece
                copies_of.append(
                    [
                        pltpu.make_async_copy(
                            sources[turn].at[span], leg_ref.at[turn, span], arrived.at[index, 0]
                        )
                    ]
                    + [
                        pltpu.make_async_copy(
                            source.at[:, :, places[turn], lines_span],
                            target.at[turn, :, :, lines_span],
                            arrived.at[index, 1 + which],
                        )
                        for which, (source, target) in enumerate(
                            ((d_ref, dn_ref), (r_ref, rn_ref))
                        )
                    ]
                )
        for triple in copies_of:
            for copy in triple:
                copy.start()

        total = None
        for ref in (own_ref, got_ref):
            for at in range(groups * slab):
                value = ref[at, tail : tail + 8, :].astype(F32)
                total = value if total is None else total + value
        line = total[0:1, :]
        line = (
            line
            + pltpu.roll(line, lanes - 2 * reals, 1)
            + pltpu.roll(line, lanes - 4 * reals, 1)
        )
        norm_old = line[:, reals : 2 * reals]
        step_size = norm_old / line[:, :reals]
        small_ref[...] = jnp.concatenate(
            [step_size, norm_old, jnp.zeros((1, lanes - 2 * reals), F32)], 1
        )
        for real in range(reals):
            step_ref[real] = jnp.broadcast_to(step_size[:, real : real + 1], (8, lanes))

        blocks = (shared_refs[0], shared_refs[1], shared_refs[2].at[0], shared_refs[2].at[1])
        for group in range(groups):
            mix = blocks[group][bands : bands + 1, :lanes]
            for comp in range(comps):
                scales = [
                    jnp.where(
                        is_first,
                        mix[:, band * columns + comp : band * columns + comp + 1],
                        mix[:, band * columns + comps + comp : band * columns + comps + comp + 1],
                    )
                    for band in range(bands)
                ]
                scales.append(jnp.zeros((1, 1), F32))
                coef_ref[group, comp] = blocks[group][...] * jnp.concatenate(scales, 0)

        for turn in range(slots):
            base = places[turn] * per_slot
            for group in range(groups):
                source = (index_band ^ group) * slab
                for band in range(bands):
                    start = pl.multiple_of(base + band * 8, 8)
                    for part in range(lines // 8):
                        span = slice(part * sector, (part + 1) * sector)
                        pieces = []
                        for z in range(slab):
                            mine = own_ref[source + z, pl.ds(start, 8), :].astype(F32)
                            theirs = got_ref[source + z, pl.ds(start, 8), :].astype(F32)
                            pieces.append(jnp.where(is_first, mine, theirs)[:, span])
                            pieces.append(jnp.where(is_first, theirs, mine)[:, span])
                        row = (group * bands + band) * lines + part * 8
                        back_ref[turn, row : row + 8, :] = jnp.concatenate(pieces, 1).astype(BF16)

        buffers = (h_ref, h2_ref)
        work = [(turn, at) for turn in range(slots) for at in range(0, count, chunk)]

        def multiply(index):
            turn, at = work[index]
            buffers[index % 2][...] = dot_nt(back_ref[turn], leg_ref[turn, at : at + chunk, :])

        for copy in copies_of[0]:
            copy.wait()
        lane = lax.broadcasted_iota(jnp.int32, (lines, lanes), 1)
        norms = [None] * reals
        leaving = []
        multiply(0)
        for index, (turn, at) in enumerate(work):
            if index + 1 < len(work):
                if work[index + 1][0] != turn:
                    for copy in copies_of[turn + 1]:
                        copy.wait()
                multiply(index + 1)
            h = buffers[index % 2]
            least = m_ref[lax.axis_index("ma") * 2 + places[turn]]
            for tile in range(tiles):
                part = slice(tile * lanes, (tile + 1) * lanes)
                here = slice(at + tile * lanes, at + (tile + 1) * lanes)
                totals = [None] * comps
                for group in range(groups):
                    for band in range(bands):
                        row = (group * bands + band) * lines
                        value = h[row : row + lines, part]
                        for comp in range(comps):
                            term = coef_ref[group, comp, band : band + 1, here] * value
                            totals[comp] = term if totals[comp] is None else totals[comp] + term
                keep = lane >= least - (at + tile * lanes)
                for comp in range(comps):
                    total = jnp.where(keep, totals[comp], 0.0)
                    for half in range(halves):
                        start = comp * block_rows + tile * halves + half
                        s_ref[index % 2, pl.ds(start, reals, stride=pitch), :] = total[
                            half * reals : (half + 1) * reals
                        ]
            first = at // lanes * halves
            for real in range(reals):
                for comp in range(comps):
                    for sub in range(0, block_rows, 8):
                        span = slice(first + sub, first + sub + 8)
                        line = real * pitch + comp * block_rows + sub
                        d = dn_ref[turn, real, comp, span, :]
                        r = rn_ref[turn, real, comp, span, :]
                        image = prior_ref[comp, span, :] * d + s_ref[index % 2, line : line + 8, :]
                        new = r - step_ref[real] * image
                        new_ref[real, comp, places[turn], span, :] = new
                        term = new * new
                        norms[real] = term if norms[real] is None else norms[real] + term
            if (at + chunk) % (count // 2) == 0:
                piece = at // (count // 2)
                span = pl.ds(piece * rows // 2, rows // 2)
                leaving.append(
                    pltpu.make_async_copy(
                        new_ref.at[:, :, places[turn], span],
                        out_ref.at[:, :, places[turn], span],
                        left.at[turn, piece],
                    )
                )
                leaving[-1].start()
        folded = [jnp.sum(norm, axis=0, keepdims=True) for norm in norms]
        folded.append(jnp.zeros((lanes - reals, lanes), F32))
        norm = lane_sums(jnp.concatenate(folded, 0))
        for at in range(copies):
            sums_ref[at] = norm
        for copy in leaving:
            copy.wait()

    return pl.pallas_call(
        kernel,
        compiler_params=limit(24),
        out_shape=(
            shape_near(direction.shape, F32),
            jax.ShapeDtypeStruct(direction.shape, F32),
            shape_near((copies, 1, lanes), F32),
            shape_near((1, lanes), F32),
        ),
        in_specs=[SCALARS] + [ON_CHIP] * 2 + [IN_PLACE] * 2 + [ON_CHIP] * 4
        + [IN_PLACE] * 2,
        out_specs=(ON_CHIP, IN_PLACE, ON_CHIP, ON_CHIP),
        scratch_shapes=[
            pltpu.VMEM((slots, total_bands * lines, cycles), BF16),
            pltpu.VMEM((total_bands * lines, chunk), F32),
            pltpu.VMEM((total_bands * lines, chunk), F32),
            pltpu.VMEM((2, reals * pitch, lanes), F32),
            pltpu.VMEM((reals, 8, lanes), F32),
            pltpu.VMEM((slots, count, cycles), BF16),
            pltpu.VMEM((slots, reals, comps, rows, lanes), F32),
            pltpu.VMEM((slots, reals, comps, rows, lanes), F32),
            pltpu.SemaphoreType.DMA((slots * pieces_count, 3)),
            pltpu.SemaphoreType.DMA((slots, 2)),
            pltpu.VMEM((groups, comps, bands + 1, count), F32),
        ],
    )(
        m_table, near(own), near(received), far(own_leg), far(got_leg),
        *(near(x) for x in (*shared, prior)), far(direction), far(residual),
    )


def advance(small, solution, direction, kept):
    reals, comps, slots, rows, lanes = direction.shape
    parts = 4
    size = reals // parts

    def kernel(small_ref, x_ref, d_ref, ox_ref, kept_ref, x_buffer, d_buffer, o_buffer, sems):
        loads = []
        for part in range(parts):
            span = pl.ds(part * size, size)
            low = part * size
            target = (
                kept_ref.at[span] if low < kept else d_buffer.at[pl.ds(low - kept, size)]
            )
            loads.append(
                (
                    pltpu.make_async_copy(x_ref.at[span], x_buffer.at[span], sems.at[0, part]),
                    pltpu.make_async_copy(d_ref.at[span], target, sems.at[1, part]),
                )
            )
        stores = [
            pltpu.make_async_copy(
                o_buffer.at[pl.ds(part * size, size)], ox_ref.at[pl.ds(part * size, size)],
                sems.at[2, part],
            )
            for part in range(parts)
        ]
        for pair in loads:
            for load in pair:
                load.start()
        for part in range(parts):
            for load in loads[part]:
                load.wait()
            for real in range(part * size, (part + 1) * size):
                step = small_ref[0:1, real : real + 1]
                d = kept_ref[real] if real < kept else d_buffer[real - kept]
                o_buffer[real] = x_buffer[real] + step[None, None] * d
            stores[part].start()
        for store in stores:
            store.wait()

    shape = direction.shape
    return pl.pallas_call(
        kernel,
        compiler_params=limit(10),
        out_shape=(
            jax.ShapeDtypeStruct(shape, F32),
            shape_near((kept,) + shape[1:], F32),
        ),
        in_specs=[ON_CHIP, IN_PLACE, IN_PLACE],
        out_specs=(IN_PLACE, ON_CHIP),
        scratch_shapes=[
            pltpu.VMEM(shape, F32),
            pltpu.VMEM((reals - kept,) + shape[1:], F32),
            pltpu.VMEM(shape, F32),
            pltpu.SemaphoreType.DMA((3, parts)),
        ],
    )(near(small), far(solution), far(direction))


def turn_direction(norms, small, kept, direction, new_residual):
    reals, comps, slots, rows, lanes = direction.shape
    sources = norms.shape[0]
    held = kept.shape[0]
    parts = 8
    size = reals // parts

    def kernel(norms_ref, small_ref, kept_ref, d_ref, r_ref, o_ref, d_buffer, buffer, sems):
        loads = {}
        for part in range(parts):
            low = part * size
            if low >= held:
                loads[part] = pltpu.make_async_copy(
                    d_ref.at[pl.ds(low, size)], d_buffer.at[pl.ds(low - held, size)],
                    sems.at[0, part],
                )
                loads[part].start()
        total = norms_ref[0]
        for at in range(1, sources):
            total = total + norms_ref[at]
        ratio = total[:, :reals] / small_ref[:, reals : 2 * reals]
        stores = [
            pltpu.make_async_copy(
                buffer.at[pl.ds(part * size, size)], o_ref.at[pl.ds(part * size, size)],
                sems.at[1, part],
            )
            for part in range(parts)
        ]
        for part in range(parts):
            if part in loads:
                loads[part].wait()
            for real in range(part * size, (part + 1) * size):
                one = ratio[:, real : real + 1]
                d = kept_ref[real] if real < held else d_buffer[real - held]
                buffer[real] = r_ref[real] + one[None, None] * d
            stores[part].start()
        for store in stores:
            store.wait()

    shape = direction.shape
    return pl.pallas_call(
        kernel,
        compiler_params=limit(8),
        out_shape=jax.ShapeDtypeStruct(shape, F32),
        in_specs=[ON_CHIP, ON_CHIP, ON_CHIP, IN_PLACE, ON_CHIP],
        out_specs=IN_PLACE,
        scratch_shapes=[
            pltpu.VMEM((reals - held,) + shape[1:], F32),
            pltpu.VMEM(shape, F32),
            pltpu.SemaphoreType.DMA((2, parts)),
        ],
    )(near(norms), near(small), near(kept), far(direction), near(new_residual))


def phase_table(m_table, pixels):
    columns = jnp.arange(pixels, dtype=jnp.int32)
    wrapped = m_table[:, None] * columns[None, :] % pixels
    angles = wrapped.astype(jnp.float32) * (2.0 * math.pi / pixels)
    weights = jnp.where(m_table == 0, 1.0, 2.0).astype(jnp.float32)[:, None] / math.sqrt(pixels)
    return jnp.stack([weights * jnp.cos(angles), -weights * jnp.sin(angles)], axis=1).astype(
        jnp.bfloat16
    )


def swap_parts(parts, axis):
    count = lax.axis_size(axis)
    got = [parts[0]]
    for step in range(1, count):
        pairs = [(i, (i + step) % count) for i in range(count)]
        got.append(lax.ppermute(parts[step], axis, pairs))
    return got


def widen(values):
    return values[:, None, None, None, None]


def general(
    solution,
    residual,
    direction,
    prior_inv,
    mixing,
    beam,
    band_lmax,
    m_table,
    legendre,
    noise_weight,
    pixel_mask,
):
    band_count = lax.axis_size("band")
    slab_count = lax.axis_size("ma")
    comp_count = lax.axis_size("comp")
    comp_index = lax.axis_index("comp")
    slab_index = lax.axis_index("ma")
    reals, comps, slots, halves, degrees_count = direction.shape
    half_count = legendre.shape[0]
    bands = mixing.shape[0]
    cycles = legendre.shape[2]
    sector = noise_weight.shape[1]
    pixels = noise_weight.shape[2]
    sectors = slab_count * comp_count
    degrees = jnp.arange(degrees_count, dtype=jnp.int32)
    f32 = jnp.float32
    bf16 = jnp.bfloat16

    first_slot = (slab_index * comp_count + comp_index) * half_count
    local_m = lax.dynamic_slice_in_dim(m_table, first_slot, half_count)
    upper = degrees[None, :] <= band_lmax[:, None]
    cut_beam = beam * upper.astype(f32)
    lower = degrees[None, :] >= local_m[:, None]
    scale = cut_beam[:, None, :] * lower[None].astype(f32)

    low = jnp.transpose(direction, (2, 1, 3, 0, 4)).astype(bf16)
    low = low.reshape((comp_count, half_count) + low.shape[1:])
    relative = [
        lax.dynamic_index_in_dim(low, (comp_index + step) % comp_count, 0, keepdims=False)
        for step in range(comp_count)
    ]
    got = swap_parts(relative, "comp")
    mixed = None
    for step in range(comp_count):
        source = (comp_index - step) % comp_count
        columns = lax.dynamic_slice_in_dim(mixing, source * comps, comps, 1)
        for comp in range(comps):
            term = columns[:, comp][:, None, None, None, None] * got[step][None, :, comp].astype(f32)
            mixed = term if mixed is None else mixed + term
    coeffs = (scale[:, :, None, None, :] * mixed).astype(bf16)
    cycle_values = jnp.einsum(
        "bmqnl,mlr->bmqnr", coeffs, legendre, preferred_element_type=f32
    ).astype(bf16)
    send = cycle_values.reshape(bands, half_count, halves, reals, sectors, sector)
    send = jnp.transpose(send, (4, 1, 2, 3, 0, 5)).reshape(
        sectors, half_count * halves, reals, bands * sector
    )
    spread = lax.all_to_all(send, ("ma", "comp"), 0, 0, tiled=True)
    rows = sectors * half_count * halves
    spread = spread.reshape(rows, reals, bands * sector).astype(f32)

    table = phase_table(m_table, pixels).reshape(rows, pixels)
    weight = (noise_weight * pixel_mask.astype(f32)).reshape(bands * sector, pixels)
    if rows <= 2 * reals:
        pairs = (table.astype(f32)[:, None, :] * table.astype(f32)[None, :, :]).reshape(
            rows * rows, pixels
        )
        gram = lax.dot_general(
            pairs, weight, (((1,), (1,)), ((), ())), precision=lax.Precision.HIGH,
            preferred_element_type=f32,
        ).reshape(rows, rows, 1, bands * sector)
        back = (gram * spread[None]).sum(1).astype(bf16)
    else:
        sky = jnp.einsum("knx,kj->nxj", spread.astype(bf16), table, preferred_element_type=f32)
        weighted = (weight[None] * sky).astype(bf16)
        back = jnp.einsum("nxj,kj->knx", weighted, table, preferred_element_type=f32).astype(bf16)

    back = back.reshape(sectors, half_count * halves, reals, bands * sector)
    everyone = jnp.broadcast_to(back[None], (band_count,) + back.shape).reshape(
        (band_count * sectors,) + back.shape[1:]
    )
    gathered = lax.all_to_all(everyone, ("band", "ma", "comp"), 0, 0, tiled=True)
    gathered = gathered.reshape(
        band_count, sectors, half_count, halves, reals, bands, sector
    )
    total_bands = band_count * bands
    own_back = jnp.transpose(gathered, (2, 0, 5, 3, 4, 1, 6)).reshape(
        half_count, total_bands, halves, reals, cycles
    )
    all_back = swap_parts([own_back] * comp_count, "comp")
    all_legendre = swap_parts([legendre] * comp_count, "comp")

    packed = jnp.concatenate([cut_beam, jnp.pad(mixing, ((0, 0), (0, 128 - mixing.shape[1])))], 1)
    packed = lax.all_to_all(
        jnp.broadcast_to(packed[None], (band_count,) + packed.shape), "band", 0, 0, tiled=True
    ).reshape(total_bands, -1)
    all_beam = packed[:, :degrees_count]
    all_mixing = packed[:, degrees_count : degrees_count + mixing.shape[1]]
    own_mixing = lax.dynamic_slice_in_dim(all_mixing, comp_index * comps, comps, 1)
    coef = own_mixing[:, :, None] * all_beam[:, None, :]

    parts = []
    for step in range(comp_count):
        source = (comp_index - step) % comp_count
        slot_m = lax.dynamic_slice_in_dim(
            m_table, (slab_index * comp_count + source) * half_count, half_count
        )
        harmonic = jnp.einsum(
            "mbqnr,mlr->bmqnl", all_back[step], all_legendre[step], preferred_element_type=f32
        )
        total = jnp.zeros((comps, half_count, halves, reals, degrees_count), f32)
        for band in range(total_bands):
            total = total + coef[band][:, None, None, None, :] * harmonic[band][None]
        keep = degrees[None, :] >= slot_m[:, None]
        parts.append(jnp.where(keep[None, :, None, None, :], total, 0.0))
    ordered = [
        lax.dynamic_index_in_dim(
            jnp.stack(parts), (comp_index - position) % comp_count, 0, keepdims=False
        )
        for position in range(comp_count)
    ]
    returned = jnp.concatenate(ordered, axis=1)
    returned = jnp.transpose(returned, (3, 0, 1, 2, 4))
    image = prior_inv[None, :, None, None, :] * direction + returned
    axes = (1, 2, 3, 4)
    sums = jnp.stack(
        [
            jnp.sum(residual * residual, axis=axes),
            jnp.sum(direction * image, axis=axes),
            jnp.sum(residual * image, axis=axes),
            jnp.sum(image * image, axis=axes),
        ]
    )
    sums = lax.all_to_all(
        jnp.broadcast_to(sums[None], (sectors,) + sums.shape), ("ma", "comp"), 0, 0, tiled=True
    ).sum(0)
    norm_old, curvature_sum, cross_sum, image_norm = sums
    step_size = norm_old / curvature_sum
    new_solution = solution + widen(step_size) * direction
    new_residual = residual - widen(step_size) * image
    norm_new = norm_old - 2.0 * step_size * cross_sum + step_size * step_size * image_norm
    new_direction = new_residual + widen(norm_new / norm_old) * direction
    return (new_solution, new_residual, new_direction)


def phase_rows(m_table, pixels):
    columns = jnp.arange(pixels, dtype=jnp.int32)
    wrapped = m_table[:, None] * columns[None, :] % pixels
    angles = wrapped.astype(F32) * (2.0 * math.pi / pixels)
    weights = jnp.where(m_table == 0, 1.0, 2.0).astype(F32)[:, None] / math.sqrt(pixels)
    rows = jnp.stack([weights * jnp.cos(angles), -weights * jnp.sin(angles)], axis=0)
    return rows.astype(BF16).astype(F32)


def fast(
    solution,
    residual,
    direction,
    prior_inv,
    mixing,
    beam,
    band_lmax,
    m_table,
    legendre,
    noise_weight,
    pixel_mask,
):
    band_count = lax.axis_size("band")
    slab_count = lax.axis_size("ma")
    comp_count = lax.axis_size("comp")
    reals, comps, slots, halves, count = direction.shape
    bands, sector, pixels = noise_weight.shape
    sectors = slab_count * comp_count
    high = reals // 8
    exchange = [(0, 1), (1, 0)]
    legendre = legendre[0]
    flat_direction = flat_view(direction)
    flat_residual = flat_view(residual)
    flat_solution = flat_view(solution)

    (sent,) = narrow(flat_direction, False, halves)
    received = lax.ppermute(sent, "comp", exchange)
    own, scale, ordered, near_legendre = narrow(
        flat_direction, True, halves, mixing, band_lmax, m_table, beam, legendre
    )
    lines = halves * reals
    mixed = None
    for turn, group in enumerate((own, received)):
        for comp in range(comps):
            column = ordered[:, turn * comps + comp][:, None, None]
            term = column * group[comp][None].astype(F32)
            mixed = term if mixed is None else mixed + term
    coeffs = (scale[:, None, :] * mixed).astype(BF16)
    cycle_values = jnp.einsum("bkl,lr->bkr", coeffs, near_legendre, preferred_element_type=F32)
    packed = pack_sectors(cycle_values.reshape(bands * lines, -1), bands, sectors)
    spread = lax.all_to_all(packed, ("ma", "comp"), 0, 0, tiled=True)

    late_table, late_legendre, unused = lax.optimization_barrier((m_table, legendre, packed))
    other_legendre = lax.ppermute(late_legendre, "comp", exchange)
    table = phase_rows(late_table, pixels)
    grams = gram(packed, table, noise_weight, pixel_mask, high, 1024)
    flat_prior = flat_view(prior_inv)
    dots = own_dots(packed, flat_prior, flat_direction, flat_residual, band_count)
    near_pair = [(i, i ^ 1) for i in range(band_count)]
    far_pair = [(i, i ^ 2) for i in range(band_count)]
    own_rows = shared_rows(packed, mixing, band_lmax, beam)
    next_rows = lax.ppermute(own_rows, "band", near_pair)
    spread, next_rows = lax.optimization_barrier((spread, next_rows))
    back = apply_gram(dots, grams, spread, band_count, comp_count)
    arrived = lax.all_to_all(back, ("band", "ma"), 0, 0, tiled=True)
    last_rows = lax.ppermute(join(back, own_rows, next_rows), "band", far_pair)
    late_prior, unused = lax.optimization_barrier((flat_prior, back))
    prior = spread_prior(late_prior, halves)
    arrived, last_rows, prior = lax.optimization_barrier((arrived, last_rows, prior))
    other_arrived = lax.ppermute(arrived, "comp", exchange)
    new_residual, out_residual, norms, small = analyze(
        m_table, arrived, other_arrived, legendre, other_legendre, (own_rows, next_rows, last_rows), prior,
        flat_direction, flat_residual, bands, comp_count * comps, sectors, halves, sectors, 512,
    )
    norms = lax.all_to_all(norms, ("ma", "comp"), 0, 0, tiled=True)
    new_solution, kept = advance(small, flat_solution, flat_direction, reals // 2)
    norms, new_solution, kept = lax.optimization_barrier((norms, new_solution, kept))
    new_direction = turn_direction(norms, small, kept, flat_direction, new_residual)
    return tuple(from_flat(out, halves) for out in (new_solution, out_residual, new_direction))


def body(*args):
    direction, legendre, noise_weight = args[2], args[8], args[9]
    reals, comps, slots, halves, count = direction.shape
    bands, sector, pixels = noise_weight.shape
    comp_count = lax.axis_size("comp")
    all_slots = lax.axis_size("ma") * comp_count * legendre.shape[0]
    fits = (
        comp_count == 2
        and slots == 2
        and legendre.shape[0] == 1
        and halves == 2
        and reals % 8 == 0
        and reals == 16
        and halves * (reals // 8) * sector == LANES
        and count % 1024 == 0
        and pixels % 1024 == 0
        and all_slots == 8
        and lax.axis_size("band") == 4
    )
    return fast(*args) if fits else general(*args)


def solution(mesh):
    in_specs = (
        P(None, "comp", "ma", None, None),
        P(None, "comp", "ma", None, None),
        P(None, "comp", "ma", None, None),
        P("comp", None),
        P("band", None),
        P("band", None),
        P("band"),
        P(),
        P(("ma", "comp"), None, None),
        P("band", ("ma", "comp"), None),
        P("band", ("ma", "comp"), None),
    )
    out_specs = (
        P(None, "comp", "ma", None, None),
        P(None, "comp", "ma", None, None),
        P(None, "comp", "ma", None, None),
    )
    return jax.shard_map(body, mesh=mesh, in_specs=in_specs, out_specs=out_specs, check_vma=False)
```

```python
import math

import jax
import jax.numpy as jnp
from jax import lax
from jax.experimental import pallas as pl
from jax.experimental.pallas import tpu as pltpu
from jax.sharding import PartitionSpec as P

LANES = 128
F32 = jnp.float32
BF16 = jnp.bfloat16
ON_CHIP = pl.BlockSpec(memory_space=pltpu.VMEM)
SCALARS = pl.BlockSpec(memory_space=pltpu.SMEM)
IN_PLACE = pl.BlockSpec(memory_space=pltpu.HBM)


def near(array):
    return pltpu.with_memory_space_constraint(array, pltpu.VMEM)


def far(array):
    return pltpu.with_memory_space_constraint(array, pltpu.HBM)


def limit(mebibytes):
    return pltpu.CompilerParams(vmem_limit_bytes=mebibytes * 1024 * 1024)


def shape_near(shape, kind):
    return pltpu.VMEM(shape, kind)


def flat_view(array):
    lead, halves, count = array.shape[:-2], array.shape[-2], array.shape[-1]
    tiles = count // LANES
    split = array.reshape(lead + (halves, tiles, LANES))
    return jnp.swapaxes(split, -3, -2).reshape(lead + (tiles * halves, LANES))


def from_flat(array, halves):
    lead, rows = array.shape[:-2], array.shape[-2]
    tiles = rows // halves
    split = jnp.swapaxes(array.reshape(lead + (tiles, halves, LANES)), -3, -2)
    return split.reshape(lead + (halves, tiles * LANES))


def dot_nt(left, right):
    return lax.dot_general(left, right, (((1,), (1,)), ((), ())), preferred_element_type=F32)


def dot_nn(left, right):
    return lax.dot_general(left, right, (((1,), (0,)), ((), ())), preferred_element_type=F32)


def split_bf16(value):
    top = value.astype(BF16)
    return top, (value - top.astype(F32)).astype(BF16)


def narrow(flat, own, halves, *extras):
    reals, comps, slots, rows, lanes = flat.shape
    tiles = rows // halves
    pitch = rows + 8
    extra = len(extras)

    def kernel(x_ref, *rest):
        o_ref = rest[extra]
        buffer, arrived = rest[-2:]
        index = lax.axis_index("comp")
        slot = index if own else 1 - index
        copies = [
            pltpu.make_async_copy(
                x_ref.at[:, comp, slot],
                buffer.at[comp, :, pl.ds(0, rows), :],
                arrived.at[comp],
            )
            for comp in range(comps)
        ]
        for copy in copies:
            copy.start()
        if extra:
            mix_ref, lmax_ref, m_ref, beam_ref, far_ref = rest[:extra]
            scale_ref, order_ref, leg_ref = rest[extra + 1 : extra + 4]
            copies.append(pltpu.make_async_copy(far_ref, leg_ref, arrived.at[comps]))
            copies[comps].start()
            bands, count = beam_ref.shape
            row = lax.broadcasted_iota(jnp.int32, (bands, 1), 0)
            most = jnp.zeros((bands, 1), jnp.int32)
            for band in range(bands):
                most = jnp.where(row == band, lmax_ref[band], most)
            degree = lax.broadcasted_iota(jnp.int32, (bands, count), 1)
            keep = (degree <= most) & (degree >= m_ref[lax.axis_index("ma") * 2 + index])
            scale_ref[...] = jnp.where(keep, beam_ref[...], 0.0)
            width = 2 * comps
            line = lax.broadcasted_iota(jnp.int32, (bands, width), 0)
            column = lax.broadcasted_iota(jnp.int32, (bands, width), 1)
            ordered = jnp.zeros((bands, width), F32)
            for band in range(bands):
                for turn, group in enumerate((index, 1 - index)):
                    for comp in range(comps):
                        here = (line == band) & (column == turn * comps + comp)
                        ordered = jnp.where(here, mix_ref[band, group * comps + comp], ordered)
            order_ref[...] = ordered
        lines = buffer.reshape(comps * reals * pitch, lanes)
        for comp in range(comps):
            copies[comp].wait()
            for tile in range(tiles):
                for half in range(halves):
                    start = comp * reals * pitch + tile * halves + half
                    picked = lines[pl.ds(start, reals, stride=pitch), :]
                    o_ref[
                        comp,
                        half * reals : (half + 1) * reals,
                        tile * lanes : (tile + 1) * lanes,
                    ] = picked.astype(BF16)
        if extra:
            copies[comps].wait()

    shapes = (shape_near((comps, halves * reals, tiles * lanes), BF16),)
    if extra:
        bands, count = extras[3].shape
        shapes += (shape_near((bands, count), F32), shape_near((bands, 2 * comps), F32))
        shapes += (shape_near(extras[4].shape, BF16),)
        extras = extras[:4] + (far(extras[4]),)
    return pl.pallas_call(
        kernel,
        compiler_params=limit(4),
        out_shape=shapes,
        in_specs=[IN_PLACE] + ([SCALARS] * 3 + [ON_CHIP, IN_PLACE] if extra else []),
        out_specs=(ON_CHIP,) * len(shapes),
        scratch_shapes=[
            pltpu.VMEM((comps, reals, pitch, lanes), F32),
            pltpu.SemaphoreType.DMA((comps + 1,)),
        ],
    )(far(flat), *extras)


def shared_rows(after, mixing, lmax, beam):
    bands, count = beam.shape
    columns = mixing.shape[1]

    def kernel(mix_ref, lmax_ref, after_ref, beam_ref, o_ref):
        row = lax.broadcasted_iota(jnp.int32, (bands, 1), 0)
        most = jnp.zeros((bands, 1), jnp.int32)
        for band in range(bands):
            most = jnp.where(row == band, lmax_ref[band], most)
        degree = lax.broadcasted_iota(jnp.int32, (bands, count), 1)
        o_ref[:bands, :] = jnp.where(degree <= most, beam_ref[...], 0.0)
        lane = lax.broadcasted_iota(jnp.int32, (1, count), 1)
        last = jnp.zeros((1, count), F32)
        for band in range(bands):
            for column in range(columns):
                last = jnp.where(lane == band * columns + column, mix_ref[band, column], last)
        o_ref[bands:, :] = last

    return pl.pallas_call(
        kernel,
        compiler_params=limit(4),
        out_shape=shape_near((bands + 1, count), F32),
        in_specs=[SCALARS, SCALARS, IN_PLACE, ON_CHIP],
        out_specs=ON_CHIP,
    )(mixing, lmax, far(after), beam)


def pack_sectors(cycles_values, bands, sectors):
    rows, cycles = cycles_values.shape
    lines = rows // bands
    sector = cycles // sectors
    parts = lines // 8

    def kernel(x_ref, o_ref):
        for band in range(bands):
            values = [x_ref[band * lines + part * 8 : band * lines + part * 8 + 8, :] for part in range(parts)]
            for at in range(sectors):
                pieces = [value[:, at * sector : (at + 1) * sector] for value in values]
                o_ref[at, band * 8 : band * 8 + 8, :] = jnp.concatenate(pieces, 1).astype(BF16)

    return pl.pallas_call(
        kernel,
        compiler_params=limit(4),
        out_shape=shape_near((sectors, bands * 8, parts * sector), BF16),
        in_specs=[ON_CHIP],
        out_specs=ON_CHIP,
    )(near(cycles_values))


def gram(after, table, noise_weight, pixel_mask, high, chunk):
    halves, slots, pixels = table.shape
    bands, sector, _ = noise_weight.shape
    lines = bands * sector
    rows = slots * slots
    pairs = ((0, 0), (0, 1), (1, 1))

    def kernel(after_ref, table_ref, noise_ref, mask_ref, o_ref, nn_ref, mn_ref, top_ref,
               weight_ref, sum_ref, sems):
        copies = [
            pltpu.make_async_copy(source, target, sems.at[which])
            for which, (source, target) in enumerate(((noise_ref, nn_ref), (mask_ref, mn_ref)))
        ]
        for copy in copies:
            copy.start()
        for at in range(0, pixels, chunk):
            span = slice(at, at + chunk)
            for which, (first, second) in enumerate(pairs):
                right = table_ref[second, :, span]
                for slot in range(0, slots, 2):
                    products = [
                        table_ref[first, at_slot : at_slot + 1, span] * right
                        for at_slot in (slot, slot + 1)
                    ]
                    row = which * rows + slot * slots
                    top_ref[row : row + 2 * slots, span] = jnp.concatenate(products, 0).astype(
                        BF16
                    )
        for copy in copies:
            copy.wait()
        for at in range(0, pixels, chunk):
            span = slice(at, at + chunk)
            weight = nn_ref[:, span] * mn_ref[:, span].astype(F32)
            top, low = split_bf16(weight)
            weight_ref[:lines, span] = top
            weight_ref[lines:, span] = low
        acc = dot_nt(top_ref[...], weight_ref[...])
        sum_ref[...] = acc[:, :lines] + acc[:, lines:]
        for band in range(bands):
            span = slice(band * sector, (band + 1) * sector)
            blocks = [sum_ref[at * rows : (at + 1) * rows, span] for at in range(len(pairs))]
            turned = jnp.concatenate(
                [
                    sum_ref[pl.ds(rows + slot, slots, stride=slots), :]
                    for slot in range(slots)
                ],
                0,
            )[:, span]
            o_ref[0, band] = jnp.concatenate([blocks[0]] * high + [blocks[2]] * high, 1)
            o_ref[1, band] = jnp.concatenate([blocks[1]] * high + [turned] * high, 1)

    return pl.pallas_call(
        kernel,
        compiler_params=limit(16),
        out_shape=shape_near((2, bands, rows, halves * high * sector), F32),
        in_specs=[IN_PLACE, ON_CHIP, IN_PLACE, IN_PLACE],
        out_specs=ON_CHIP,
        scratch_shapes=[
            pltpu.VMEM((lines, pixels), F32),
            pltpu.VMEM((lines, pixels), jnp.int32),
            pltpu.VMEM((len(pairs) * rows, pixels), BF16),
            pltpu.VMEM((2 * lines, pixels), BF16),
            pltpu.VMEM((len(pairs) * rows, lines), F32),
            pltpu.SemaphoreType.DMA((2,)),
        ],
    )(
        far(after),
        near(table),
        far(noise_weight.reshape(lines, pixels)),
        far(pixel_mask.reshape(lines, pixels)),
    )


def lane_sums(rows):
    return jnp.sum(rows.T, axis=0, keepdims=True)


def own_dots(after, prior, direction, residual, shares):
    reals, comps, slots, rows, lanes = direction.shape
    size = rows // shares

    def kernel(after_ref, prior_ref, d_ref, r_ref, o_ref, dn_ref, rn_ref, arrived):
        start = pl.multiple_of(lax.axis_index("band") * size, 8)
        copies = [
            pltpu.make_async_copy(source.at[:, :, :, pl.ds(start, size)], target, arrived.at[which])
            for which, (source, target) in enumerate(((d_ref, dn_ref), (r_ref, rn_ref)))
        ]
        for copy in copies:
            copy.start()
        odd = lax.broadcasted_iota(jnp.int32, (8, lanes), 0) % 2 == 1
        priors = [[], []]
        for at in range(0, size, 8):
            value = prior_ref[pl.ds(start + at, 8), :]
            priors[0].append(jnp.where(odd, pltpu.roll(value, 1, 0), value))
            priors[1].append(jnp.where(odd, value, pltpu.roll(value, 7, 0)))
        for copy in copies:
            copy.wait()
        folded = []
        for which, ref in enumerate((dn_ref, rn_ref)):
            for real in range(reals):
                total = None
                for comp in range(comps):
                    for slot in range(slots):
                        for at in range(0, size, 8):
                            value = ref[real, comp, slot, at : at + 8, :]
                            term = value * value
                            if which == 0:
                                term = priors[comp][at // 8] * term
                            total = term if total is None else total + term
                folded.append(jnp.sum(total, axis=0, keepdims=True))
        folded.append(jnp.zeros((lanes - 2 * reals, lanes), F32))
        o_ref[...] = lane_sums(jnp.concatenate(folded, 0))

    share = direction.shape[:3] + (size, lanes)
    return pl.pallas_call(
        kernel,
        compiler_params=limit(8),
        out_shape=shape_near((1, lanes), F32),
        in_specs=[IN_PLACE, ON_CHIP, IN_PLACE, IN_PLACE],
        out_specs=ON_CHIP,
        scratch_shapes=[
            pltpu.VMEM(share, F32),
            pltpu.VMEM(share, F32),
            pltpu.SemaphoreType.DMA((2,)),
        ],
    )(far(after), prior, far(direction), far(residual))


def apply_gram(dots, grams, spread, copies, group):
    slots, lines, lanes = spread.shape
    bands = grams.shape[1]
    readers = slots // group
    sector = lanes // 4
    reals = 16

    def kernel(dots_ref, g_ref, x_ref, o_ref):
        product = None
        for band in range(bands):
            straight, turned = [], []
            for slot in range(slots):
                value = x_ref[slot, band * 8 : band * 8 + 8, :].astype(F32)
                straight.append(value)
                turned.append(pltpu.roll(value, lanes // 2, 1))
            for slot in range(slots):
                total = None
                for other in range(slots):
                    row = slot * slots + other
                    term = g_ref[0, band, row : row + 1, :] * straight[other]
                    term = term + g_ref[1, band, row : row + 1, :] * turned[other]
                    total = term if total is None else total + term
                total = total.astype(BF16)
                term = total.astype(F32) * straight[slot]
                product = term if product is None else product + term
                line = (slot % group) * lines + band * 8
                for copy in range(copies):
                    o_ref[copy * readers + slot // group, line : line + 8, :] = total
        product = product + pltpu.roll(product, lanes // 2, 1)
        halves = [product[:, :sector], product[:, sector : 2 * sector]]
        tall = jnp.concatenate(
            [
                jnp.concatenate([half, jnp.zeros((8, lanes - sector), F32)], 1)
                for half in halves
            ]
            + [jnp.zeros((lanes - 16, lanes), F32)],
            0,
        )
        value = lane_sums(tall) + dots_ref[...]
        top = value.astype(BF16).astype(F32)
        rest = value - top
        middle = rest.astype(BF16).astype(F32)
        last = (rest - middle).astype(BF16).astype(F32)
        row = top + pltpu.roll(middle, 2 * reals, 1) + pltpu.roll(last, 4 * reals, 1)
        tail = jnp.concatenate([row, jnp.zeros((7, lanes), F32)], 0).astype(BF16)
        for reader in range(copies * readers):
            o_ref[reader, group * lines : group * lines + 8, :] = tail

    return pl.pallas_call(
        kernel,
        compiler_params=limit(4),
        out_shape=shape_near((copies * readers, group * lines + 8, lanes), BF16),
        in_specs=[ON_CHIP] * 3,
        out_specs=ON_CHIP,
    )(near(dots), near(grams), near(spread))


def analyze(m_table, own, received, own_leg, got_leg, shared, prior, direction, residual,
            bands, columns, sectors, halves, copies, chunk):
    reals, comps, slots, rows, lanes = direction.shape
    groups = len(shared)
    total_bands = groups * bands
    count, cycles = own_leg.shape
    sector = cycles // sectors
    high = reals // 8
    lines = halves * reals
    tiles = chunk // lanes
    block_rows = tiles * halves
    pitch = comps * block_rows + 8
    per_slot = bands * 8
    slab = sectors // 2
    tail = slots * per_slot
    pieces_count = 1

    def kernel(m_ref, own_ref, got_ref, own_leg_ref, got_leg_ref, *rest):
        blocks = rest[:groups]
        (prior_ref, d_ref, r_ref, new_ref, out_ref, sums_ref, small_ref, back_ref, h_ref, h2_ref, s_ref,
         step_ref, leg_ref, dn_ref, rn_ref, arrived, left, coef_ref, p_ref) = rest[groups:]
        index_comp = lax.axis_index("comp")
        index_band = lax.axis_index("band")
        places = (index_comp, 1 - index_comp)
        is_first = index_comp == 0
        sources = (own_leg_ref, got_leg_ref)
        copies_of = []
        for turn in range(slots):
            for piece in range(pieces_count):
                size = count // pieces_count
                span = pl.ds(piece * size, size)
                size = rows // pieces_count
                lines_span = pl.ds(piece * size, size)
                index = turn * pieces_count + piece
                copies_of.append(
                    [
                        pltpu.make_async_copy(
                            sources[turn].at[span], leg_ref.at[turn, span], arrived.at[index, 0]
                        )
                    ]
                    + [
                        pltpu.make_async_copy(
                            source.at[:, :, places[turn], lines_span],
                            target.at[turn, :, :, lines_span],
                            arrived.at[index, 1 + which],
                        )
                        for which, (source, target) in enumerate(
                            ((d_ref, dn_ref), (r_ref, rn_ref))
                        )
                    ]
                )
        for triple in copies_of:
            for copy in triple:
                copy.start()

        total = None
        for ref in (own_ref, got_ref):
            for at in range(groups * slab):
                value = ref[at, tail : tail + 8, :].astype(F32)
                total = value if total is None else total + value
        line = total[0:1, :]
        line = (
            line
            + pltpu.roll(line, lanes - 2 * reals, 1)
            + pltpu.roll(line, lanes - 4 * reals, 1)
        )
        norm_old = line[:, reals : 2 * reals]
        step_size = norm_old / line[:, :reals]
        small_ref[...] = jnp.concatenate(
            [step_size, norm_old, jnp.zeros((1, lanes - 2 * reals), F32)], 1
        )
        for real in range(reals):
            step_ref[real] = jnp.broadcast_to(step_size[:, real : real + 1], (8, lanes))

        odd = lax.broadcasted_iota(jnp.int32, (8, lanes), 0) % 2 == 1
        for at in range(0, rows, 8):
            value = prior_ref[at : at + 8, :]
            p_ref[0, at : at + 8, :] = jnp.where(odd, pltpu.roll(value, 1, 0), value)
            p_ref[1, at : at + 8, :] = jnp.where(odd, value, pltpu.roll(value, 7, 0))
        for group in range(groups):
            mix = blocks[group][bands : bands + 1, :lanes]
            for comp in range(comps):
                scales = [
                    jnp.where(
                        is_first,
                        mix[:, band * columns + comp : band * columns + comp + 1],
                        mix[:, band * columns + comps + comp : band * columns + comps + comp + 1],
                    )
                    for band in range(bands)
                ]
                scales.append(jnp.zeros((1, 1), F32))
                coef_ref[group, comp] = blocks[group][...] * jnp.concatenate(scales, 0)

        for turn in range(slots):
            base = places[turn] * per_slot
            for group in range(groups):
                source = (index_band ^ group) * slab
                for band in range(bands):
                    start = pl.multiple_of(base + band * 8, 8)
                    for part in range(lines // 8):
                        span = slice(part * sector, (part + 1) * sector)
                        pieces = []
                        for z in range(slab):
                            mine = own_ref[source + z, pl.ds(start, 8), :].astype(F32)
                            theirs = got_ref[source + z, pl.ds(start, 8), :].astype(F32)
                            pieces.append(jnp.where(is_first, mine, theirs)[:, span])
                            pieces.append(jnp.where(is_first, theirs, mine)[:, span])
                        row = (group * bands + band) * lines + part * 8
                        back_ref[turn, row : row + 8, :] = jnp.concatenate(pieces, 1).astype(BF16)

        buffers = (h_ref, h2_ref)
        work = [(turn, at) for turn in range(slots) for at in range(0, count, chunk)]

        def multiply(index):
            turn, at = work[index]
            buffers[index % 2][...] = dot_nt(back_ref[turn], leg_ref[turn, at : at + chunk, :])

        for copy in copies_of[0]:
            copy.wait()
        lane = lax.broadcasted_iota(jnp.int32, (lines, lanes), 1)
        norms = [None] * reals
        leaving = []
        multiply(0)
        for index, (turn, at) in enumerate(work):
            if index + 1 < len(work):
                if work[index + 1][0] != turn:
                    for copy in copies_of[turn + 1]:
                        copy.wait()
                multiply(index + 1)
            h = buffers[index % 2]
            least = m_ref[lax.axis_index("ma") * 2 + places[turn]]
            for tile in range(tiles):
                part = slice(tile * lanes, (tile + 1) * lanes)
                here = slice(at + tile * lanes, at + (tile + 1) * lanes)
                totals = [None] * comps
                for group in range(groups):
                    for band in range(bands):
                        row = (group * bands + band) * lines
                        value = h[row : row + lines, part]
                        for comp in range(comps):
                            term = coef_ref[group, comp, band : band + 1, here] * value
                            totals[comp] = term if totals[comp] is None else totals[comp] + term
                keep = lane >= least - (at + tile * lanes)
                for comp in range(comps):
                    total = jnp.where(keep, totals[comp], 0.0)
                    for half in range(halves):
                        start = comp * block_rows + tile * halves + half
                        s_ref[index % 2, pl.ds(start, reals, stride=pitch), :] = total[
                            half * reals : (half + 1) * reals
                        ]
            first = at // lanes * halves
            for real in range(reals):
                for comp in range(comps):
                    for sub in range(0, block_rows, 8):
                        span = slice(first + sub, first + sub + 8)
                        line = real * pitch + comp * block_rows + sub
                        d = dn_ref[turn, real, comp, span, :]
                        r = rn_ref[turn, real, comp, span, :]
                        image = p_ref[comp, span, :] * d + s_ref[index % 2, line : line + 8, :]
                        new = r - step_ref[real] * image
                        new_ref[real, comp, places[turn], span, :] = new
                        term = new * new
                        norms[real] = term if norms[real] is None else norms[real] + term
            if (at + chunk) % (count // 2) == 0:
                piece = at // (count // 2)
                span = pl.ds(piece * rows // 2, rows // 2)
                leaving.append(
                    pltpu.make_async_copy(
                        new_ref.at[:, :, places[turn], span],
                        out_ref.at[:, :, places[turn], span],
                        left.at[turn, piece],
                    )
                )
                leaving[-1].start()
        folded = [jnp.sum(norm, axis=0, keepdims=True) for norm in norms]
        folded.append(jnp.zeros((lanes - reals, lanes), F32))
        norm = lane_sums(jnp.concatenate(folded, 0))
        for at in range(copies):
            sums_ref[at] = norm
        for copy in leaving:
            copy.wait()

    return pl.pallas_call(
        kernel,
        compiler_params=limit(24),
        out_shape=(
            shape_near(direction.shape, F32),
            jax.ShapeDtypeStruct(direction.shape, F32),
            shape_near((copies, 1, lanes), F32),
            shape_near((1, lanes), F32),
        ),
        in_specs=[SCALARS] + [ON_CHIP] * 2 + [IN_PLACE] * 2 + [ON_CHIP] * (groups + 1)
        + [IN_PLACE] * 2,
        out_specs=(ON_CHIP, IN_PLACE, ON_CHIP, ON_CHIP),
        scratch_shapes=[
            pltpu.VMEM((slots, total_bands * lines, cycles), BF16),
            pltpu.VMEM((total_bands * lines, chunk), F32),
            pltpu.VMEM((total_bands * lines, chunk), F32),
            pltpu.VMEM((2, reals * pitch, lanes), F32),
            pltpu.VMEM((reals, 8, lanes), F32),
            pltpu.VMEM((slots, count, cycles), BF16),
            pltpu.VMEM((slots, reals, comps, rows, lanes), F32),
            pltpu.VMEM((slots, reals, comps, rows, lanes), F32),
            pltpu.SemaphoreType.DMA((slots * pieces_count, 3)),
            pltpu.SemaphoreType.DMA((slots, 2)),
            pltpu.VMEM((groups, comps, bands + 1, count), F32),
            pltpu.VMEM((comps, rows, lanes), F32),
        ],
    )(
        m_table, near(own), near(received), far(own_leg), far(got_leg),
        *(near(x) for x in shared), prior, far(direction), far(residual),
    )


def advance(small, solution, direction, kept):
    reals, comps, slots, rows, lanes = direction.shape
    parts = 4
    size = reals // parts

    def kernel(small_ref, x_ref, d_ref, ox_ref, kept_ref, x_buffer, d_buffer, o_buffer, sems):
        loads = []
        for part in range(parts):
            span = pl.ds(part * size, size)
            low = part * size
            target = (
                kept_ref.at[span] if low < kept else d_buffer.at[pl.ds(low - kept, size)]
            )
            loads.append(
                (
                    pltpu.make_async_copy(x_ref.at[span], x_buffer.at[span], sems.at[0, part]),
                    pltpu.make_async_copy(d_ref.at[span], target, sems.at[1, part]),
                )
            )
        stores = [
            pltpu.make_async_copy(
                o_buffer.at[pl.ds(part * size, size)], ox_ref.at[pl.ds(part * size, size)],
                sems.at[2, part],
            )
            for part in range(parts)
        ]
        for pair in loads:
            for load in pair:
                load.start()
        for part in range(parts):
            for load in loads[part]:
                load.wait()
            for real in range(part * size, (part + 1) * size):
                step = small_ref[0:1, real : real + 1]
                d = kept_ref[real] if real < kept else d_buffer[real - kept]
                o_buffer[real] = x_buffer[real] + step[None, None] * d
            stores[part].start()
        for store in stores:
            store.wait()

    shape = direction.shape
    return pl.pallas_call(
        kernel,
        compiler_params=limit(10),
        out_shape=(
            jax.ShapeDtypeStruct(shape, F32),
            shape_near((kept,) + shape[1:], F32),
        ),
        in_specs=[ON_CHIP, IN_PLACE, IN_PLACE],
        out_specs=(IN_PLACE, ON_CHIP),
        scratch_shapes=[
            pltpu.VMEM(shape, F32),
            pltpu.VMEM((reals - kept,) + shape[1:], F32),
            pltpu.VMEM(shape, F32),
            pltpu.SemaphoreType.DMA((3, parts)),
        ],
    )(near(small), far(solution), far(direction))


def turn_direction(norms, small, kept, direction, new_residual):
    reals, comps, slots, rows, lanes = direction.shape
    sources = norms.shape[0]
    held = kept.shape[0]
    parts = 8
    size = reals // parts

    def kernel(norms_ref, small_ref, kept_ref, d_ref, r_ref, o_ref, d_buffer, buffer, sems):
        loads = {}
        for part in range(parts):
            low = part * size
            if low >= held:
                loads[part] = pltpu.make_async_copy(
                    d_ref.at[pl.ds(low, size)], d_buffer.at[pl.ds(low - held, size)],
                    sems.at[0, part],
                )
                loads[part].start()
        total = norms_ref[0]
        for at in range(1, sources):
            total = total + norms_ref[at]
        ratio = total[:, :reals] / small_ref[:, reals : 2 * reals]
        stores = [
            pltpu.make_async_copy(
                buffer.at[pl.ds(part * size, size)], o_ref.at[pl.ds(part * size, size)],
                sems.at[1, part],
            )
            for part in range(parts)
        ]
        for part in range(parts):
            if part in loads:
                loads[part].wait()
            for real in range(part * size, (part + 1) * size):
                one = ratio[:, real : real + 1]
                d = kept_ref[real] if real < held else d_buffer[real - held]
                buffer[real] = r_ref[real] + one[None, None] * d
            stores[part].start()
        for store in stores:
            store.wait()

    shape = direction.shape
    return pl.pallas_call(
        kernel,
        compiler_params=limit(8),
        out_shape=jax.ShapeDtypeStruct(shape, F32),
        in_specs=[ON_CHIP, ON_CHIP, ON_CHIP, IN_PLACE, ON_CHIP],
        out_specs=IN_PLACE,
        scratch_shapes=[
            pltpu.VMEM((reals - held,) + shape[1:], F32),
            pltpu.VMEM(shape, F32),
            pltpu.SemaphoreType.DMA((2, parts)),
        ],
    )(near(norms), near(small), near(kept), far(direction), near(new_residual))


def phase_table(m_table, pixels):
    columns = jnp.arange(pixels, dtype=jnp.int32)
    wrapped = m_table[:, None] * columns[None, :] % pixels
    angles = wrapped.astype(jnp.float32) * (2.0 * math.pi / pixels)
    weights = jnp.where(m_table == 0, 1.0, 2.0).astype(jnp.float32)[:, None] / math.sqrt(pixels)
    return jnp.stack([weights * jnp.cos(angles), -weights * jnp.sin(angles)], axis=1).astype(
        jnp.bfloat16
    )


def swap_parts(parts, axis):
    count = lax.axis_size(axis)
    got = [parts[0]]
    for step in range(1, count):
        pairs = [(i, (i + step) % count) for i in range(count)]
        got.append(lax.ppermute(parts[step], axis, pairs))
    return got


def widen(values):
    return values[:, None, None, None, None]


def general(
    solution,
    residual,
    direction,
    prior_inv,
    mixing,
    beam,
    band_lmax,
    m_table,
    legendre,
    noise_weight,
    pixel_mask,
):
    band_count = lax.axis_size("band")
    slab_count = lax.axis_size("ma")
    comp_count = lax.axis_size("comp")
    comp_index = lax.axis_index("comp")
    slab_index = lax.axis_index("ma")
    reals, comps, slots, halves, degrees_count = direction.shape
    half_count = legendre.shape[0]
    bands = mixing.shape[0]
    cycles = legendre.shape[2]
    sector = noise_weight.shape[1]
    pixels = noise_weight.shape[2]
    sectors = slab_count * comp_count
    degrees = jnp.arange(degrees_count, dtype=jnp.int32)
    f32 = jnp.float32
    bf16 = jnp.bfloat16

    first_slot = (slab_index * comp_count + comp_index) * half_count
    local_m = lax.dynamic_slice_in_dim(m_table, first_slot, half_count)
    upper = degrees[None, :] <= band_lmax[:, None]
    cut_beam = beam * upper.astype(f32)
    lower = degrees[None, :] >= local_m[:, None]
    scale = cut_beam[:, None, :] * lower[None].astype(f32)

    low = jnp.transpose(direction, (2, 1, 3, 0, 4)).astype(bf16)
    low = low.reshape((comp_count, half_count) + low.shape[1:])
    relative = [
        lax.dynamic_index_in_dim(low, (comp_index + step) % comp_count, 0, keepdims=False)
        for step in range(comp_count)
    ]
    got = swap_parts(relative, "comp")
    mixed = None
    for step in range(comp_count):
        source = (comp_index - step) % comp_count
        columns = lax.dynamic_slice_in_dim(mixing, source * comps, comps, 1)
        for comp in range(comps):
            term = columns[:, comp][:, None, None, None, None] * got[step][None, :, comp].astype(f32)
            mixed = term if mixed is None else mixed + term
    coeffs = (scale[:, :, None, None, :] * mixed).astype(bf16)
    cycle_values = jnp.einsum(
        "bmqnl,mlr->bmqnr", coeffs, legendre, preferred_element_type=f32
    ).astype(bf16)
    send = cycle_values.reshape(bands, half_count, halves, reals, sectors, sector)
    send = jnp.transpose(send, (4, 1, 2, 3, 0, 5)).reshape(
        sectors, half_count * halves, reals, bands * sector
    )
    spread = lax.all_to_all(send, ("ma", "comp"), 0, 0, tiled=True)
    rows = sectors * half_count * halves
    spread = spread.reshape(rows, reals, bands * sector).astype(f32)

    table = phase_table(m_table, pixels).reshape(rows, pixels)
    weight = (noise_weight * pixel_mask.astype(f32)).reshape(bands * sector, pixels)
    if rows <= 2 * reals:
        pairs = (table.astype(f32)[:, None, :] * table.astype(f32)[None, :, :]).reshape(
            rows * rows, pixels
        )
        gram = lax.dot_general(
            pairs, weight, (((1,), (1,)), ((), ())), precision=lax.Precision.HIGH,
            preferred_element_type=f32,
        ).reshape(rows, rows, 1, bands * sector)
        back = (gram * spread[None]).sum(1).astype(bf16)
    else:
        sky = jnp.einsum("knx,kj->nxj", spread.astype(bf16), table, preferred_element_type=f32)
        weighted = (weight[None] * sky).astype(bf16)
        back = jnp.einsum("nxj,kj->knx", weighted, table, preferred_element_type=f32).astype(bf16)

    back = back.reshape(sectors, half_count * halves, reals, bands * sector)
    everyone = jnp.broadcast_to(back[None], (band_count,) + back.shape).reshape(
        (band_count * sectors,) + back.shape[1:]
    )
    gathered = lax.all_to_all(everyone, ("band", "ma", "comp"), 0, 0, tiled=True)
    gathered = gathered.reshape(
        band_count, sectors, half_count, halves, reals, bands, sector
    )
    total_bands = band_count * bands
    own_back = jnp.transpose(gathered, (2, 0, 5, 3, 4, 1, 6)).reshape(
        half_count, total_bands, halves, reals, cycles
    )
    all_back = swap_parts([own_back] * comp_count, "comp")
    all_legendre = swap_parts([legendre] * comp_count, "comp")

    packed = jnp.concatenate([cut_beam, jnp.pad(mixing, ((0, 0), (0, 128 - mixing.shape[1])))], 1)
    packed = lax.all_to_all(
        jnp.broadcast_to(packed[None], (band_count,) + packed.shape), "band", 0, 0, tiled=True
    ).reshape(total_bands, -1)
    all_beam = packed[:, :degrees_count]
    all_mixing = packed[:, degrees_count : degrees_count + mixing.shape[1]]
    own_mixing = lax.dynamic_slice_in_dim(all_mixing, comp_index * comps, comps, 1)
    coef = own_mixing[:, :, None] * all_beam[:, None, :]

    parts = []
    for step in range(comp_count):
        source = (comp_index - step) % comp_count
        slot_m = lax.dynamic_slice_in_dim(
            m_table, (slab_index * comp_count + source) * half_count, half_count
        )
        harmonic = jnp.einsum(
            "mbqnr,mlr->bmqnl", all_back[step], all_legendre[step], preferred_element_type=f32
        )
        total = jnp.zeros((comps, half_count, halves, reals, degrees_count), f32)
        for band in range(total_bands):
            total = total + coef[band][:, None, None, None, :] * harmonic[band][None]
        keep = degrees[None, :] >= slot_m[:, None]
        parts.append(jnp.where(keep[None, :, None, None, :], total, 0.0))
    ordered = [
        lax.dynamic_index_in_dim(
            jnp.stack(parts), (comp_index - position) % comp_count, 0, keepdims=False
        )
        for position in range(comp_count)
    ]
    returned = jnp.concatenate(ordered, axis=1)
    returned = jnp.transpose(returned, (3, 0, 1, 2, 4))
    image = prior_inv[None, :, None, None, :] * direction + returned
    axes = (1, 2, 3, 4)
    sums = jnp.stack(
        [
            jnp.sum(residual * residual, axis=axes),
            jnp.sum(direction * image, axis=axes),
            jnp.sum(residual * image, axis=axes),
            jnp.sum(image * image, axis=axes),
        ]
    )
    sums = lax.all_to_all(
        jnp.broadcast_to(sums[None], (sectors,) + sums.shape), ("ma", "comp"), 0, 0, tiled=True
    ).sum(0)
    norm_old, curvature_sum, cross_sum, image_norm = sums
    step_size = norm_old / curvature_sum
    new_solution = solution + widen(step_size) * direction
    new_residual = residual - widen(step_size) * image
    norm_new = norm_old - 2.0 * step_size * cross_sum + step_size * step_size * image_norm
    new_direction = new_residual + widen(norm_new / norm_old) * direction
    return (new_solution, new_residual, new_direction)


def phase_rows(m_table, pixels):
    columns = jnp.arange(pixels, dtype=jnp.int32)
    wrapped = m_table[:, None] * columns[None, :] % pixels
    angles = wrapped.astype(F32) * (2.0 * math.pi / pixels)
    weights = jnp.where(m_table == 0, 1.0, 2.0).astype(F32)[:, None] / math.sqrt(pixels)
    rows = jnp.stack([weights * jnp.cos(angles), -weights * jnp.sin(angles)], axis=0)
    return rows.astype(BF16).astype(F32)


def fast(
    solution,
    residual,
    direction,
    prior_inv,
    mixing,
    beam,
    band_lmax,
    m_table,
    legendre,
    noise_weight,
    pixel_mask,
):
    band_count = lax.axis_size("band")
    slab_count = lax.axis_size("ma")
    comp_count = lax.axis_size("comp")
    reals, comps, slots, halves, count = direction.shape
    bands, sector, pixels = noise_weight.shape
    sectors = slab_count * comp_count
    high = reals // 8
    exchange = [(0, 1), (1, 0)]
    legendre = legendre[0]
    flat_direction = flat_view(direction)
    flat_residual = flat_view(residual)
    flat_solution = flat_view(solution)

    (sent,) = narrow(flat_direction, False, halves)
    received = lax.ppermute(sent, "comp", exchange)
    own, scale, ordered, near_legendre = narrow(
        flat_direction, True, halves, mixing, band_lmax, m_table, beam, legendre
    )
    lines = halves * reals
    mixed = None
    for turn, group in enumerate((own, received)):
        for comp in range(comps):
            column = ordered[:, turn * comps + comp][:, None, None]
            term = column * group[comp][None].astype(F32)
            mixed = term if mixed is None else mixed + term
    coeffs = (scale[:, None, :] * mixed).astype(BF16)
    cycle_values = jnp.einsum("bkl,lr->bkr", coeffs, near_legendre, preferred_element_type=F32)
    packed = pack_sectors(cycle_values.reshape(bands * lines, -1), bands, sectors)
    spread = lax.all_to_all(packed, ("ma", "comp"), 0, 0, tiled=True)

    late_table, late_legendre, unused = lax.optimization_barrier((m_table, legendre, packed))
    other_legendre = lax.ppermute(late_legendre, "comp", exchange)
    table = phase_rows(late_table, pixels)
    grams = gram(packed, table, noise_weight, pixel_mask, high, 1024)
    flat_prior = flat_view(prior_inv)
    dots = own_dots(packed, flat_prior, flat_direction, flat_residual, band_count)
    back = apply_gram(dots, grams, spread, band_count, comp_count)
    arrived = lax.all_to_all(back, ("band", "ma"), 0, 0, tiled=True)
    own_rows = shared_rows(back, mixing, band_lmax, beam)
    shared = [own_rows] + [
        lax.ppermute(own_rows, "band", [(i, i ^ step) for i in range(band_count)])
        for step in range(1, band_count)
    ]
    arrived, shared = lax.optimization_barrier((arrived, shared))
    other_arrived = lax.ppermute(arrived, "comp", exchange)
    new_residual, out_residual, norms, small = analyze(
        m_table, arrived, other_arrived, legendre, other_legendre, shared, flat_prior,
        flat_direction, flat_residual, bands, comp_count * comps, sectors, halves, sectors, 512,
    )
    norms = lax.all_to_all(norms, ("ma", "comp"), 0, 0, tiled=True)
    new_solution, kept = advance(small, flat_solution, flat_direction, reals // 2)
    norms, new_solution, kept = lax.optimization_barrier((norms, new_solution, kept))
    new_direction = turn_direction(norms, small, kept, flat_direction, new_residual)
    return tuple(from_flat(out, halves) for out in (new_solution, out_residual, new_direction))


def body(*args):
    direction, legendre, noise_weight = args[2], args[8], args[9]
    reals, comps, slots, halves, count = direction.shape
    bands, sector, pixels = noise_weight.shape
    comp_count = lax.axis_size("comp")
    all_slots = lax.axis_size("ma") * comp_count * legendre.shape[0]
    fits = (
        comp_count == 2
        and slots == 2
        and legendre.shape[0] == 1
        and halves == 2
        and reals % 8 == 0
        and reals == 16
        and halves * (reals // 8) * sector == LANES
        and count % 1024 == 0
        and pixels % 1024 == 0
        and all_slots == 8
        and lax.axis_size("band") == 4
    )
    return fast(*args) if fits else general(*args)


def solution(mesh):
    in_specs = (
        P(None, "comp", "ma", None, None),
        P(None, "comp", "ma", None, None),
        P(None, "comp", "ma", None, None),
        P("comp", None),
        P("band", None),
        P("band", None),
        P("band"),
        P(),
        P(("ma", "comp"), None, None),
        P("band", ("ma", "comp"), None),
        P("band", ("ma", "comp"), None),
    )
    out_specs = (
        P(None, "comp", "ma", None, None),
        P(None, "comp", "ma", None, None),
        P(None, "comp", "ma", None, None),
    )
    return jax.shard_map(body, mesh=mesh, in_specs=in_specs, out_specs=out_specs, check_vma=False)
```

```python
import math

import jax
import jax.numpy as jnp
from jax import lax
from jax.experimental import pallas as pl
from jax.experimental.pallas import tpu as pltpu
from jax.sharding import PartitionSpec as P

LANES = 128
F32 = jnp.float32
BF16 = jnp.bfloat16
ON_CHIP = pl.BlockSpec(memory_space=pltpu.VMEM)
SCALARS = pl.BlockSpec(memory_space=pltpu.SMEM)
IN_PLACE = pl.BlockSpec(memory_space=pltpu.HBM)


def near(array):
    return pltpu.with_memory_space_constraint(array, pltpu.VMEM)


def far(array):
    return pltpu.with_memory_space_constraint(array, pltpu.HBM)


def limit(mebibytes):
    return pltpu.CompilerParams(vmem_limit_bytes=mebibytes * 1024 * 1024)


def shape_near(shape, kind):
    return pltpu.VMEM(shape, kind)


def flat_view(array):
    lead, halves, count = array.shape[:-2], array.shape[-2], array.shape[-1]
    tiles = count // LANES
    split = array.reshape(lead + (halves, tiles, LANES))
    return jnp.swapaxes(split, -3, -2).reshape(lead + (tiles * halves, LANES))


def from_flat(array, halves):
    lead, rows = array.shape[:-2], array.shape[-2]
    tiles = rows // halves
    split = jnp.swapaxes(array.reshape(lead + (tiles, halves, LANES)), -3, -2)
    return split.reshape(lead + (halves, tiles * LANES))


def dot_nt(left, right):
    return lax.dot_general(left, right, (((1,), (1,)), ((), ())), preferred_element_type=F32)


def dot_nn(left, right):
    return lax.dot_general(left, right, (((1,), (0,)), ((), ())), preferred_element_type=F32)


def split_bf16(value):
    top = value.astype(BF16)
    return top, (value - top.astype(F32)).astype(BF16)


def narrow(flat, own, halves, *extras):
    reals, comps, slots, rows, lanes = flat.shape
    tiles = rows // halves
    pitch = rows + 8
    extra = len(extras)

    def kernel(x_ref, *rest):
        o_ref = rest[extra]
        buffer, arrived = rest[-2:]
        index = lax.axis_index("comp")
        slot = index if own else 1 - index
        copies = [
            pltpu.make_async_copy(
                x_ref.at[:, comp, slot],
                buffer.at[comp, :, pl.ds(0, rows), :],
                arrived.at[comp],
            )
            for comp in range(comps)
        ]
        for copy in copies:
            copy.start()
        if extra:
            mix_ref, lmax_ref, m_ref, beam_ref, far_ref = rest[:extra]
            scale_ref, order_ref, leg_ref = rest[extra + 1 : extra + 4]
            copies.append(pltpu.make_async_copy(far_ref, leg_ref, arrived.at[comps]))
            copies[comps].start()
            bands, count = beam_ref.shape
            row = lax.broadcasted_iota(jnp.int32, (bands, 1), 0)
            most = jnp.zeros((bands, 1), jnp.int32)
            for band in range(bands):
                most = jnp.where(row == band, lmax_ref[band], most)
            degree = lax.broadcasted_iota(jnp.int32, (bands, count), 1)
            keep = (degree <= most) & (degree >= m_ref[lax.axis_index("ma") * 2 + index])
            scale_ref[...] = jnp.where(keep, beam_ref[...], 0.0)
            width = 2 * comps
            line = lax.broadcasted_iota(jnp.int32, (bands, width), 0)
            column = lax.broadcasted_iota(jnp.int32, (bands, width), 1)
            ordered = jnp.zeros((bands, width), F32)
            for band in range(bands):
                for turn, group in enumerate((index, 1 - index)):
                    for comp in range(comps):
                        here = (line == band) & (column == turn * comps + comp)
                        ordered = jnp.where(here, mix_ref[band, group * comps + comp], ordered)
            order_ref[...] = ordered
        lines = buffer.reshape(comps * reals * pitch, lanes)
        for comp in range(comps):
            copies[comp].wait()
            for tile in range(tiles):
                for half in range(halves):
                    start = comp * reals * pitch + tile * halves + half
                    picked = lines[pl.ds(start, reals, stride=pitch), :]
                    o_ref[
                        comp,
                        half * reals : (half + 1) * reals,
                        tile * lanes : (tile + 1) * lanes,
                    ] = picked.astype(BF16)
        if extra:
            copies[comps].wait()

    shapes = (shape_near((comps, halves * reals, tiles * lanes), BF16),)
    if extra:
        bands, count = extras[3].shape
        shapes += (shape_near((bands, count), F32), shape_near((bands, 2 * comps), F32))
        shapes += (shape_near(extras[4].shape, BF16),)
        extras = extras[:4] + (far(extras[4]),)
    return pl.pallas_call(
        kernel,
        compiler_params=limit(4),
        out_shape=shapes,
        in_specs=[IN_PLACE] + ([SCALARS] * 3 + [ON_CHIP, IN_PLACE] if extra else []),
        out_specs=(ON_CHIP,) * len(shapes),
        scratch_shapes=[
            pltpu.VMEM((comps, reals, pitch, lanes), F32),
            pltpu.SemaphoreType.DMA((comps + 1,)),
        ],
    )(far(flat), *extras)


def shared_rows(after, mixing, lmax, beam):
    bands, count = beam.shape
    columns = mixing.shape[1]

    def kernel(mix_ref, lmax_ref, after_ref, beam_ref, o_ref):
        row = lax.broadcasted_iota(jnp.int32, (bands, 1), 0)
        most = jnp.zeros((bands, 1), jnp.int32)
        for band in range(bands):
            most = jnp.where(row == band, lmax_ref[band], most)
        degree = lax.broadcasted_iota(jnp.int32, (bands, count), 1)
        o_ref[:bands, :] = jnp.where(degree <= most, beam_ref[...], 0.0)
        lane = lax.broadcasted_iota(jnp.int32, (1, count), 1)
        last = jnp.zeros((1, count), F32)
        for band in range(bands):
            for column in range(columns):
                last = jnp.where(lane == band * columns + column, mix_ref[band, column], last)
        o_ref[bands:, :] = last

    return pl.pallas_call(
        kernel,
        compiler_params=limit(4),
        out_shape=shape_near((bands + 1, count), F32),
        in_specs=[SCALARS, SCALARS, ON_CHIP, ON_CHIP],
        out_specs=ON_CHIP,
    )(mixing, lmax, near(after), beam)


def pack_sectors(cycles_values, bands, sectors):
    rows, cycles = cycles_values.shape
    lines = rows // bands
    sector = cycles // sectors
    parts = lines // 8

    def kernel(x_ref, o_ref):
        for band in range(bands):
            values = [x_ref[band * lines + part * 8 : band * lines + part * 8 + 8, :] for part in range(parts)]
            for at in range(sectors):
                pieces = [value[:, at * sector : (at + 1) * sector] for value in values]
                o_ref[at, band * 8 : band * 8 + 8, :] = jnp.concatenate(pieces, 1).astype(BF16)

    return pl.pallas_call(
        kernel,
        compiler_params=limit(4),
        out_shape=shape_near((sectors, bands * 8, parts * sector), BF16),
        in_specs=[ON_CHIP],
        out_specs=ON_CHIP,
    )(near(cycles_values))


def gram(after, table, noise_weight, pixel_mask, high, chunk):
    halves, slots, pixels = table.shape
    bands, sector, _ = noise_weight.shape
    lines = bands * sector
    rows = slots * slots
    pairs = ((0, 0), (0, 1), (1, 1))

    def kernel(after_ref, table_ref, noise_ref, mask_ref, o_ref, nn_ref, mn_ref, top_ref,
               weight_ref, sum_ref, sems):
        copies = [
            pltpu.make_async_copy(source, target, sems.at[which])
            for which, (source, target) in enumerate(((noise_ref, nn_ref), (mask_ref, mn_ref)))
        ]
        for copy in copies:
            copy.start()
        for at in range(0, pixels, chunk):
            span = slice(at, at + chunk)
            for which, (first, second) in enumerate(pairs):
                right = table_ref[second, :, span]
                for slot in range(0, slots, 2):
                    products = [
                        table_ref[first, at_slot : at_slot + 1, span] * right
                        for at_slot in (slot, slot + 1)
                    ]
                    row = which * rows + slot * slots
                    top_ref[row : row + 2 * slots, span] = jnp.concatenate(products, 0).astype(
                        BF16
                    )
        for copy in copies:
            copy.wait()
        for at in range(0, pixels, chunk):
            span = slice(at, at + chunk)
            weight = nn_ref[:, span] * mn_ref[:, span].astype(F32)
            top, low = split_bf16(weight)
            weight_ref[:lines, span] = top
            weight_ref[lines:, span] = low
        acc = dot_nt(top_ref[...], weight_ref[...])
        sum_ref[...] = acc[:, :lines] + acc[:, lines:]
        for band in range(bands):
            span = slice(band * sector, (band + 1) * sector)
            blocks = [sum_ref[at * rows : (at + 1) * rows, span] for at in range(len(pairs))]
            turned = jnp.concatenate(
                [
                    sum_ref[pl.ds(rows + slot, slots, stride=slots), :]
                    for slot in range(slots)
                ],
                0,
            )[:, span]
            o_ref[0, band] = jnp.concatenate([blocks[0]] * high + [blocks[2]] * high, 1)
            o_ref[1, band] = jnp.concatenate([blocks[1]] * high + [turned] * high, 1)

    return pl.pallas_call(
        kernel,
        compiler_params=limit(16),
        out_shape=shape_near((2, bands, rows, halves * high * sector), F32),
        in_specs=[ON_CHIP, ON_CHIP, IN_PLACE, IN_PLACE],
        out_specs=ON_CHIP,
        scratch_shapes=[
            pltpu.VMEM((lines, pixels), F32),
            pltpu.VMEM((lines, pixels), jnp.int32),
            pltpu.VMEM((len(pairs) * rows, pixels), BF16),
            pltpu.VMEM((2 * lines, pixels), BF16),
            pltpu.VMEM((len(pairs) * rows, lines), F32),
            pltpu.SemaphoreType.DMA((2,)),
        ],
    )(
        near(after),
        near(table),
        far(noise_weight.reshape(lines, pixels)),
        far(pixel_mask.reshape(lines, pixels)),
    )


def lane_sums(rows):
    return jnp.sum(rows.T, axis=0, keepdims=True)


def own_dots(after, prior, direction, residual, shares):
    reals, comps, slots, rows, lanes = direction.shape
    size = rows // shares

    def kernel(after_ref, prior_ref, d_ref, r_ref, o_ref, dn_ref, rn_ref, arrived):
        start = pl.multiple_of(lax.axis_index("band") * size, 8)
        copies = [
            pltpu.make_async_copy(source.at[:, :, :, pl.ds(start, size)], target, arrived.at[which])
            for which, (source, target) in enumerate(((d_ref, dn_ref), (r_ref, rn_ref)))
        ]
        for copy in copies:
            copy.start()
        odd = lax.broadcasted_iota(jnp.int32, (8, lanes), 0) % 2 == 1
        priors = [[], []]
        for at in range(0, size, 8):
            value = prior_ref[pl.ds(start + at, 8), :]
            priors[0].append(jnp.where(odd, pltpu.roll(value, 1, 0), value))
            priors[1].append(jnp.where(odd, value, pltpu.roll(value, 7, 0)))
        for copy in copies:
            copy.wait()
        folded = []
        for which, ref in enumerate((dn_ref, rn_ref)):
            for real in range(reals):
                total = None
                for comp in range(comps):
                    for slot in range(slots):
                        for at in range(0, size, 8):
                            value = ref[real, comp, slot, at : at + 8, :]
                            term = value * value
                            if which == 0:
                                term = priors[comp][at // 8] * term
                            total = term if total is None else total + term
                folded.append(jnp.sum(total, axis=0, keepdims=True))
        folded.append(jnp.zeros((lanes - 2 * reals, lanes), F32))
        o_ref[...] = lane_sums(jnp.concatenate(folded, 0))

    share = direction.shape[:3] + (size, lanes)
    return pl.pallas_call(
        kernel,
        compiler_params=limit(8),
        out_shape=shape_near((1, lanes), F32),
        in_specs=[ON_CHIP, ON_CHIP, IN_PLACE, IN_PLACE],
        out_specs=ON_CHIP,
        scratch_shapes=[
            pltpu.VMEM(share, F32),
            pltpu.VMEM(share, F32),
            pltpu.SemaphoreType.DMA((2,)),
        ],
    )(near(after), prior, far(direction), far(residual))


def apply_gram(dots, grams, spread, copies, group):
    slots, lines, lanes = spread.shape
    bands = grams.shape[1]
    readers = slots // group
    sector = lanes // 4
    reals = 16

    def kernel(dots_ref, g_ref, x_ref, o_ref):
        product = None
        for band in range(bands):
            straight, turned = [], []
            for slot in range(slots):
                value = x_ref[slot, band * 8 : band * 8 + 8, :].astype(F32)
                straight.append(value)
                turned.append(pltpu.roll(value, lanes // 2, 1))
            for slot in range(slots):
                total = None
                for other in range(slots):
                    row = slot * slots + other
                    term = g_ref[0, band, row : row + 1, :] * straight[other]
                    term = term + g_ref[1, band, row : row + 1, :] * turned[other]
                    total = term if total is None else total + term
                total = total.astype(BF16)
                term = total.astype(F32) * straight[slot]
                product = term if product is None else product + term
                line = (slot % group) * lines + band * 8
                for copy in range(copies):
                    o_ref[copy * readers + slot // group, line : line + 8, :] = total
        product = product + pltpu.roll(product, lanes // 2, 1)
        halves = [product[:, :sector], product[:, sector : 2 * sector]]
        tall = jnp.concatenate(
            [
                jnp.concatenate([half, jnp.zeros((8, lanes - sector), F32)], 1)
                for half in halves
            ]
            + [jnp.zeros((lanes - 16, lanes), F32)],
            0,
        )
        value = lane_sums(tall) + dots_ref[...]
        top = value.astype(BF16).astype(F32)
        rest = value - top
        middle = rest.astype(BF16).astype(F32)
        last = (rest - middle).astype(BF16).astype(F32)
        row = top + pltpu.roll(middle, 2 * reals, 1) + pltpu.roll(last, 4 * reals, 1)
        tail = jnp.concatenate([row, jnp.zeros((7, lanes), F32)], 0).astype(BF16)
        for reader in range(copies * readers):
            o_ref[reader, group * lines : group * lines + 8, :] = tail

    return pl.pallas_call(
        kernel,
        compiler_params=limit(4),
        out_shape=shape_near((copies * readers, group * lines + 8, lanes), BF16),
        in_specs=[ON_CHIP] * 3,
        out_specs=ON_CHIP,
    )(near(dots), near(grams), near(spread))


def analyze(m_table, own, received, own_leg, got_leg, shared, prior, direction, residual,
            bands, columns, sectors, halves, copies, chunk):
    reals, comps, slots, rows, lanes = direction.shape
    groups = len(shared)
    total_bands = groups * bands
    count, cycles = own_leg.shape
    sector = cycles // sectors
    high = reals // 8
    lines = halves * reals
    tiles = chunk // lanes
    block_rows = tiles * halves
    pitch = comps * block_rows + 8
    per_slot = bands * 8
    slab = sectors // 2
    tail = slots * per_slot
    pieces_count = 1

    def kernel(m_ref, own_ref, got_ref, own_leg_ref, got_leg_ref, *rest):
        blocks = rest[:groups]
        (prior_ref, d_ref, r_ref, new_ref, out_ref, sums_ref, small_ref, back_ref, h_ref, h2_ref, s_ref,
         step_ref, leg_ref, dn_ref, rn_ref, arrived, left, coef_ref, p_ref) = rest[groups:]
        index_comp = lax.axis_index("comp")
        index_band = lax.axis_index("band")
        places = (index_comp, 1 - index_comp)
        is_first = index_comp == 0
        sources = (own_leg_ref, got_leg_ref)
        copies_of = []
        for turn in range(slots):
            for piece in range(pieces_count):
                size = count // pieces_count
                span = pl.ds(piece * size, size)
                size = rows // pieces_count
                lines_span = pl.ds(piece * size, size)
                index = turn * pieces_count + piece
                copies_of.append(
                    [
                        pltpu.make_async_copy(
                            sources[turn].at[span], leg_ref.at[turn, span], arrived.at[index, 0]
                        )
                    ]
                    + [
                        pltpu.make_async_copy(
                            source.at[:, :, places[turn], lines_span],
                            target.at[turn, :, :, lines_span],
                            arrived.at[index, 1 + which],
                        )
                        for which, (source, target) in enumerate(
                            ((d_ref, dn_ref), (r_ref, rn_ref))
                        )
                    ]
                )
        for triple in copies_of:
            for copy in triple:
                copy.start()

        total = None
        for ref in (own_ref, got_ref):
            for at in range(groups * slab):
                value = ref[at, tail : tail + 8, :].astype(F32)
                total = value if total is None else total + value
        line = total[0:1, :]
        line = (
            line
            + pltpu.roll(line, lanes - 2 * reals, 1)
            + pltpu.roll(line, lanes - 4 * reals, 1)
        )
        norm_old = line[:, reals : 2 * reals]
        step_size = norm_old / line[:, :reals]
        small_ref[...] = jnp.concatenate(
            [step_size, norm_old, jnp.zeros((1, lanes - 2 * reals), F32)], 1
        )
        for real in range(reals):
            step_ref[real] = jnp.broadcast_to(step_size[:, real : real + 1], (8, lanes))

        odd = lax.broadcasted_iota(jnp.int32, (8, lanes), 0) % 2 == 1
        for at in range(0, rows, 8):
            value = prior_ref[at : at + 8, :]
            p_ref[0, at : at + 8, :] = jnp.where(odd, pltpu.roll(value, 1, 0), value)
            p_ref[1, at : at + 8, :] = jnp.where(odd, value, pltpu.roll(value, 7, 0))
        for group in range(groups):
            mix = blocks[group][bands : bands + 1, :lanes]
            for comp in range(comps):
                scales = [
                    jnp.where(
                        is_first,
                        mix[:, band * columns + comp : band * columns + comp + 1],
                        mix[:, band * columns + comps + comp : band * columns + comps + comp + 1],
                    )
                    for band in range(bands)
                ]
                scales.append(jnp.zeros((1, 1), F32))
                coef_ref[group, comp] = blocks[group][...] * jnp.concatenate(scales, 0)

        for turn in range(slots):
            base = places[turn] * per_slot
            for group in range(groups):
                source = (index_band ^ group) * slab
                for band in range(bands):
                    start = pl.multiple_of(base + band * 8, 8)
                    for part in range(lines // 8):
                        span = slice(part * sector, (part + 1) * sector)
                        pieces = []
                        for z in range(slab):
                            mine = own_ref[source + z, pl.ds(start, 8), :].astype(F32)
                            theirs = got_ref[source + z, pl.ds(start, 8), :].astype(F32)
                            pieces.append(jnp.where(is_first, mine, theirs)[:, span])
                            pieces.append(jnp.where(is_first, theirs, mine)[:, span])
                        row = (group * bands + band) * lines + part * 8
                        back_ref[turn, row : row + 8, :] = jnp.concatenate(pieces, 1).astype(BF16)

        buffers = (h_ref, h2_ref)
        work = [(turn, at) for turn in range(slots) for at in range(0, count, chunk)]

        def multiply(index):
            turn, at = work[index]
            buffers[index % 2][...] = dot_nt(back_ref[turn], leg_ref[turn, at : at + chunk, :])

        for copy in copies_of[0]:
            copy.wait()
        lane = lax.broadcasted_iota(jnp.int32, (lines, lanes), 1)
        norms = [None] * reals
        leaving = []
        multiply(0)
        for index, (turn, at) in enumerate(work):
            if index + 1 < len(work):
                if work[index + 1][0] != turn:
                    for copy in copies_of[turn + 1]:
                        copy.wait()
                multiply(index + 1)
            h = buffers[index % 2]
            least = m_ref[lax.axis_index("ma") * 2 + places[turn]]
            for tile in range(tiles):
                part = slice(tile * lanes, (tile + 1) * lanes)
                here = slice(at + tile * lanes, at + (tile + 1) * lanes)
                totals = [None] * comps
                for group in range(groups):
                    for band in range(bands):
                        row = (group * bands + band) * lines
                        value = h[row : row + lines, part]
                        for comp in range(comps):
                            term = coef_ref[group, comp, band : band + 1, here] * value
                            totals[comp] = term if totals[comp] is None else totals[comp] + term
                keep = lane >= least - (at + tile * lanes)
                for comp in range(comps):
                    total = jnp.where(keep, totals[comp], 0.0)
                    for half in range(halves):
                        start = comp * block_rows + tile * halves + half
                        s_ref[index % 2, pl.ds(start, reals, stride=pitch), :] = total[
                            half * reals : (half + 1) * reals
                        ]
            first = at // lanes * halves
            for real in range(reals):
                for comp in range(comps):
                    for sub in range(0, block_rows, 8):
                        span = slice(first + sub, first + sub + 8)
                        line = real * pitch + comp * block_rows + sub
                        d = dn_ref[turn, real, comp, span, :]
                        r = rn_ref[turn, real, comp, span, :]
                        image = p_ref[comp, span, :] * d + s_ref[index % 2, line : line + 8, :]
                        new = r - step_ref[real] * image
                        new_ref[real, comp, places[turn], span, :] = new
                        term = new * new
                        norms[real] = term if norms[real] is None else norms[real] + term
            if (at + chunk) % (count // 2) == 0:
                piece = at // (count // 2)
                span = pl.ds(piece * rows // 2, rows // 2)
                leaving.append(
                    pltpu.make_async_copy(
                        new_ref.at[:, :, places[turn], span],
                        out_ref.at[:, :, places[turn], span],
                        left.at[turn, piece],
                    )
                )
                leaving[-1].start()
        folded = [jnp.sum(norm, axis=0, keepdims=True) for norm in norms]
        folded.append(jnp.zeros((lanes - reals, lanes), F32))
        norm = lane_sums(jnp.concatenate(folded, 0))
        for at in range(copies):
            sums_ref[at] = norm
        for copy in leaving:
            copy.wait()

    return pl.pallas_call(
        kernel,
        compiler_params=limit(24),
        out_shape=(
            shape_near(direction.shape, F32),
            jax.ShapeDtypeStruct(direction.shape, F32),
            shape_near((copies, 1, lanes), F32),
            shape_near((1, lanes), F32),
        ),
        in_specs=[SCALARS] + [ON_CHIP] * 2 + [IN_PLACE] * 2 + [ON_CHIP] * (groups + 1)
        + [IN_PLACE] * 2,
        out_specs=(ON_CHIP, IN_PLACE, ON_CHIP, ON_CHIP),
        scratch_shapes=[
            pltpu.VMEM((slots, total_bands * lines, cycles), BF16),
            pltpu.VMEM((total_bands * lines, chunk), F32),
            pltpu.VMEM((total_bands * lines, chunk), F32),
            pltpu.VMEM((2, reals * pitch, lanes), F32),
            pltpu.VMEM((reals, 8, lanes), F32),
            pltpu.VMEM((slots, count, cycles), BF16),
            pltpu.VMEM((slots, reals, comps, rows, lanes), F32),
            pltpu.VMEM((slots, reals, comps, rows, lanes), F32),
            pltpu.SemaphoreType.DMA((slots * pieces_count, 3)),
            pltpu.SemaphoreType.DMA((slots, 2)),
            pltpu.VMEM((groups, comps, bands + 1, count), F32),
            pltpu.VMEM((comps, rows, lanes), F32),
        ],
    )(
        m_table, near(own), near(received), far(own_leg), far(got_leg),
        *(near(x) for x in shared), prior, far(direction), far(residual),
    )


def advance(small, solution, direction, kept):
    reals, comps, slots, rows, lanes = direction.shape
    parts = 4
    size = reals // parts

    def kernel(small_ref, x_ref, d_ref, ox_ref, kept_ref, x_buffer, d_buffer, o_buffer, sems):
        loads = []
        for part in range(parts):
            span = pl.ds(part * size, size)
            low = part * size
            target = (
                kept_ref.at[span] if low < kept else d_buffer.at[pl.ds(low - kept, size)]
            )
            loads.append(
                (
                    pltpu.make_async_copy(x_ref.at[span], x_buffer.at[span], sems.at[0, part]),
                    pltpu.make_async_copy(d_ref.at[span], target, sems.at[1, part]),
                )
            )
        stores = [
            pltpu.make_async_copy(
                o_buffer.at[pl.ds(part * size, size)], ox_ref.at[pl.ds(part * size, size)],
                sems.at[2, part],
            )
            for part in range(parts)
        ]
        for pair in loads:
            for load in pair:
                load.start()
        for part in range(parts):
            for load in loads[part]:
                load.wait()
            for real in range(part * size, (part + 1) * size):
                step = small_ref[0:1, real : real + 1]
                d = kept_ref[real] if real < kept else d_buffer[real - kept]
                o_buffer[real] = x_buffer[real] + step[None, None] * d
            stores[part].start()
        for store in stores:
            store.wait()

    shape = direction.shape
    return pl.pallas_call(
        kernel,
        compiler_params=limit(10),
        out_shape=(
            jax.ShapeDtypeStruct(shape, F32),
            shape_near((kept,) + shape[1:], F32),
        ),
        in_specs=[ON_CHIP, IN_PLACE, IN_PLACE],
        out_specs=(IN_PLACE, ON_CHIP),
        scratch_shapes=[
            pltpu.VMEM(shape, F32),
            pltpu.VMEM((reals - kept,) + shape[1:], F32),
            pltpu.VMEM(shape, F32),
            pltpu.SemaphoreType.DMA((3, parts)),
        ],
    )(near(small), far(solution), far(direction))


def turn_direction(norms, small, kept, direction, new_residual):
    reals, comps, slots, rows, lanes = direction.shape
    sources = norms.shape[0]
    held = kept.shape[0]
    parts = 8
    size = reals // parts

    def kernel(norms_ref, small_ref, kept_ref, d_ref, r_ref, o_ref, d_buffer, buffer, sems):
        loads = {}
        for part in range(parts):
            low = part * size
            if low >= held:
                loads[part] = pltpu.make_async_copy(
                    d_ref.at[pl.ds(low, size)], d_buffer.at[pl.ds(low - held, size)],
                    sems.at[0, part],
                )
                loads[part].start()
        total = norms_ref[0]
        for at in range(1, sources):
            total = total + norms_ref[at]
        ratio = total[:, :reals] / small_ref[:, reals : 2 * reals]
        stores = [
            pltpu.make_async_copy(
                buffer.at[pl.ds(part * size, size)], o_ref.at[pl.ds(part * size, size)],
                sems.at[1, part],
            )
            for part in range(parts)
        ]
        for part in range(parts):
            if part in loads:
                loads[part].wait()
            for real in range(part * size, (part + 1) * size):
                one = ratio[:, real : real + 1]
                d = kept_ref[real] if real < held else d_buffer[real - held]
                buffer[real] = r_ref[real] + one[None, None] * d
            stores[part].start()
        for store in stores:
            store.wait()

    shape = direction.shape
    return pl.pallas_call(
        kernel,
        compiler_params=limit(8),
        out_shape=jax.ShapeDtypeStruct(shape, F32),
        in_specs=[ON_CHIP, ON_CHIP, ON_CHIP, IN_PLACE, ON_CHIP],
        out_specs=IN_PLACE,
        scratch_shapes=[
            pltpu.VMEM((reals - held,) + shape[1:], F32),
            pltpu.VMEM(shape, F32),
            pltpu.SemaphoreType.DMA((2, parts)),
        ],
    )(near(norms), near(small), near(kept), far(direction), near(new_residual))


def phase_table(m_table, pixels):
    columns = jnp.arange(pixels, dtype=jnp.int32)
    wrapped = m_table[:, None] * columns[None, :] % pixels
    angles = wrapped.astype(jnp.float32) * (2.0 * math.pi / pixels)
    weights = jnp.where(m_table == 0, 1.0, 2.0).astype(jnp.float32)[:, None] / math.sqrt(pixels)
    return jnp.stack([weights * jnp.cos(angles), -weights * jnp.sin(angles)], axis=1).astype(
        jnp.bfloat16
    )


def swap_parts(parts, axis):
    count = lax.axis_size(axis)
    got = [parts[0]]
    for step in range(1, count):
        pairs = [(i, (i + step) % count) for i in range(count)]
        got.append(lax.ppermute(parts[step], axis, pairs))
    return got


def widen(values):
    return values[:, None, None, None, None]


def general(
    solution,
    residual,
    direction,
    prior_inv,
    mixing,
    beam,
    band_lmax,
    m_table,
    legendre,
    noise_weight,
    pixel_mask,
):
    band_count = lax.axis_size("band")
    slab_count = lax.axis_size("ma")
    comp_count = lax.axis_size("comp")
    comp_index = lax.axis_index("comp")
    slab_index = lax.axis_index("ma")
    reals, comps, slots, halves, degrees_count = direction.shape
    half_count = legendre.shape[0]
    bands = mixing.shape[0]
    cycles = legendre.shape[2]
    sector = noise_weight.shape[1]
    pixels = noise_weight.shape[2]
    sectors = slab_count * comp_count
    degrees = jnp.arange(degrees_count, dtype=jnp.int32)
    f32 = jnp.float32
    bf16 = jnp.bfloat16

    first_slot = (slab_index * comp_count + comp_index) * half_count
    local_m = lax.dynamic_slice_in_dim(m_table, first_slot, half_count)
    upper = degrees[None, :] <= band_lmax[:, None]
    cut_beam = beam * upper.astype(f32)
    lower = degrees[None, :] >= local_m[:, None]
    scale = cut_beam[:, None, :] * lower[None].astype(f32)

    low = jnp.transpose(direction, (2, 1, 3, 0, 4)).astype(bf16)
    low = low.reshape((comp_count, half_count) + low.shape[1:])
    relative = [
        lax.dynamic_index_in_dim(low, (comp_index + step) % comp_count, 0, keepdims=False)
        for step in range(comp_count)
    ]
    got = swap_parts(relative, "comp")
    mixed = None
    for step in range(comp_count):
        source = (comp_index - step) % comp_count
        columns = lax.dynamic_slice_in_dim(mixing, source * comps, comps, 1)
        for comp in range(comps):
            term = columns[:, comp][:, None, None, None, None] * got[step][None, :, comp].astype(f32)
            mixed = term if mixed is None else mixed + term
    coeffs = (scale[:, :, None, None, :] * mixed).astype(bf16)
    cycle_values = jnp.einsum(
        "bmqnl,mlr->bmqnr", coeffs, legendre, preferred_element_type=f32
    ).astype(bf16)
    send = cycle_values.reshape(bands, half_count, halves, reals, sectors, sector)
    send = jnp.transpose(send, (4, 1, 2, 3, 0, 5)).reshape(
        sectors, half_count * halves, reals, bands * sector
    )
    spread = lax.all_to_all(send, ("ma", "comp"), 0, 0, tiled=True)
    rows = sectors * half_count * halves
    spread = spread.reshape(rows, reals, bands * sector).astype(f32)

    table = phase_table(m_table, pixels).reshape(rows, pixels)
    weight = (noise_weight * pixel_mask.astype(f32)).reshape(bands * sector, pixels)
    if rows <= 2 * reals:
        pairs = (table.astype(f32)[:, None, :] * table.astype(f32)[None, :, :]).reshape(
            rows * rows, pixels
        )
        gram = lax.dot_general(
            pairs, weight, (((1,), (1,)), ((), ())), precision=lax.Precision.HIGH,
            preferred_element_type=f32,
        ).reshape(rows, rows, 1, bands * sector)
        back = (gram * spread[None]).sum(1).astype(bf16)
    else:
        sky = jnp.einsum("knx,kj->nxj", spread.astype(bf16), table, preferred_element_type=f32)
        weighted = (weight[None] * sky).astype(bf16)
        back = jnp.einsum("nxj,kj->knx", weighted, table, preferred_element_type=f32).astype(bf16)

    back = back.reshape(sectors, half_count * halves, reals, bands * sector)
    everyone = jnp.broadcast_to(back[None], (band_count,) + back.shape).reshape(
        (band_count * sectors,) + back.shape[1:]
    )
    gathered = lax.all_to_all(everyone, ("band", "ma", "comp"), 0, 0, tiled=True)
    gathered = gathered.reshape(
        band_count, sectors, half_count, halves, reals, bands, sector
    )
    total_bands = band_count * bands
    own_back = jnp.transpose(gathered, (2, 0, 5, 3, 4, 1, 6)).reshape(
        half_count, total_bands, halves, reals, cycles
    )
    all_back = swap_parts([own_back] * comp_count, "comp")
    all_legendre = swap_parts([legendre] * comp_count, "comp")

    packed = jnp.concatenate([cut_beam, jnp.pad(mixing, ((0, 0), (0, 128 - mixing.shape[1])))], 1)
    packed = lax.all_to_all(
        jnp.broadcast_to(packed[None], (band_count,) + packed.shape), "band", 0, 0, tiled=True
    ).reshape(total_bands, -1)
    all_beam = packed[:, :degrees_count]
    all_mixing = packed[:, degrees_count : degrees_count + mixing.shape[1]]
    own_mixing = lax.dynamic_slice_in_dim(all_mixing, comp_index * comps, comps, 1)
    coef = own_mixing[:, :, None] * all_beam[:, None, :]

    parts = []
    for step in range(comp_count):
        source = (comp_index - step) % comp_count
        slot_m = lax.dynamic_slice_in_dim(
            m_table, (slab_index * comp_count + source) * half_count, half_count
        )
        harmonic = jnp.einsum(
            "mbqnr,mlr->bmqnl", all_back[step], all_legendre[step], preferred_element_type=f32
        )
        total = jnp.zeros((comps, half_count, halves, reals, degrees_count), f32)
        for band in range(total_bands):
            total = total + coef[band][:, None, None, None, :] * harmonic[band][None]
        keep = degrees[None, :] >= slot_m[:, None]
        parts.append(jnp.where(keep[None, :, None, None, :], total, 0.0))
    ordered = [
        lax.dynamic_index_in_dim(
            jnp.stack(parts), (comp_index - position) % comp_count, 0, keepdims=False
        )
        for position in range(comp_count)
    ]
    returned = jnp.concatenate(ordered, axis=1)
    returned = jnp.transpose(returned, (3, 0, 1, 2, 4))
    image = prior_inv[None, :, None, None, :] * direction + returned
    axes = (1, 2, 3, 4)
    sums = jnp.stack(
        [
            jnp.sum(residual * residual, axis=axes),
            jnp.sum(direction * image, axis=axes),
            jnp.sum(residual * image, axis=axes),
            jnp.sum(image * image, axis=axes),
        ]
    )
    sums = lax.all_to_all(
        jnp.broadcast_to(sums[None], (sectors,) + sums.shape), ("ma", "comp"), 0, 0, tiled=True
    ).sum(0)
    norm_old, curvature_sum, cross_sum, image_norm = sums
    step_size = norm_old / curvature_sum
    new_solution = solution + widen(step_size) * direction
    new_residual = residual - widen(step_size) * image
    norm_new = norm_old - 2.0 * step_size * cross_sum + step_size * step_size * image_norm
    new_direction = new_residual + widen(norm_new / norm_old) * direction
    return (new_solution, new_residual, new_direction)


def phase_rows(m_table, pixels):
    columns = jnp.arange(pixels, dtype=jnp.int32)
    wrapped = m_table[:, None] * columns[None, :] % pixels
    angles = wrapped.astype(F32) * (2.0 * math.pi / pixels)
    weights = jnp.where(m_table == 0, 1.0, 2.0).astype(F32)[:, None] / math.sqrt(pixels)
    rows = jnp.stack([weights * jnp.cos(angles), -weights * jnp.sin(angles)], axis=0)
    return rows.astype(BF16).astype(F32)


def fast(
    solution,
    residual,
    direction,
    prior_inv,
    mixing,
    beam,
    band_lmax,
    m_table,
    legendre,
    noise_weight,
    pixel_mask,
):
    band_count = lax.axis_size("band")
    slab_count = lax.axis_size("ma")
    comp_count = lax.axis_size("comp")
    reals, comps, slots, halves, count = direction.shape
    bands, sector, pixels = noise_weight.shape
    sectors = slab_count * comp_count
    high = reals // 8
    exchange = [(0, 1), (1, 0)]
    legendre = legendre[0]
    flat_direction = flat_view(direction)
    flat_residual = flat_view(residual)
    flat_solution = flat_view(solution)

    (sent,) = narrow(flat_direction, False, halves)
    received = lax.ppermute(sent, "comp", exchange)
    own, scale, ordered, near_legendre = narrow(
        flat_direction, True, halves, mixing, band_lmax, m_table, beam, legendre
    )
    lines = halves * reals
    mixed = None
    for turn, group in enumerate((own, received)):
        for comp in range(comps):
            column = ordered[:, turn * comps + comp][:, None, None]
            term = column * group[comp][None].astype(F32)
            mixed = term if mixed is None else mixed + term
    coeffs = (scale[:, None, :] * mixed).astype(BF16)
    cycle_values = jnp.einsum("bkl,lr->bkr", coeffs, near_legendre, preferred_element_type=F32)
    packed = pack_sectors(cycle_values.reshape(bands * lines, -1), bands, sectors)
    spread = lax.all_to_all(packed, ("ma", "comp"), 0, 0, tiled=True)

    late_table, late_legendre, unused = lax.optimization_barrier((m_table, legendre, packed))
    other_legendre = lax.ppermute(late_legendre, "comp", exchange)
    table = phase_rows(late_table, pixels)
    grams = gram(packed, table, noise_weight, pixel_mask, high, 1024)
    flat_prior = flat_view(prior_inv)
    dots = own_dots(packed, flat_prior, flat_direction, flat_residual, band_count)
    back = apply_gram(dots, grams, spread, band_count, comp_count)
    arrived = lax.all_to_all(back, ("band", "ma"), 0, 0, tiled=True)
    own_rows = shared_rows(back, mixing, band_lmax, beam)
    shared = [own_rows] + [
        lax.ppermute(own_rows, "band", [(i, i ^ step) for i in range(band_count)])
        for step in range(1, band_count)
    ]
    arrived, shared = lax.optimization_barrier((arrived, shared))
    other_arrived = lax.ppermute(arrived, "comp", exchange)
    new_residual, out_residual, norms, small = analyze(
        m_table, arrived, other_arrived, legendre, other_legendre, shared, flat_prior,
        flat_direction, flat_residual, bands, comp_count * comps, sectors, halves, sectors, 512,
    )
    norms = lax.all_to_all(norms, ("ma", "comp"), 0, 0, tiled=True)
    new_solution, kept = advance(small, flat_solution, flat_direction, reals // 2)
    norms, new_solution, kept = lax.optimization_barrier((norms, new_solution, kept))
    new_direction = turn_direction(norms, small, kept, flat_direction, new_residual)
    return tuple(from_flat(out, halves) for out in (new_solution, out_residual, new_direction))


def body(*args):
    direction, legendre, noise_weight = args[2], args[8], args[9]
    reals, comps, slots, halves, count = direction.shape
    bands, sector, pixels = noise_weight.shape
    comp_count = lax.axis_size("comp")
    all_slots = lax.axis_size("ma") * comp_count * legendre.shape[0]
    fits = (
        comp_count == 2
        and slots == 2
        and legendre.shape[0] == 1
        and halves == 2
        and reals % 8 == 0
        and reals == 16
        and halves * (reals // 8) * sector == LANES
        and count % 1024 == 0
        and pixels % 1024 == 0
        and all_slots == 8
        and lax.axis_size("band") == 4
    )
    return fast(*args) if fits else general(*args)


def solution(mesh):
    in_specs = (
        P(None, "comp", "ma", None, None),
        P(None, "comp", "ma", None, None),
        P(None, "comp", "ma", None, None),
        P("comp", None),
        P("band", None),
        P("band", None),
        P("band"),
        P(),
        P(("ma", "comp"), None, None),
        P("band", ("ma", "comp"), None),
        P("band", ("ma", "comp"), None),
    )
    out_specs = (
        P(None, "comp", "ma", None, None),
        P(None, "comp", "ma", None, None),
        P(None, "comp", "ma", None, None),
    )
    return jax.shard_map(body, mesh=mesh, in_specs=in_specs, out_specs=out_specs, check_vma=False)
```
